256 devices in a mesh: rev: 16 (over x, y), cust: 8 (over z), prod: 2 (over core).
Axes of the slice: x: 4, y: 4, z: 8, core: 2. Of those that a mesh axis runs over, the one named last changes fastest.
Arguments:
- review_cols: bfloat16 [131072, 2048], P(('rev', 'cust', 'prod')), may hold values from -24 to 24
- cust_state: bfloat16 [65536, 512], P(('rev', 'cust')), may hold values from -6 to 6
- prod_state: bfloat16 [8192, 512], P(('cust', 'prod')), may hold values from -6 to 6
- w_qkv: bfloat16 [512, 1536], replicated, may hold values from -0.25 to 0.25
- w_out: bfloat16 [512, 512], replicated, may hold values from -0.25 to 0.25
- w_msg: bfloat16 [512, 1024], replicated, may hold values from -0.25 to 0.25
- w_cust_up: bfloat16 [512, 512], replicated, may hold values from -0.25 to 0.25
- w_prod_up: bfloat16 [512, 512], replicated, may hold values from -0.25 to 0.25
- w_back: bfloat16 [1024, 512], replicated, may hold values from -0.1875 to 0.1875
- cust_slot: int32 [131072], P(('rev', 'cust', 'prod')), may hold values from 0 to 511
- prod_slot: int32 [131072], P(('rev', 'cust', 'prod')), may hold values from 0 to 511
- prod_pos: int32 [256, 512], P(('rev', 'cust', 'prod')), may hold values from 0 to 511, each once within a row
- live_count: int32 [256, 128], P(('rev', 'cust', 'prod')), may hold values from 1 to 4, 320 in all within a row
Outputs:
- review_out: bfloat16 [131072, 512], P(('rev', 'cust', 'prod'))
- new_cust: bfloat16 [65536, 512], P(('rev', 'cust'))
- new_prod: bfloat16 [8192, 512], P(('cust', 'prod'))
The draws below stay inside these ranges and needn't reach their ends.
Inputs may be any that keep to these rules, and one draw needn't show every extreme that they name: `prod_pos`: each device's row is a permutation of 0 to 511. `live_count`: each device's counts sum to 320, and some block holds 4 live reviews.
All inputs are finite; a program needn't handle non-finite values.
Results may differ from the reference program's by a relative error of at most 0.011.
Values may be sent and summed in bfloat16 or wider, within the bound.
A program may use at most 128 MiB of HBM per device.

```python
import math
import jax
import jax.numpy as jnp
import numpy as np
from jax import lax

H = 512
HEADS = 8
NCOL = 4
R_DEV = 512
C_ROWS = 512
P_ROWS = 512
HD = 64
CSLOT = 4
PCAP = 32
LIVE = 320
REVIEWS = 131072
CUSTOMERS = 65536
PRODUCTS = 8192
N_REV = 16
N_CUST = 8
DEVICES = 256


def draw_review_cols(key, part):
    first_key = jax.random.fold_in(key, 0)
    result = jnp.clip(jax.random.normal(first_key, (REVIEWS, NCOL * H), jnp.float32), -6.0, 6.0)
    return result.astype(jnp.bfloat16)


def with_ends(values, own_key, smallest, largest):
    index_at = [jax.random.randint(jax.random.fold_in(own_key, axis), (), 0, length) for axis, length in enumerate(values.shape)]
    longest = values.shape.index(max(values.shape))
    beside = index_at[:longest] + [(index_at[longest] + 1) % values.shape[longest]] + index_at[longest + 1:]
    return values.at[tuple(index_at)].set(smallest).at[tuple(beside)].set(largest)


def block_scale(key, shape, shards, low, largest):
    loudness, own = 1.0, jax.random.fold_in(key, 6)
    for dim, shards_of in shards:
        steps = jnp.exp(jax.random.uniform(jax.random.fold_in(own, dim), (shards_of,), jnp.float32, low / len(shards), largest / len(shards)))
        loudness = loudness * jnp.repeat(steps, shape[dim] // shards_of).reshape([-1 if axis == dim else 1 for axis in range(len(shape))])
    return loudness


def rank_table(amount, lean):
    loads = [(1 << 20) // math.isqrt(rank ** lean) + 1 for rank in range(1, amount + 1)]
    spread = 1 + sum(loads) // (1 << 30)
    return np.cumsum(np.array([max(1, weight // spread) for weight in loads]))


def ranked(own_key, extent, amount, lean):
    listing = rank_table(amount, lean)
    pick = jax.random.randint(jax.random.fold_in(own_key, 1), extent, 0, int(listing[amount - 1]))
    grade = jnp.searchsorted(jnp.asarray(listing, jnp.int32), pick, side="right")
    return jax.random.permutation(jax.random.fold_in(own_key, 2), amount)[grade].astype(jnp.int32)


def length_profile(amount, total, limit, lean):
    weights = [(1 << 20) // math.isqrt(grade ** lean) + 1 for grade in range(2, amount + 1)]
    rest, given = total - limit - (amount - 1), [1] * (amount - 1)
    while rest > 0:
        free = [i for i in range(amount - 1) if given[i] < limit]
        mass, remaining = sum([weights[i] for i in free]), rest
        for i in free:
            addition = min(limit - given[i], max(1, remaining * weights[i] // mass), rest)
            given[i] = given[i] + addition
            rest = rest - addition
    return np.array([limit] + given)


def ragged_sizes(stream_key, number_of, total, bound, skew):
    if number_of == 2:
        one = jax.random.randint(stream_key, (), max(1, total - bound), min(bound, total - 1) + 1)
        return jnp.stack([one, total - one])
    tallies = jnp.asarray(length_profile(number_of, total, bound, skew), jnp.int32)
    pairs = (number_of - 1) // 2
    source_of, receiver = tallies[1:1 + 2 * pairs:2], tallies[2:2 + 2 * pairs:2]
    slack = jnp.minimum(source_of - 1, bound - receiver)
    shifted = jax.random.randint(jax.random.fold_in(stream_key, 1), (pairs,), 0, 1 << 20) % (slack + 1)
    tallies = tallies.at[1:1 + 2 * pairs:2].set(source_of - shifted).at[2:2 + 2 * pairs:2].set(receiver + shifted)
    return tallies[jax.random.permutation(jax.random.fold_in(stream_key, 2), number_of)]


def noise(own_key, extent, scale, most, pieces=(), kind=jnp.bfloat16):
    drawn = jax.random.normal(own_key, extent, jnp.float32) * scale
    if len(pieces) > 0:
        drawn = block_scale(own_key, extent, pieces, -0.22, 0.18) * drawn
    return jnp.clip(drawn, min=-most, max=most).astype(kind)


def setup_inputs(seed: int = 0) -> dict:
    keys = jax.random.split(jax.random.key(seed), 14)
    review_cols = draw_review_cols(jax.random.fold_in(keys[13], 71), 0)
    cust_state = noise(keys[1], (CUSTOMERS, H), 1.0, 6.0, ((0, 128),))
    prod_state = noise(keys[2], (PRODUCTS, H), 1.0, 6.0, ((0, 16),))
    w_qkv = noise(keys[3], (H, 3 * H), H ** -0.5, 0.25)
    w_out = noise(keys[4], (H, H), H ** -0.5, 0.25)
    w_msg = noise(keys[5], (H, 2 * H), H ** -0.5, 0.25)
    w_cust_up = noise(keys[6], (H, H), H ** -0.5, 0.25)
    w_prod_up = noise(keys[7], (H, H), H ** -0.5, 0.25)
    w_back = noise(keys[8], (2 * H, H), (2 * H) ** -0.5, 0.1875)
    cust_slot = with_ends(ranked(keys[9], (REVIEWS,), C_ROWS, 2), jax.random.fold_in(keys[9], 3), 0, C_ROWS - 1).astype(jnp.int32)
    prod_slot = with_ends(ranked(keys[10], (REVIEWS,), P_ROWS, 2), jax.random.fold_in(keys[10], 3), 0, P_ROWS - 1).astype(jnp.int32)
    prod_pos = jax.vmap(lambda own: jax.random.permutation(own, R_DEV))(jax.random.split(keys[11], DEVICES)).reshape((DEVICES, R_DEV)).astype(jnp.int32)
    live_count = jax.vmap(lambda own: ragged_sizes(own, N_REV * N_CUST, LIVE, CSLOT, 2))(jax.random.split(keys[12], DEVICES)).reshape((DEVICES, N_REV * N_CUST)).astype(jnp.int32)
    return {"review_cols": review_cols, "cust_state": cust_state, "prod_state": prod_state, "w_qkv": w_qkv, "w_out": w_out, "w_msg": w_msg, "w_cust_up": w_cust_up, "w_prod_up": w_prod_up, "w_back": w_back, "cust_slot": cust_slot, "prod_slot": prod_slot, "prod_pos": prod_pos, "live_count": live_count}


def rms_norm(vector):
    return vector * lax.rsqrt(lax.optimization_barrier(jnp.mean(vector * vector, axis=-1, keepdims=True)) + 1e-06)

def encode(columns, w_qkv, w_out):
    count_rows = columns.shape[0]
    column_tok = columns.reshape(count_rows * NCOL, H)
    qkv_rows = jnp.dot(column_tok, w_qkv, preferred_element_type=jnp.float32).astype(jnp.bfloat16)
    qkv_rows = qkv_rows.reshape(count_rows, NCOL, 3, HEADS, HD).astype(jnp.float32)
    queries = qkv_rows[:, :, 0]
    key_part = qkv_rows[:, :, 1]
    val_part = qkv_rows[:, :, 2]
    scores = jnp.einsum('rihd,rjhd->rhij', queries, key_part) * (1.0 / math.sqrt(HD))
    scores = scores - lax.optimization_barrier(jnp.max(scores, axis=-1, keepdims=True))
    expon = jnp.exp(scores)
    att_weight = (expon / lax.optimization_barrier(jnp.sum(expon, axis=-1, keepdims=True))).astype(jnp.bfloat16)
    attended = jnp.einsum('rhij,rjhd->rihd', att_weight.astype(jnp.float32), val_part).astype(jnp.bfloat16)
    attended = attended.reshape(count_rows * NCOL, H)
    mixed_tok = column_tok.astype(jnp.float32) + jnp.dot(attended, w_out, preferred_element_type=jnp.float32)
    pooled = lax.optimization_barrier(jnp.mean(mixed_tok.reshape(count_rows, NCOL, H), axis=1))
    return rms_norm(pooled).astype(jnp.bfloat16)

def refresh(totals, counts, states, weight):
    normed_sum = (totals / jnp.sqrt(jnp.maximum(counts, 1.0))[:, None]).astype(jnp.bfloat16)
    update = jax.nn.silu(jnp.dot(normed_sum, weight, preferred_element_type=jnp.float32))
    return rms_norm(states.astype(jnp.float32) + update).astype(jnp.bfloat16)

def reference(review_cols, cust_state, prod_state, w_qkv, w_out, w_msg, w_cust_up, w_prod_up, w_back, cust_slot, prod_slot, prod_pos, live_count):
    blocks = review_cols.reshape(DEVICES, R_DEV, NCOL * H)
    review_h = lax.map(lambda block_cols: encode(block_cols, w_qkv, w_out), blocks).reshape(REVIEWS, H)
    message = jnp.dot(review_h, w_msg, preferred_element_type=jnp.float32).astype(jnp.bfloat16)
    to_cust = message[:, :H].astype(jnp.float32)
    to_prod = message[:, H:].astype(jnp.float32)
    slot_row = jnp.arange(R_DEV, dtype=jnp.int32)
    block_of = slot_row // CSLOT
    live_rows = ((slot_row % CSLOT)[None, :] < live_count[:, block_of]).reshape(REVIEWS)
    cust_global = (block_of[None, :] * C_ROWS + cust_slot.reshape(DEVICES, R_DEV)).reshape(REVIEWS).astype(jnp.int32)
    prod_global = (prod_pos // PCAP * P_ROWS + prod_slot.reshape(DEVICES, R_DEV)).reshape(REVIEWS).astype(jnp.int32)
    live_f = live_rows.astype(jnp.float32)
    cust_sum = jax.ops.segment_sum(to_cust * live_f[:, None], cust_global, CUSTOMERS)
    cust_count = jax.ops.segment_sum(live_f, cust_global, CUSTOMERS)
    new_cust = refresh(cust_sum, cust_count, cust_state, w_cust_up)
    prod_sum = jax.ops.segment_sum(to_prod * live_f[:, None], prod_global, PRODUCTS)
    prod_count = jax.ops.segment_sum(live_f, prod_global, PRODUCTS)
    new_prod = refresh(prod_sum, prod_count, prod_state, w_prod_up)
    zero_rows = jnp.zeros((REVIEWS, H), jnp.bfloat16)
    ret_cust = jnp.where(live_rows[:, None], new_cust[cust_global], zero_rows)
    ret_prod = jnp.where(live_rows[:, None], new_prod[prod_global], zero_rows)
    back_proj = jnp.dot(jnp.concatenate([ret_cust, ret_prod], axis=1), w_back, preferred_element_type=jnp.float32)
    review_out = rms_norm(review_h.astype(jnp.float32) + back_proj).astype(jnp.bfloat16)
    return (review_out, new_cust, new_prod)
```

```python
import math

import jax
import jax.numpy as jnp
from jax import lax
from jax.experimental import pallas as pl
from jax.sharding import PartitionSpec as P

H = 512
HEADS = 8
NCOL = 4
HD = 64
LANES = 128
f32 = jnp.float32
bf16 = jnp.bfloat16


def rms_norm(vector):
    return vector * lax.rsqrt(jnp.mean(vector * vector, axis=-1, keepdims=True) + 1e-06)


def head_mats():
    lane = jnp.arange(H, dtype=jnp.int32)[:, None] // HD
    col = jnp.arange(LANES, dtype=jnp.int32)[None, :]
    e = (lane == col).astype(bf16)
    return e, e.T


def encode_kernel(x_ref, wqkv_ref, wout_ref, wmsg_ref, e_ref, et_ref, h_ref, msg_ref):
    e = e_ref[...]
    et = et_ref[...]
    xs = [x_ref[:, i * H:(i + 1) * H] for i in range(NCOL)]
    q, k, v = [], [], []
    for i in range(NCOL):
        qkv = jnp.dot(xs[i], wqkv_ref[...], preferred_element_type=f32).astype(bf16)
        q.append(qkv[:, :H].astype(f32))
        k.append(qkv[:, H:2 * H].astype(f32))
        v.append(qkv[:, 2 * H:].astype(f32))
    pooled = None
    for i in range(NCOL):
        scores = []
        for j in range(NCOL):
            prod = q[i] * k[j]
            hi = prod.astype(bf16)
            lo = (prod - hi.astype(f32)).astype(bf16)
            s = jnp.dot(hi, e, preferred_element_type=f32) + jnp.dot(lo, e, preferred_element_type=f32)
            scores.append(s * (1.0 / math.sqrt(HD)))
        top = jnp.maximum(jnp.maximum(scores[0], scores[1]), jnp.maximum(scores[2], scores[3]))
        expon = [jnp.exp(s - top) for s in scores]
        total = (expon[0] + expon[1]) + (expon[2] + expon[3])
        att = None
        for j in range(NCOL):
            a = (expon[j] / total).astype(bf16)
            term = jnp.dot(a, et, preferred_element_type=f32) * v[j]
            att = term if att is None else att + term
        mixed = xs[i].astype(f32) + jnp.dot(att.astype(bf16), wout_ref[...], preferred_element_type=f32)
        pooled = mixed if pooled is None else pooled + mixed
    pooled = pooled * (1.0 / NCOL)
    h = rms_norm(pooled).astype(bf16)
    h_ref[...] = h
    msg_ref[...] = jnp.dot(h, wmsg_ref[...], preferred_element_type=f32).astype(bf16)


def encode(cols, w_qkv, w_out, w_msg, tile=128):
    rows = cols.shape[0]
    e, et = head_mats()
    full = lambda a: pl.BlockSpec(a.shape, lambda t: (0, 0))
    return pl.pallas_call(
        encode_kernel,
        grid=(rows // tile,),
        in_specs=[
            pl.BlockSpec((tile, NCOL * H), lambda t: (t, 0)),
            full(w_qkv),
            full(w_out),
            full(w_msg),
            full(e),
            full(et),
        ],
        out_specs=[
            pl.BlockSpec((tile, H), lambda t: (t, 0)),
            pl.BlockSpec((tile, 2 * H), lambda t: (t, 0)),
        ],
        out_shape=[
            jax.ShapeDtypeStruct((rows, H), bf16),
            jax.ShapeDtypeStruct((rows, 2 * H), bf16),
        ],
    )(cols, w_qkv, w_out, w_msg, e, et)


def refresh(totals, counts, states, weight):
    normed_sum = (totals / jnp.sqrt(jnp.maximum(counts, 1.0))[:, None]).astype(bf16)
    update = jax.nn.silu(jnp.dot(normed_sum, weight, preferred_element_type=f32))
    return rms_norm(states.astype(f32) + update).astype(bf16)


def pick_back(picker, states):
    return lax.dot_general(
        picker, states, (((0,), (0,)), ((), ())), preferred_element_type=f32
    ).astype(bf16)


def one_hot_rows(ids, rows):
    return (ids.reshape(1, -1) == jnp.arange(rows, dtype=jnp.int32)[:, None]).astype(bf16)


def on_device(
    review_cols,
    cust_state,
    prod_state,
    w_qkv,
    w_out,
    w_msg,
    w_cust_up,
    w_prod_up,
    w_back,
    cust_slot,
    prod_slot,
    prod_pos,
    live_count,
):
    review_rows = review_cols.shape[0]
    rev_size = lax.axis_size("rev")
    cust_size = lax.axis_size("cust")
    prod_size = lax.axis_size("prod")
    cust_owners = rev_size * cust_size
    cust_slots = review_rows // cust_owners
    prod_owners = cust_size * prod_size
    prod_slots = review_rows // prod_owners
    cust_rows = cust_state.shape[0]
    prod_rows = prod_state.shape[0]
    own_rows = prod_rows // rev_size

    review_h, message = encode(review_cols, w_qkv, w_out, w_msg)
    to_cust = message[:, :H]
    to_prod = message[:, H:]
    filled = jnp.arange(cust_slots, dtype=jnp.int32)[None, :] < live_count.reshape(cust_owners, 1)
    live = filled.reshape(review_rows)
    cust_ids = jnp.where(filled, cust_slot.reshape(cust_owners, cust_slots), -1)
    position = prod_pos.reshape(review_rows)
    perm = one_hot_rows(position, review_rows)
    prod_ids = jnp.zeros((review_rows,), jnp.int32).at[position].set(jnp.where(live, prod_slot, -1))
    prod_msgs = jnp.dot(perm, to_prod, preferred_element_type=f32).astype(bf16)

    got_rows = lax.all_to_all(
        to_cust.reshape(cust_owners, cust_slots, H), ("rev", "cust"), 0, 0, tiled=True
    )
    got_ids = lax.all_to_all(cust_ids, ("rev", "cust"), 0, 0, tiled=True)
    cust_pick = one_hot_rows(got_ids, cust_rows)
    cust_part = jnp.dot(cust_pick, got_rows.reshape(review_rows, H), preferred_element_type=f32)
    cust_cnt = jnp.sum(cust_pick, axis=1, dtype=f32)
    cust_pack = jnp.concatenate(
        [cust_part, jnp.broadcast_to(cust_cnt[:, None], (cust_rows, LANES))], axis=1
    )
    cust_other = lax.ppermute(cust_pack, "prod", [(0, 1), (1, 0)])
    cust_tot = cust_pack + cust_other
    new_cust = refresh(cust_tot[:, :H], cust_tot[:, H], cust_state, w_cust_up)
    ret_cust = lax.all_to_all(
        pick_back(cust_pick, new_cust).reshape(cust_owners, cust_slots, H),
        ("rev", "cust"),
        0,
        0,
        tiled=True,
    ).reshape(review_rows, H)

    prod_got = lax.all_to_all(
        prod_msgs.reshape(prod_owners, prod_slots, H), ("cust", "prod"), 0, 0, tiled=True
    )
    prod_got_ids = lax.all_to_all(
        prod_ids.reshape(prod_owners, prod_slots), ("cust", "prod"), 0, 0, tiled=True
    )
    prod_pick = one_hot_rows(prod_got_ids, prod_rows)
    prod_part = jnp.dot(prod_pick, prod_got.reshape(review_rows, H), preferred_element_type=f32)
    prod_cnt = jnp.sum(prod_pick, axis=1, dtype=f32)
    cnt_hi = jnp.floor(prod_cnt * (1.0 / 64.0))
    cnt_lo = prod_cnt - 64.0 * cnt_hi
    lane = jnp.arange(LANES, dtype=jnp.int32)[None, :]
    cnt_block = jnp.where(lane == 0, cnt_hi[:, None], jnp.where(lane == 1, cnt_lo[:, None], 0.0))
    prod_pack = jnp.concatenate([prod_part, cnt_block], axis=1).astype(bf16)
    spread = lax.all_to_all(
        prod_pack.reshape(rev_size, own_rows, H + LANES), "rev", 0, 0, tiled=True
    )
    whole = jnp.sum(spread.reshape(rev_size, own_rows, H + LANES).astype(f32), axis=0)
    whole_cnt = whole[:, H] * 64.0 + whole[:, H + 1]
    me = lax.axis_index("rev")
    own_state = lax.dynamic_slice_in_dim(prod_state, me * own_rows, own_rows, axis=0)
    own_new = refresh(whole[:, :H], whole_cnt, own_state, w_prod_up)
    new_prod = lax.all_to_all(
        jnp.broadcast_to(own_new[None], (rev_size, own_rows, H)), "rev", 0, 0, tiled=True
    ).reshape(prod_rows, H)
    ret_sorted = lax.all_to_all(
        pick_back(prod_pick, new_prod).reshape(prod_owners, prod_slots, H),
        ("cust", "prod"),
        0,
        0,
        tiled=True,
    ).reshape(review_rows, H)
    ret_prod = pick_back(perm, ret_sorted)

    back_proj = jnp.dot(
        jnp.concatenate([ret_cust, ret_prod], axis=1), w_back, preferred_element_type=f32
    )
    review_out = rms_norm(review_h.astype(f32) + back_proj).astype(bf16)
    return (review_out, new_cust, new_prod)


def solution(mesh):
    in_specs = (
        P(("rev", "cust", "prod"), None),
        P(("rev", "cust"), None),
        P(("cust", "prod"), None),
        P(),
        P(),
        P(),
        P(),
        P(),
        P(),
        P(("rev", "cust", "prod")),
        P(("rev", "cust", "prod")),
        P(("rev", "cust", "prod"), None),
        P(("rev", "cust", "prod"), None),
    )
    out_specs = (
        P(("rev", "cust", "prod"), None),
        P(("rev", "cust"), None),
        P(("cust", "prod"), None),
    )
    return jax.shard_map(
        on_device, mesh=mesh, in_specs=in_specs, out_specs=out_specs, check_vma=False
    )
```

```python
import math

import jax
import jax.numpy as jnp
from jax import lax
import functools

import numpy as np
from jax.experimental import pallas as pl
from jax.experimental.pallas import tpu as pltpu
from jax.sharding import PartitionSpec as P

H = 512
HEADS = 8
NCOL = 4
HD = 64
LANES = 128
f32 = jnp.float32
bf16 = jnp.bfloat16


def rms_norm(vector):
    return vector * lax.rsqrt(jnp.mean(vector * vector, axis=-1, keepdims=True) + 1e-06)


def head_mats():
    lane = jnp.arange(H, dtype=jnp.int32)[:, None] // HD
    col = jnp.arange(LANES, dtype=jnp.int32)[None, :]
    e = (lane == col).astype(bf16)
    return e, e.T


def encode_kernel(x_ref, wqkv_ref, wout_ref, wmsg_ref, e_ref, et_ref, h_ref, msg_ref):
    e = e_ref[...]
    et = et_ref[...]
    xs = [x_ref[:, i * H:(i + 1) * H] for i in range(NCOL)]
    q, k, v = [], [], []
    for i in range(NCOL):
        qkv = jnp.dot(xs[i], wqkv_ref[...], preferred_element_type=f32).astype(bf16)
        q.append(qkv[:, :H].astype(f32))
        k.append(qkv[:, H:2 * H].astype(f32))
        v.append(qkv[:, 2 * H:].astype(f32))
    pooled = None
    for i in range(NCOL):
        scores = []
        for j in range(NCOL):
            prod = q[i] * k[j]
            hi = prod.astype(bf16)
            lo = (prod - hi.astype(f32)).astype(bf16)
            s = jnp.dot(hi, e, preferred_element_type=f32) + jnp.dot(lo, e, preferred_element_type=f32)
            scores.append(s * (1.0 / math.sqrt(HD)))
        top = jnp.maximum(jnp.maximum(scores[0], scores[1]), jnp.maximum(scores[2], scores[3]))
        expon = [jnp.exp(s - top) for s in scores]
        total = (expon[0] + expon[1]) + (expon[2] + expon[3])
        att = None
        for j in range(NCOL):
            a = (expon[j] / total).astype(bf16)
            term = jnp.dot(a, et, preferred_element_type=f32) * v[j]
            att = term if att is None else att + term
        mixed = xs[i].astype(f32) + jnp.dot(att.astype(bf16), wout_ref[...], preferred_element_type=f32)
        pooled = mixed if pooled is None else pooled + mixed
    pooled = pooled * (1.0 / NCOL)
    h = rms_norm(pooled).astype(bf16)
    h_ref[...] = h
    msg_ref[...] = jnp.dot(h, wmsg_ref[...], preferred_element_type=f32).astype(bf16)


def encode(cols, w_qkv, w_out, w_msg, tile=128):
    rows = cols.shape[0]
    e, et = head_mats()
    full = lambda a: pl.BlockSpec(a.shape, lambda t: (0, 0))
    return pl.pallas_call(
        encode_kernel,
        grid=(rows // tile,),
        in_specs=[
            pl.BlockSpec((tile, NCOL * H), lambda t: (t, 0)),
            full(w_qkv),
            full(w_out),
            full(w_msg),
            full(e),
            full(et),
        ],
        out_specs=[
            pl.BlockSpec((tile, H), lambda t: (t, 0)),
            pl.BlockSpec((tile, 2 * H), lambda t: (t, 0)),
        ],
        out_shape=[
            jax.ShapeDtypeStruct((rows, H), bf16),
            jax.ShapeDtypeStruct((rows, 2 * H), bf16),
        ],
    )(cols, w_qkv, w_out, w_msg, e, et)


def _coords(axes, sizes, t):
    out = {}
    for name, size in reversed(list(zip(axes, sizes))):
        out[name] = t % size
        t = t // size
    return out

def a2a_kernel(axes, sizes, count, *refs):
    ins = refs[:count]
    outs = refs[count:2 * count]
    send_sem, recv_sem, local_sem = refs[2 * count:]
    n = 1
    for s in sizes:
        n *= s
    me = 0
    for name, size in zip(axes, sizes):
        me = me * size + lax.axis_index(name)

    def copies(t):
        dev = _coords(axes, sizes, t)
        return [
            pltpu.make_async_remote_copy(
                src_ref=ins[a].at[t], dst_ref=outs[a].at[me],
                send_sem=send_sem.at[a, t], recv_sem=recv_sem.at[a, me],
                device_id=dev, device_id_type=pl.DeviceIdType.MESH)
            for a in range(count)
        ]

    def incoming(t):
        dev = _coords(axes, sizes, t)
        return [
            pltpu.make_async_remote_copy(
                src_ref=ins[a].at[me], dst_ref=outs[a].at[t],
                send_sem=send_sem.at[a, me], recv_sem=recv_sem.at[a, t],
                device_id=dev, device_id_type=pl.DeviceIdType.MESH)
            for a in range(count)
        ]

    local = [pltpu.make_async_copy(ins[a].at[me], outs[a].at[me], local_sem.at[a]) for a in range(count)]
    for c in local:
        c.start()

    def start(o, carry):
        t = lax.rem(me + o, n)
        for c in copies(t):
            c.start()
        return carry
    lax.fori_loop(1, n, start, 0)

    def finish(o, carry):
        t = lax.rem(me + o, n)
        for c in copies(t):
            c.wait_send()
        s = lax.rem(me + n - o, n)
        for c in incoming(s):
            c.wait_recv()
        return carry
    lax.fori_loop(1, n, finish, 0)
    for c in local:
        c.wait()

def all_to_all(arrays, axes):
    axes = tuple(axes)
    sizes = tuple(lax.axis_size(a) for a in axes)
    n = int(np.prod(sizes))
    count = len(arrays)
    vmem = pl.BlockSpec(memory_space=pltpu.VMEM)
    return pl.pallas_call(
        functools.partial(a2a_kernel, axes, sizes, count),
        out_shape=[jax.ShapeDtypeStruct(a.shape, a.dtype) for a in arrays],
        in_specs=[vmem] * count,
        out_specs=[vmem] * count,
        scratch_shapes=[
            pltpu.SemaphoreType.DMA((count, n)),
            pltpu.SemaphoreType.DMA((count, n)),
            pltpu.SemaphoreType.DMA((count,)),
        ],
        compiler_params=pltpu.CompilerParams(has_side_effects=True),
    )(*arrays)


def refresh(totals, counts, states, weight):
    normed_sum = (totals / jnp.sqrt(jnp.maximum(counts, 1.0))[:, None]).astype(bf16)
    update = jax.nn.silu(jnp.dot(normed_sum, weight, preferred_element_type=f32))
    return rms_norm(states.astype(f32) + update).astype(bf16)


def pick_back(picker, states):
    return lax.dot_general(
        picker, states, (((0,), (0,)), ((), ())), preferred_element_type=f32
    ).astype(bf16)


def one_hot_rows(ids, rows):
    return (ids.reshape(1, -1) == jnp.arange(rows, dtype=jnp.int32)[:, None]).astype(bf16)


def on_device(
    review_cols,
    cust_state,
    prod_state,
    w_qkv,
    w_out,
    w_msg,
    w_cust_up,
    w_prod_up,
    w_back,
    cust_slot,
    prod_slot,
    prod_pos,
    live_count,
):
    review_rows = review_cols.shape[0]
    rev_size = lax.axis_size("rev")
    cust_size = lax.axis_size("cust")
    prod_size = lax.axis_size("prod")
    cust_owners = rev_size * cust_size
    cust_slots = review_rows // cust_owners
    prod_owners = cust_size * prod_size
    prod_slots = review_rows // prod_owners
    cust_rows = cust_state.shape[0]
    prod_rows = prod_state.shape[0]
    own_rows = prod_rows // rev_size

    review_h, message = encode(review_cols, w_qkv, w_out, w_msg)
    to_cust = message[:, :H]
    to_prod = message[:, H:]
    filled = jnp.arange(cust_slots, dtype=jnp.int32)[None, :] < live_count.reshape(cust_owners, 1)
    live = filled.reshape(review_rows)
    cust_ids = jnp.where(filled, cust_slot.reshape(cust_owners, cust_slots), -1)
    position = prod_pos.reshape(review_rows)
    perm = one_hot_rows(position, review_rows)
    prod_ids = jnp.zeros((review_rows,), jnp.int32).at[position].set(jnp.where(live, prod_slot, -1))
    prod_msgs = jnp.dot(perm, to_prod, preferred_element_type=f32).astype(bf16)

    got_rows, got_ids = all_to_all(
        [to_cust.reshape(cust_owners, cust_slots, H), cust_ids.reshape(cust_owners, 1, cust_slots)],
        ("rev", "cust"),
    )
    cust_pick = one_hot_rows(got_ids, cust_rows)
    cust_part = jnp.dot(cust_pick, got_rows.reshape(review_rows, H), preferred_element_type=f32)
    cust_cnt = jnp.sum(cust_pick, axis=1, dtype=f32)
    cust_pack = jnp.concatenate(
        [cust_part, jnp.broadcast_to(cust_cnt[:, None], (cust_rows, LANES))], axis=1
    )
    cust_other = lax.ppermute(cust_pack, "prod", [(0, 1), (1, 0)])
    cust_tot = cust_pack + cust_other
    new_cust = refresh(cust_tot[:, :H], cust_tot[:, H], cust_state, w_cust_up)
    (ret_cust,) = all_to_all(
        [pick_back(cust_pick, new_cust).reshape(cust_owners, cust_slots, H)], ("rev", "cust")
    )
    ret_cust = ret_cust.reshape(review_rows, H)

    prod_got, prod_got_ids = all_to_all(
        [prod_msgs.reshape(prod_owners, prod_slots, H), prod_ids.reshape(prod_owners, 1, prod_slots)],
        ("cust", "prod"),
    )
    prod_pick = one_hot_rows(prod_got_ids, prod_rows)
    prod_part = jnp.dot(prod_pick, prod_got.reshape(review_rows, H), preferred_element_type=f32)
    prod_cnt = jnp.sum(prod_pick, axis=1, dtype=f32)
    cnt_hi = jnp.floor(prod_cnt * (1.0 / 64.0))
    cnt_lo = prod_cnt - 64.0 * cnt_hi
    lane = jnp.arange(LANES, dtype=jnp.int32)[None, :]
    cnt_block = jnp.where(lane == 0, cnt_hi[:, None], jnp.where(lane == 1, cnt_lo[:, None], 0.0))
    prod_pack = jnp.concatenate([prod_part, cnt_block], axis=1).astype(bf16)
    (spread,) = all_to_all([prod_pack.reshape(rev_size, own_rows, H + LANES)], ("rev",))
    whole = jnp.sum(spread.reshape(rev_size, own_rows, H + LANES).astype(f32), axis=0)
    whole_cnt = whole[:, H] * 64.0 + whole[:, H + 1]
    me = lax.axis_index("rev")
    own_state = lax.dynamic_slice_in_dim(prod_state, me * own_rows, own_rows, axis=0)
    own_new = refresh(whole[:, :H], whole_cnt, own_state, w_prod_up)
    (new_prod,) = all_to_all([jnp.broadcast_to(own_new[None], (rev_size, own_rows, H))], ("rev",))
    new_prod = new_prod.reshape(prod_rows, H)
    (ret_sorted,) = all_to_all(
        [pick_back(prod_pick, new_prod).reshape(prod_owners, prod_slots, H)], ("cust", "prod")
    )
    ret_sorted = ret_sorted.reshape(review_rows, H)
    ret_prod = pick_back(perm, ret_sorted)

    back_proj = jnp.dot(
        jnp.concatenate([ret_cust, ret_prod], axis=1), w_back, preferred_element_type=f32
    )
    review_out = rms_norm(review_h.astype(f32) + back_proj).astype(bf16)
    return (review_out, new_cust, new_prod)


def solution(mesh):
    in_specs = (
        P(("rev", "cust", "prod"), None),
        P(("rev", "cust"), None),
        P(("cust", "prod"), None),
        P(),
        P(),
        P(),
        P(),
        P(),
        P(),
        P(("rev", "cust", "prod")),
        P(("rev", "cust", "prod")),
        P(("rev", "cust", "prod"), None),
        P(("rev", "cust", "prod"), None),
    )
    out_specs = (
        P(("rev", "cust", "prod"), None),
        P(("rev", "cust"), None),
        P(("cust", "prod"), None),
    )
    return jax.shard_map(
        on_device, mesh=mesh, in_specs=in_specs, out_specs=out_specs, check_vma=False
    )
```

```python
import math

import jax
import jax.numpy as jnp
from jax import lax
import functools

import numpy as np
from jax.experimental import pallas as pl
from jax.experimental.pallas import tpu as pltpu
from jax.sharding import PartitionSpec as P

H = 512
HEADS = 8
NCOL = 4
HD = 64
LANES = 128
f32 = jnp.float32
bf16 = jnp.bfloat16


def rms_norm(vector):
    return vector * lax.rsqrt(jnp.mean(vector * vector, axis=-1, keepdims=True) + 1e-06)


def head_mats():
    lane = jnp.arange(H, dtype=jnp.int32)[:, None] // HD
    col = jnp.arange(LANES, dtype=jnp.int32)[None, :]
    e = (lane == col).astype(bf16)
    return e, e.T


def encode_kernel(x_ref, wqkv_ref, wout_ref, wmsg_ref, e_ref, et_ref, h_ref, msg_ref):
    e = e_ref[...]
    et = et_ref[...]
    xs = [x_ref[:, i * H:(i + 1) * H] for i in range(NCOL)]
    q, k, v = [], [], []
    for i in range(NCOL):
        qkv = jnp.dot(xs[i], wqkv_ref[...], preferred_element_type=f32).astype(bf16)
        q.append(qkv[:, :H].astype(f32))
        k.append(qkv[:, H:2 * H].astype(f32))
        v.append(qkv[:, 2 * H:].astype(f32))
    pooled = None
    for i in range(NCOL):
        scores = []
        for j in range(NCOL):
            prod = q[i] * k[j]
            hi = prod.astype(bf16)
            lo = (prod - hi.astype(f32)).astype(bf16)
            s = jnp.dot(hi, e, preferred_element_type=f32) + jnp.dot(lo, e, preferred_element_type=f32)
            scores.append(s * (1.0 / math.sqrt(HD)))
        top = jnp.maximum(jnp.maximum(scores[0], scores[1]), jnp.maximum(scores[2], scores[3]))
        expon = [jnp.exp(s - top) for s in scores]
        total = (expon[0] + expon[1]) + (expon[2] + expon[3])
        att = None
        for j in range(NCOL):
            a = (expon[j] / total).astype(bf16)
            term = jnp.dot(a, et, preferred_element_type=f32) * v[j]
            att = term if att is None else att + term
        mixed = xs[i].astype(f32) + jnp.dot(att.astype(bf16), wout_ref[...], preferred_element_type=f32)
        pooled = mixed if pooled is None else pooled + mixed
    pooled = pooled * (1.0 / NCOL)
    h = rms_norm(pooled).astype(bf16)
    h_ref[...] = h
    msg_ref[...] = jnp.dot(h, wmsg_ref[...], preferred_element_type=f32).astype(bf16)


def encode(cols, w_qkv, w_out, w_msg, tile=128):
    rows = cols.shape[0]
    e, et = head_mats()
    full = lambda a: pl.BlockSpec(a.shape, lambda t: (0, 0))
    return pl.pallas_call(
        encode_kernel,
        grid=(rows // tile,),
        in_specs=[
            pl.BlockSpec((tile, NCOL * H), lambda t: (t, 0)),
            full(w_qkv),
            full(w_out),
            full(w_msg),
            full(e),
            full(et),
        ],
        out_specs=[
            pl.BlockSpec((tile, H), lambda t: (t, 0)),
            pl.BlockSpec((tile, 2 * H), lambda t: (t, 0)),
        ],
        out_shape=[
            jax.ShapeDtypeStruct((rows, H), bf16),
            jax.ShapeDtypeStruct((rows, 2 * H), bf16),
        ],
    )(cols, w_qkv, w_out, w_msg, e, et)


MESH = pl.DeviceIdType.MESH


def _coords(axes, sizes, t):
    out = {}
    for name, size in reversed(list(zip(axes, sizes))):
        out[name] = t % size
        t = t // size
    return out


def exchange_kernel(plan, *refs):
    total = sum(c for _, _, c in plan)
    ins, outs = refs[:total], refs[total:2 * total]
    sems = refs[2 * total:]
    groups = []
    at, s_at = 0, 0
    for axes, sizes, count in plan:
        n = int(np.prod(sizes))
        me = 0
        for name, size in zip(axes, sizes):
            me = me * size + lax.axis_index(name)
        groups.append(dict(axes=axes, sizes=sizes, n=n, me=me, ins=ins[at:at + count], outs=outs[at:at + count],
                           send=sems[s_at], recv=sems[s_at + 1], local=sems[s_at + 2]))
        at += count
        s_at += 3

    barrier = pltpu.get_barrier_semaphore()
    expected = 0
    for g in groups:
        n, me = g["n"], g["me"]
        def greet(o, carry, g=g, n=n, me=me):
            t = lax.rem(me + o, n)
            pl.semaphore_signal(barrier, inc=1, device_id=_coords(g["axes"], g["sizes"], t), device_id_type=MESH)
            return carry
        lax.fori_loop(1, n, greet, 0)
        expected += n - 1
    pl.semaphore_wait(barrier, expected)

    def remote(g, a, src, dst, t):
        return pltpu.make_async_remote_copy(
            src_ref=g["ins"][a].at[src], dst_ref=g["outs"][a].at[dst],
            send_sem=g["send"].at[a, src], recv_sem=g["recv"].at[a, dst],
            device_id=_coords(g["axes"], g["sizes"], t), device_id_type=MESH)

    for g in groups:
        for a in range(len(g["ins"])):
            pltpu.make_async_copy(g["ins"][a].at[g["me"]], g["outs"][a].at[g["me"]], g["local"].at[a]).start()
    for g in groups:
        n, me = g["n"], g["me"]
        def start(o, carry, g=g, n=n, me=me):
            t = lax.rem(me + o, n)
            for a in range(len(g["ins"])):
                remote(g, a, t, me, t).start()
            return carry
        lax.fori_loop(1, n, start, 0)
    for g in groups:
        n, me = g["n"], g["me"]
        def finish(o, carry, g=g, n=n, me=me):
            t = lax.rem(me + o, n)
            s = lax.rem(me + n - o, n)
            for a in range(len(g["ins"])):
                remote(g, a, t, me, t).wait_send()
                remote(g, a, me, s, s).wait_recv()
            return carry
        lax.fori_loop(1, n, finish, 0)
        for a in range(len(g["ins"])):
            pltpu.make_async_copy(g["ins"][a].at[me], g["outs"][a].at[me], g["local"].at[a]).wait()


def exchange(groups, collective_id):
    plan, arrays, scratch = [], [], []
    for axes, arrs in groups:
        axes = tuple(axes)
        sizes = tuple(lax.axis_size(a) for a in axes)
        n = int(np.prod(sizes))
        plan.append((axes, sizes, len(arrs)))
        arrays.extend(arrs)
        scratch += [pltpu.SemaphoreType.DMA((len(arrs), n)), pltpu.SemaphoreType.DMA((len(arrs), n)),
                    pltpu.SemaphoreType.DMA((len(arrs),))]
    vmem = pl.BlockSpec(memory_space=pltpu.VMEM)
    return pl.pallas_call(
        functools.partial(exchange_kernel, tuple(plan)),
        out_shape=[jax.ShapeDtypeStruct(a.shape, a.dtype) for a in arrays],
        in_specs=[vmem] * len(arrays),
        out_specs=[vmem] * len(arrays),
        scratch_shapes=scratch,
        compiler_params=pltpu.CompilerParams(has_side_effects=True, collective_id=collective_id),
    )(*arrays)


def refresh(totals, counts, states, weight):
    normed_sum = (totals / jnp.sqrt(jnp.maximum(counts, 1.0))[:, None]).astype(bf16)
    update = jax.nn.silu(jnp.dot(normed_sum, weight, preferred_element_type=f32))
    return rms_norm(states.astype(f32) + update).astype(bf16)


def pick_back(picker, states):
    return lax.dot_general(
        picker, states, (((0,), (0,)), ((), ())), preferred_element_type=f32
    ).astype(bf16)


def one_hot_rows(ids, rows):
    return (ids.reshape(1, -1) == jnp.arange(rows, dtype=jnp.int32)[:, None]).astype(bf16)


def on_device(
    review_cols,
    cust_state,
    prod_state,
    w_qkv,
    w_out,
    w_msg,
    w_cust_up,
    w_prod_up,
    w_back,
    cust_slot,
    prod_slot,
    prod_pos,
    live_count,
):
    review_rows = review_cols.shape[0]
    rev_size = lax.axis_size("rev")
    cust_size = lax.axis_size("cust")
    prod_size = lax.axis_size("prod")
    cust_owners = rev_size * cust_size
    cust_slots = review_rows // cust_owners
    prod_owners = cust_size * prod_size
    prod_slots = review_rows // prod_owners
    cust_rows = cust_state.shape[0]
    prod_rows = prod_state.shape[0]
    own_rows = prod_rows // rev_size

    review_h, message = encode(review_cols, w_qkv, w_out, w_msg)
    to_cust = message[:, :H]
    to_prod = message[:, H:]
    filled = jnp.arange(cust_slots, dtype=jnp.int32)[None, :] < live_count.reshape(cust_owners, 1)
    live = filled.reshape(review_rows)
    cust_ids = jnp.where(filled, cust_slot.reshape(cust_owners, cust_slots), -1)
    position = prod_pos.reshape(review_rows)
    perm = one_hot_rows(position, review_rows)
    prod_ids = jnp.zeros((review_rows,), jnp.int32).at[position].set(jnp.where(live, prod_slot, -1))
    prod_msgs = jnp.dot(perm, to_prod, preferred_element_type=f32).astype(bf16)

    got_rows, got_ids, prod_got, prod_got_ids = exchange(
        [
            (("rev", "cust"), [to_cust.reshape(cust_owners, cust_slots, H),
                               cust_ids.reshape(cust_owners, 1, cust_slots)]),
            (("cust", "prod"), [prod_msgs.reshape(prod_owners, prod_slots, H),
                                prod_ids.reshape(prod_owners, 1, prod_slots)]),
        ],
        0,
    )
    cust_pick = one_hot_rows(got_ids, cust_rows)
    cust_part = jnp.dot(cust_pick, got_rows.reshape(review_rows, H), preferred_element_type=f32)
    cust_cnt = jnp.sum(cust_pick, axis=1, dtype=f32)
    cust_pack = jnp.concatenate(
        [cust_part, jnp.broadcast_to(cust_cnt[:, None], (cust_rows, LANES))], axis=1
    )
    prod_pick = one_hot_rows(prod_got_ids, prod_rows)
    prod_part = jnp.dot(prod_pick, prod_got.reshape(review_rows, H), preferred_element_type=f32)
    prod_cnt = jnp.sum(prod_pick, axis=1, dtype=f32)
    cnt_hi = jnp.floor(prod_cnt * (1.0 / 64.0))
    cnt_lo = prod_cnt - 64.0 * cnt_hi
    lane = jnp.arange(LANES, dtype=jnp.int32)[None, :]
    cnt_block = jnp.where(lane == 0, cnt_hi[:, None], jnp.where(lane == 1, cnt_lo[:, None], 0.0))
    prod_pack = jnp.concatenate([prod_part, cnt_block], axis=1).astype(bf16)

    cust_both, spread = exchange(
        [
            (("prod",), [jnp.broadcast_to(cust_pack[None], (prod_size, cust_rows, H + LANES))]),
            (("rev",), [prod_pack.reshape(rev_size, own_rows, H + LANES)]),
        ],
        1,
    )
    cust_tot = jnp.sum(cust_both, axis=0)
    new_cust = refresh(cust_tot[:, :H], cust_tot[:, H], cust_state, w_cust_up)
    whole = jnp.sum(spread.astype(f32), axis=0)
    whole_cnt = whole[:, H] * 64.0 + whole[:, H + 1]
    me = lax.axis_index("rev")
    own_state = lax.dynamic_slice_in_dim(prod_state, me * own_rows, own_rows, axis=0)
    own_new = refresh(whole[:, :H], whole_cnt, own_state, w_prod_up)

    new_prod, ret_cust = exchange(
        [
            (("rev",), [jnp.broadcast_to(own_new[None], (rev_size, own_rows, H))]),
            (("rev", "cust"), [pick_back(cust_pick, new_cust).reshape(cust_owners, cust_slots, H)]),
        ],
        2,
    )
    new_prod = new_prod.reshape(prod_rows, H)
    ret_cust = ret_cust.reshape(review_rows, H)
    (ret_sorted,) = exchange(
        [(("cust", "prod"), [pick_back(prod_pick, new_prod).reshape(prod_owners, prod_slots, H)])], 3
    )
    ret_prod = pick_back(perm, ret_sorted.reshape(review_rows, H))

    back_proj = jnp.dot(
        jnp.concatenate([ret_cust, ret_prod], axis=1), w_back, preferred_element_type=f32
    )
    review_out = rms_norm(review_h.astype(f32) + back_proj).astype(bf16)
    return (review_out, new_cust, new_prod)


def solution(mesh):
    in_specs = (
        P(("rev", "cust", "prod"), None),
        P(("rev", "cust"), None),
        P(("cust", "prod"), None),
        P(),
        P(),
        P(),
        P(),
        P(),
        P(),
        P(("rev", "cust", "prod")),
        P(("rev", "cust", "prod")),
        P(("rev", "cust", "prod"), None),
        P(("rev", "cust", "prod"), None),
    )
    out_specs = (
        P(("rev", "cust", "prod"), None),
        P(("rev", "cust"), None),
        P(("cust", "prod"), None),
    )
    return jax.shard_map(
        on_device, mesh=mesh, in_specs=in_specs, out_specs=out_specs, check_vma=False
    )
```

```python
import math

import jax
import jax.numpy as jnp
from jax import lax
import functools

import numpy as np
from jax.experimental import pallas as pl
from jax.experimental.pallas import tpu as pltpu
from jax.sharding import PartitionSpec as P

H = 512
HEADS = 8
NCOL = 4
HD = 64
LANES = 128
f32 = jnp.float32
bf16 = jnp.bfloat16


def rms_norm(vector):
    return vector * lax.rsqrt(jnp.mean(vector * vector, axis=-1, keepdims=True) + 1e-06)


def head_mats():
    lane = jnp.arange(H, dtype=jnp.int32)[:, None] // HD
    col = jnp.arange(LANES, dtype=jnp.int32)[None, :]
    e = (lane == col).astype(bf16)
    return e, e.T


def encode_kernel(x_ref, wqkv_ref, wout_ref, wmsg_ref, e_ref, et_ref, h_ref, msg_ref):
    e = e_ref[...]
    et = et_ref[...]
    xs = [x_ref[:, i * H:(i + 1) * H] for i in range(NCOL)]
    q, k, v = [], [], []
    for i in range(NCOL):
        qkv = jnp.dot(xs[i], wqkv_ref[...], preferred_element_type=f32).astype(bf16)
        q.append(qkv[:, :H].astype(f32))
        k.append(qkv[:, H:2 * H].astype(f32))
        v.append(qkv[:, 2 * H:].astype(f32))
    pooled = None
    for i in range(NCOL):
        scores = []
        for j in range(NCOL):
            prod = q[i] * k[j]
            hi = prod.astype(bf16)
            lo = (prod - hi.astype(f32)).astype(bf16)
            s = jnp.dot(hi, e, preferred_element_type=f32) + jnp.dot(lo, e, preferred_element_type=f32)
            scores.append(s * (1.0 / math.sqrt(HD)))
        top = jnp.maximum(jnp.maximum(scores[0], scores[1]), jnp.maximum(scores[2], scores[3]))
        expon = [jnp.exp(s - top) for s in scores]
        total = (expon[0] + expon[1]) + (expon[2] + expon[3])
        att = None
        for j in range(NCOL):
            a = (expon[j] / total).astype(bf16)
            term = jnp.dot(a, et, preferred_element_type=f32) * v[j]
            att = term if att is None else att + term
        mixed = xs[i].astype(f32) + jnp.dot(att.astype(bf16), wout_ref[...], preferred_element_type=f32)
        pooled = mixed if pooled is None else pooled + mixed
    pooled = pooled * (1.0 / NCOL)
    h = rms_norm(pooled).astype(bf16)
    h_ref[...] = h
    msg_ref[...] = jnp.dot(h, wmsg_ref[...], preferred_element_type=f32).astype(bf16)


def encode(cols, w_qkv, w_out, w_msg, tile=128):
    rows = cols.shape[0]
    e, et = head_mats()
    full = lambda a: pl.BlockSpec(a.shape, lambda t: (0, 0))
    return pl.pallas_call(
        encode_kernel,
        grid=(rows // tile,),
        in_specs=[
            pl.BlockSpec((tile, NCOL * H), lambda t: (t, 0)),
            full(w_qkv),
            full(w_out),
            full(w_msg),
            full(e),
            full(et),
        ],
        out_specs=[
            pl.BlockSpec((tile, H), lambda t: (t, 0)),
            pl.BlockSpec((tile, 2 * H), lambda t: (t, 0)),
        ],
        out_shape=[
            jax.ShapeDtypeStruct((rows, H), bf16),
            jax.ShapeDtypeStruct((rows, 2 * H), bf16),
        ],
    )(cols, w_qkv, w_out, w_msg, e, et)


MESH = pl.DeviceIdType.MESH


def _coords(axes, sizes, t):
    out = {}
    for name, size in reversed(list(zip(axes, sizes))):
        out[name] = t % size
        t = t // size
    return out


def exchange_kernel(plan, *refs):
    total = sum(c for _, _, c in plan)
    ins, outs = refs[:total], refs[total:2 * total]
    sems = refs[2 * total:]
    groups = []
    at, s_at = 0, 0
    for axes, sizes, count in plan:
        n = int(np.prod(sizes))
        me = 0
        for name, size in zip(axes, sizes):
            me = me * size + lax.axis_index(name)
        groups.append(dict(axes=axes, sizes=sizes, n=n, me=me, ins=ins[at:at + count], outs=outs[at:at + count],
                           send=sems[s_at], recv=sems[s_at + 1], local=sems[s_at + 2]))
        at += count
        s_at += 3

    barrier = pltpu.get_barrier_semaphore()
    expected = 0
    for g in groups:
        n, me = g["n"], g["me"]
        def greet(o, carry, g=g, n=n, me=me):
            t = lax.rem(me + o, n)
            pl.semaphore_signal(barrier, inc=1, device_id=_coords(g["axes"], g["sizes"], t), device_id_type=MESH)
            return carry
        lax.fori_loop(1, n, greet, 0)
        expected += n - 1
    pl.semaphore_wait(barrier, expected)

    def remote(g, a, src, dst, t):
        return pltpu.make_async_remote_copy(
            src_ref=g["ins"][a].at[src], dst_ref=g["outs"][a].at[dst],
            send_sem=g["send"].at[a, src], recv_sem=g["recv"].at[a, dst],
            device_id=_coords(g["axes"], g["sizes"], t), device_id_type=MESH)

    for g in groups:
        for a in range(len(g["ins"])):
            pltpu.make_async_copy(g["ins"][a].at[g["me"]], g["outs"][a].at[g["me"]], g["local"].at[a]).start()
    for g in groups:
        n, me = g["n"], g["me"]
        def start(o, carry, g=g, n=n, me=me):
            t = lax.rem(me + o, n)
            for a in range(len(g["ins"])):
                remote(g, a, t, me, t).start()
            return carry
        lax.fori_loop(1, n, start, 0)
    for g in groups:
        n, me = g["n"], g["me"]
        def finish(o, carry, g=g, n=n, me=me):
            t = lax.rem(me + o, n)
            s = lax.rem(me + n - o, n)
            for a in range(len(g["ins"])):
                remote(g, a, t, me, t).wait_send()
                remote(g, a, me, s, s).wait_recv()
            return carry
        lax.fori_loop(1, n, finish, 0)
        for a in range(len(g["ins"])):
            pltpu.make_async_copy(g["ins"][a].at[me], g["outs"][a].at[me], g["local"].at[a]).wait()


def exchange(groups, collective_id):
    plan, arrays, scratch = [], [], []
    for axes, arrs in groups:
        axes = tuple(axes)
        sizes = tuple(lax.axis_size(a) for a in axes)
        n = int(np.prod(sizes))
        plan.append((axes, sizes, len(arrs)))
        arrays.extend(arrs)
        scratch += [pltpu.SemaphoreType.DMA((len(arrs), n)), pltpu.SemaphoreType.DMA((len(arrs), n)),
                    pltpu.SemaphoreType.DMA((len(arrs),))]
    vmem = pl.BlockSpec(memory_space=pltpu.VMEM)
    return pl.pallas_call(
        functools.partial(exchange_kernel, tuple(plan)),
        out_shape=[jax.ShapeDtypeStruct(a.shape, a.dtype) for a in arrays],
        in_specs=[vmem] * len(arrays),
        out_specs=[vmem] * len(arrays),
        scratch_shapes=scratch,
        compiler_params=pltpu.CompilerParams(has_side_effects=True, collective_id=collective_id),
    )(*arrays)


def refresh(totals, counts, states, weight):
    normed_sum = (totals / jnp.sqrt(jnp.maximum(counts, 1.0))[:, None]).astype(bf16)
    update = jax.nn.silu(jnp.dot(normed_sum, weight, preferred_element_type=f32))
    return rms_norm(states.astype(f32) + update).astype(bf16)


def pick_back(picker, states):
    return lax.dot_general(
        picker, states, (((0,), (0,)), ((), ())), preferred_element_type=f32
    ).astype(bf16)


def one_hot_rows(ids, rows):
    return (ids.reshape(1, -1) == jnp.arange(rows, dtype=jnp.int32)[:, None]).astype(bf16)


def on_device(
    review_cols,
    cust_state,
    prod_state,
    w_qkv,
    w_out,
    w_msg,
    w_cust_up,
    w_prod_up,
    w_back,
    cust_slot,
    prod_slot,
    prod_pos,
    live_count,
):
    review_rows = review_cols.shape[0]
    rev_size = lax.axis_size("rev")
    cust_size = lax.axis_size("cust")
    prod_size = lax.axis_size("prod")
    cust_owners = rev_size * cust_size
    cust_slots = review_rows // cust_owners
    prod_owners = cust_size * prod_size
    prod_slots = review_rows // prod_owners
    cust_rows = cust_state.shape[0]
    prod_rows = prod_state.shape[0]
    own_rows = prod_rows // rev_size

    review_h, message = encode(review_cols, w_qkv, w_out, w_msg)
    to_cust = message[:, :H]
    to_prod = message[:, H:]
    filled = jnp.arange(cust_slots, dtype=jnp.int32)[None, :] < live_count.reshape(cust_owners, 1)
    live = filled.reshape(review_rows)
    cust_ids = jnp.where(filled, cust_slot.reshape(cust_owners, cust_slots), -1)
    position = prod_pos.reshape(review_rows)
    perm = one_hot_rows(position, review_rows)
    prod_ids = jnp.zeros((review_rows,), jnp.int32).at[position].set(jnp.where(live, prod_slot, -1))
    prod_msgs = jnp.dot(perm, to_prod, preferred_element_type=f32).astype(bf16)

    got_rows, got_ids, prod_got, prod_got_ids = exchange(
        [
            (("rev", "cust"), [to_cust.reshape(cust_owners, cust_slots * H // LANES, LANES),
                               cust_ids.reshape(cust_owners, 1, cust_slots)]),
            (("cust", "prod"), [prod_msgs.reshape(prod_owners, prod_slots, H),
                                prod_ids.reshape(prod_owners, 1, prod_slots)]),
        ],
        0,
    )
    cust_pick = one_hot_rows(got_ids, cust_rows)
    cust_part = jnp.dot(cust_pick, got_rows.reshape(review_rows, H), preferred_element_type=f32)
    cust_cnt = jnp.sum(cust_pick, axis=1, dtype=f32)
    cust_pack = jnp.concatenate(
        [cust_part, jnp.broadcast_to(cust_cnt[:, None], (cust_rows, LANES))], axis=1
    )
    prod_pick = one_hot_rows(prod_got_ids, prod_rows)
    prod_part = jnp.dot(prod_pick, prod_got.reshape(review_rows, H), preferred_element_type=f32)
    prod_cnt = jnp.sum(prod_pick, axis=1, dtype=f32)
    cnt_hi = jnp.floor(prod_cnt * (1.0 / 64.0))
    cnt_lo = prod_cnt - 64.0 * cnt_hi
    lane = jnp.arange(LANES, dtype=jnp.int32)[None, :]
    cnt_block = jnp.where(lane == 0, cnt_hi[:, None], jnp.where(lane == 1, cnt_lo[:, None], 0.0))
    prod_pack = jnp.concatenate([prod_part, cnt_block], axis=1).astype(bf16)

    cust_both, spread = exchange(
        [
            (("prod",), [jnp.broadcast_to(cust_pack[None], (prod_size, cust_rows, H + LANES))]),
            (("rev",), [prod_pack.reshape(rev_size, own_rows, H + LANES)]),
        ],
        1,
    )
    cust_tot = jnp.sum(cust_both, axis=0)
    new_cust = refresh(cust_tot[:, :H], cust_tot[:, H], cust_state, w_cust_up)
    whole = jnp.sum(spread.astype(f32), axis=0)
    whole_cnt = whole[:, H] * 64.0 + whole[:, H + 1]
    me = lax.axis_index("rev")
    own_state = lax.dynamic_slice_in_dim(prod_state, me * own_rows, own_rows, axis=0)
    own_new = refresh(whole[:, :H], whole_cnt, own_state, w_prod_up)

    new_prod, ret_cust = exchange(
        [
            (("rev",), [jnp.broadcast_to(own_new[None], (rev_size, own_rows, H))]),
            (("rev", "cust"), [pick_back(cust_pick, new_cust).reshape(cust_owners, cust_slots * H // LANES, LANES)]),
        ],
        2,
    )
    new_prod = new_prod.reshape(prod_rows, H)
    ret_cust = ret_cust.reshape(review_rows, H)
    (ret_sorted,) = exchange(
        [(("cust", "prod"), [pick_back(prod_pick, new_prod).reshape(prod_owners, prod_slots, H)])], 3
    )
    ret_prod = pick_back(perm, ret_sorted.reshape(review_rows, H))

    back_proj = jnp.dot(
        jnp.concatenate([ret_cust, ret_prod], axis=1), w_back, preferred_element_type=f32
    )
    review_out = rms_norm(review_h.astype(f32) + back_proj).astype(bf16)
    return (review_out, new_cust, new_prod)


def solution(mesh):
    in_specs = (
        P(("rev", "cust", "prod"), None),
        P(("rev", "cust"), None),
        P(("cust", "prod"), None),
        P(),
        P(),
        P(),
        P(),
        P(),
        P(),
        P(("rev", "cust", "prod")),
        P(("rev", "cust", "prod")),
        P(("rev", "cust", "prod"), None),
        P(("rev", "cust", "prod"), None),
    )
    out_specs = (
        P(("rev", "cust", "prod"), None),
        P(("rev", "cust"), None),
        P(("cust", "prod"), None),
    )
    return jax.shard_map(
        on_device, mesh=mesh, in_specs=in_specs, out_specs=out_specs, check_vma=False
    )
```

```python
import math

import jax
import jax.numpy as jnp
from jax import lax
import functools

import numpy as np
from jax.experimental import pallas as pl
from jax.experimental.pallas import tpu as pltpu
from jax.sharding import PartitionSpec as P

H = 512
HEADS = 8
NCOL = 4
HD = 64
LANES = 128
f32 = jnp.float32
bf16 = jnp.bfloat16


def rms_norm(vector):
    return vector * lax.rsqrt(jnp.mean(vector * vector, axis=-1, keepdims=True) + 1e-06)


def head_mats():
    lane = jnp.arange(H, dtype=jnp.int32)[:, None] // HD
    col = jnp.arange(LANES, dtype=jnp.int32)[None, :]
    e = (lane == col).astype(bf16)
    return e, e.T


def encode_kernel(x_ref, wqkv_ref, wout_ref, wmsg_ref, e_ref, et_ref, h_ref, msg_ref):
    e = e_ref[...]
    et = et_ref[...]
    xs = [x_ref[:, i * H:(i + 1) * H] for i in range(NCOL)]
    q, k, v = [], [], []
    for i in range(NCOL):
        qkv = jnp.dot(xs[i], wqkv_ref[...], preferred_element_type=f32).astype(bf16)
        q.append(qkv[:, :H].astype(f32))
        k.append(qkv[:, H:2 * H].astype(f32))
        v.append(qkv[:, 2 * H:].astype(f32))
    pooled = None
    for i in range(NCOL):
        scores = []
        for j in range(NCOL):
            prod = q[i] * k[j]
            hi = prod.astype(bf16)
            lo = (prod - hi.astype(f32)).astype(bf16)
            s = jnp.dot(hi, e, preferred_element_type=f32) + jnp.dot(lo, e, preferred_element_type=f32)
            scores.append(s * (1.0 / math.sqrt(HD)))
        top = jnp.maximum(jnp.maximum(scores[0], scores[1]), jnp.maximum(scores[2], scores[3]))
        expon = [jnp.exp(s - top) for s in scores]
        total = (expon[0] + expon[1]) + (expon[2] + expon[3])
        att = None
        for j in range(NCOL):
            a = (expon[j] / total).astype(bf16)
            term = jnp.dot(a, et, preferred_element_type=f32) * v[j]
            att = term if att is None else att + term
        mixed = xs[i].astype(f32) + jnp.dot(att.astype(bf16), wout_ref[...], preferred_element_type=f32)
        pooled = mixed if pooled is None else pooled + mixed
    pooled = pooled * (1.0 / NCOL)
    h = rms_norm(pooled).astype(bf16)
    h_ref[...] = h
    msg_ref[...] = jnp.dot(h, wmsg_ref[...], preferred_element_type=f32).astype(bf16)


def encode(cols, w_qkv, w_out, w_msg, tile=128):
    rows = cols.shape[0]
    e, et = head_mats()
    full = lambda a: pl.BlockSpec(a.shape, lambda t: (0, 0))
    return pl.pallas_call(
        encode_kernel,
        grid=(rows // tile,),
        in_specs=[
            pl.BlockSpec((tile, NCOL * H), lambda t: (t, 0)),
            full(w_qkv),
            full(w_out),
            full(w_msg),
            full(e),
            full(et),
        ],
        out_specs=[
            pl.BlockSpec((tile, H), lambda t: (t, 0)),
            pl.BlockSpec((tile, 2 * H), lambda t: (t, 0)),
        ],
        out_shape=[
            jax.ShapeDtypeStruct((rows, H), bf16),
            jax.ShapeDtypeStruct((rows, 2 * H), bf16),
        ],
    )(cols, w_qkv, w_out, w_msg, e, et)


MESH = pl.DeviceIdType.MESH


def _coords(axes, sizes, t):
    out = {}
    for name, size in reversed(list(zip(axes, sizes))):
        out[name] = t % size
        t = t // size
    return out


def exchange_kernel(plan, *refs):
    total = sum(c for _, _, c in plan)
    ins, outs = refs[:total], refs[total:2 * total]
    sems = refs[2 * total:]
    groups = []
    at, s_at = 0, 0
    for axes, sizes, count in plan:
        n = int(np.prod(sizes))
        me = 0
        for name, size in zip(axes, sizes):
            me = me * size + lax.axis_index(name)
        groups.append(dict(axes=axes, sizes=sizes, n=n, me=me, ins=ins[at:at + count], outs=outs[at:at + count],
                           send=sems[s_at], recv=sems[s_at + 1], local=sems[s_at + 2]))
        at += count
        s_at += 3

    barrier = pltpu.get_barrier_semaphore()
    expected = 0
    for g in groups:
        n, me = g["n"], g["me"]
        def greet(o, carry, g=g, n=n, me=me):
            t = lax.rem(me + o, n)
            pl.semaphore_signal(barrier, inc=1, device_id=_coords(g["axes"], g["sizes"], t), device_id_type=MESH)
            return carry
        lax.fori_loop(1, n, greet, 0)
        expected += n - 1
    pl.semaphore_wait(barrier, expected)

    def remote(g, a, src, dst, t):
        return pltpu.make_async_remote_copy(
            src_ref=g["ins"][a].at[src], dst_ref=g["outs"][a].at[dst],
            send_sem=g["send"].at[a, src], recv_sem=g["recv"].at[a, dst],
            device_id=_coords(g["axes"], g["sizes"], t), device_id_type=MESH)

    for g in groups:
        for a in range(len(g["ins"])):
            pltpu.make_async_copy(g["ins"][a].at[g["me"]], g["outs"][a].at[g["me"]], g["local"].at[a]).start()
    for g in groups:
        n, me = g["n"], g["me"]
        def start(o, carry, g=g, n=n, me=me):
            t = lax.rem(me + o, n)
            for a in range(len(g["ins"])):
                remote(g, a, t, me, t).start()
            return carry
        lax.fori_loop(1, n, start, 0)
    for g in groups:
        n, me = g["n"], g["me"]
        def finish(o, carry, g=g, n=n, me=me):
            t = lax.rem(me + o, n)
            s = lax.rem(me + n - o, n)
            for a in range(len(g["ins"])):
                remote(g, a, t, me, t).wait_send()
                remote(g, a, me, s, s).wait_recv()
            return carry
        lax.fori_loop(1, n, finish, 0)
        for a in range(len(g["ins"])):
            pltpu.make_async_copy(g["ins"][a].at[me], g["outs"][a].at[me], g["local"].at[a]).wait()


def exchange(groups, collective_id):
    plan, arrays, scratch = [], [], []
    for axes, arrs in groups:
        axes = tuple(axes)
        sizes = tuple(lax.axis_size(a) for a in axes)
        n = int(np.prod(sizes))
        plan.append((axes, sizes, len(arrs)))
        arrays.extend(arrs)
        scratch += [pltpu.SemaphoreType.DMA((len(arrs), n)), pltpu.SemaphoreType.DMA((len(arrs), n)),
                    pltpu.SemaphoreType.DMA((len(arrs),))]
    vmem = pl.BlockSpec(memory_space=pltpu.VMEM)
    return pl.pallas_call(
        functools.partial(exchange_kernel, tuple(plan)),
        out_shape=[jax.ShapeDtypeStruct(a.shape, a.dtype) for a in arrays],
        in_specs=[vmem] * len(arrays),
        out_specs=[vmem] * len(arrays),
        scratch_shapes=scratch,
        compiler_params=pltpu.CompilerParams(has_side_effects=True, collective_id=collective_id),
    )(*arrays)


def refresh(totals, counts, states, weight):
    normed_sum = (totals / jnp.sqrt(jnp.maximum(counts, 1.0))[:, None]).astype(bf16)
    update = jax.nn.silu(jnp.dot(normed_sum, weight, preferred_element_type=f32))
    return rms_norm(states.astype(f32) + update).astype(bf16)


def pick_back(picker, states):
    return lax.dot_general(
        picker, states, (((0,), (0,)), ((), ())), preferred_element_type=f32
    ).astype(bf16)


def one_hot_rows(ids, rows):
    return (ids.reshape(1, -1) == jnp.arange(rows, dtype=jnp.int32)[:, None]).astype(bf16)


def on_device(
    review_cols,
    cust_state,
    prod_state,
    w_qkv,
    w_out,
    w_msg,
    w_cust_up,
    w_prod_up,
    w_back,
    cust_slot,
    prod_slot,
    prod_pos,
    live_count,
):
    review_rows = review_cols.shape[0]
    rev_size = lax.axis_size("rev")
    cust_size = lax.axis_size("cust")
    prod_size = lax.axis_size("prod")
    cust_owners = rev_size * cust_size
    cust_slots = review_rows // cust_owners
    prod_owners = cust_size * prod_size
    prod_slots = review_rows // prod_owners
    cust_rows = cust_state.shape[0]
    prod_rows = prod_state.shape[0]
    own_rows = prod_rows // rev_size

    review_h, message = encode(review_cols, w_qkv, w_out, w_msg)
    to_cust = message[:, :H]
    to_prod = message[:, H:]
    filled = jnp.arange(cust_slots, dtype=jnp.int32)[None, :] < live_count.reshape(cust_owners, 1)
    live = filled.reshape(review_rows)
    cust_ids = jnp.where(filled, cust_slot.reshape(cust_owners, cust_slots), -1)
    position = prod_pos.reshape(review_rows)
    perm = one_hot_rows(position, review_rows)
    prod_ids = jnp.zeros((review_rows,), jnp.int32).at[position].set(jnp.where(live, prod_slot, -1))
    prod_msgs = jnp.dot(perm, to_prod, preferred_element_type=f32).astype(bf16)

    cust_run = cust_size * cust_slots
    stage_rows = rev_size * cust_slots
    sent1, ids1, prod_got, prod_got_ids = exchange(
        [
            (("rev",), [to_cust.reshape(rev_size, cust_run, H), cust_ids.reshape(rev_size, 1, cust_run)]),
            (("cust", "prod"), [prod_msgs.reshape(prod_owners, prod_slots, H),
                                prod_ids.reshape(prod_owners, 1, prod_slots)]),
        ],
        0,
    )
    prod_pick = one_hot_rows(prod_got_ids, prod_rows)
    prod_part = jnp.dot(prod_pick, prod_got.reshape(review_rows, H), preferred_element_type=f32)
    prod_cnt = jnp.sum(prod_pick, axis=1, dtype=f32)
    cnt_hi = jnp.floor(prod_cnt * (1.0 / 64.0))
    cnt_lo = prod_cnt - 64.0 * cnt_hi
    lane = jnp.arange(LANES, dtype=jnp.int32)[None, :]
    cnt_block = jnp.where(lane == 0, cnt_hi[:, None], jnp.where(lane == 1, cnt_lo[:, None], 0.0))
    prod_pack = jnp.concatenate([prod_part, cnt_block], axis=1).astype(bf16)
    stage2 = sent1.reshape(rev_size, cust_size, cust_slots, H).transpose(1, 0, 2, 3)
    ids2 = ids1.reshape(rev_size, cust_size, cust_slots).transpose(1, 0, 2)
    got_rows, got_ids, spread = exchange(
        [
            (("cust",), [stage2.reshape(cust_size, stage_rows, H), ids2.reshape(cust_size, 1, stage_rows)]),
            (("rev",), [prod_pack.reshape(rev_size, own_rows, H + LANES)]),
        ],
        1,
    )
    cust_pick = one_hot_rows(got_ids, cust_rows)
    cust_part = jnp.dot(cust_pick, got_rows.reshape(review_rows, H), preferred_element_type=f32)
    cust_cnt = jnp.sum(cust_pick, axis=1, dtype=f32)
    cust_pack = jnp.concatenate(
        [cust_part, jnp.broadcast_to(cust_cnt[:, None], (cust_rows, LANES))], axis=1
    )
    whole = jnp.sum(spread.astype(f32), axis=0)
    whole_cnt = whole[:, H] * 64.0 + whole[:, H + 1]
    me = lax.axis_index("rev")
    own_state = lax.dynamic_slice_in_dim(prod_state, me * own_rows, own_rows, axis=0)
    own_new = refresh(whole[:, :H], whole_cnt, own_state, w_prod_up)

    cust_both, new_prod = exchange(
        [
            (("prod",), [jnp.broadcast_to(cust_pack[None], (prod_size, cust_rows, H + LANES))]),
            (("rev",), [jnp.broadcast_to(own_new[None], (rev_size, own_rows, H))]),
        ],
        2,
    )
    cust_tot = jnp.sum(cust_both, axis=0)
    new_cust = refresh(cust_tot[:, :H], cust_tot[:, H], cust_state, w_cust_up)
    new_prod = new_prod.reshape(prod_rows, H)

    reply = pick_back(cust_pick, new_cust).reshape(cust_size, rev_size, cust_slots, H).transpose(1, 0, 2, 3)
    back1, ret_sorted = exchange(
        [
            (("rev",), [reply.reshape(rev_size, cust_run, H)]),
            (("cust", "prod"), [pick_back(prod_pick, new_prod).reshape(prod_owners, prod_slots, H)]),
        ],
        3,
    )
    back2 = back1.reshape(rev_size, cust_size, cust_slots, H).transpose(1, 0, 2, 3)
    (ret_cust,) = exchange([(("cust",), [back2.reshape(cust_size, stage_rows, H)])], 4)
    ret_cust = ret_cust.reshape(cust_size, rev_size, cust_slots, H).transpose(1, 0, 2, 3).reshape(review_rows, H)
    ret_prod = pick_back(perm, ret_sorted.reshape(review_rows, H))

    back_proj = jnp.dot(
        jnp.concatenate([ret_cust, ret_prod], axis=1), w_back, preferred_element_type=f32
    )
    review_out = rms_norm(review_h.astype(f32) + back_proj).astype(bf16)
    return (review_out, new_cust, new_prod)


def solution(mesh):
    in_specs = (
        P(("rev", "cust", "prod"), None),
        P(("rev", "cust"), None),
        P(("cust", "prod"), None),
        P(),
        P(),
        P(),
        P(),
        P(),
        P(),
        P(("rev", "cust", "prod")),
        P(("rev", "cust", "prod")),
        P(("rev", "cust", "prod"), None),
        P(("rev", "cust", "prod"), None),
    )
    out_specs = (
        P(("rev", "cust", "prod"), None),
        P(("rev", "cust"), None),
        P(("cust", "prod"), None),
    )
    return jax.shard_map(
        on_device, mesh=mesh, in_specs=in_specs, out_specs=out_specs, check_vma=False
    )
```

```python
import math

import jax
import jax.numpy as jnp
from jax import lax
import functools

import numpy as np
from jax.experimental import pallas as pl
from jax.experimental.pallas import tpu as pltpu
from jax.sharding import PartitionSpec as P

H = 512
HEADS = 8
NCOL = 4
HD = 64
LANES = 128
f32 = jnp.float32
bf16 = jnp.bfloat16


def rms_norm(vector):
    return vector * lax.rsqrt(jnp.mean(vector * vector, axis=-1, keepdims=True) + 1e-06)


def head_mats():
    lane = jnp.arange(H, dtype=jnp.int32)[:, None] // HD
    col = jnp.arange(LANES, dtype=jnp.int32)[None, :]
    e = (lane == col).astype(bf16)
    return e, e.T


def encode_kernel(x_ref, wqkv_ref, wout_ref, wmsg_ref, e_ref, et_ref, h_ref, msg_ref):
    e = e_ref[...]
    et = et_ref[...]
    xs = [x_ref[:, i * H:(i + 1) * H] for i in range(NCOL)]
    q, k, v = [], [], []
    for i in range(NCOL):
        qkv = jnp.dot(xs[i], wqkv_ref[...], preferred_element_type=f32).astype(bf16)
        q.append(qkv[:, :H].astype(f32))
        k.append(qkv[:, H:2 * H].astype(f32))
        v.append(qkv[:, 2 * H:].astype(f32))
    pooled = None
    for i in range(NCOL):
        scores = []
        for j in range(NCOL):
            prod = q[i] * k[j]
            hi = prod.astype(bf16)
            lo = (prod - hi.astype(f32)).astype(bf16)
            s = jnp.dot(hi, e, preferred_element_type=f32) + jnp.dot(lo, e, preferred_element_type=f32)
            scores.append(s * (1.0 / math.sqrt(HD)))
        top = jnp.maximum(jnp.maximum(scores[0], scores[1]), jnp.maximum(scores[2], scores[3]))
        expon = [jnp.exp(s - top) for s in scores]
        total = (expon[0] + expon[1]) + (expon[2] + expon[3])
        att = None
        for j in range(NCOL):
            a = (expon[j] / total).astype(bf16)
            term = jnp.dot(a, et, preferred_element_type=f32) * v[j]
            att = term if att is None else att + term
        mixed = xs[i].astype(f32) + jnp.dot(att.astype(bf16), wout_ref[...], preferred_element_type=f32)
        pooled = mixed if pooled is None else pooled + mixed
    pooled = pooled * (1.0 / NCOL)
    h = rms_norm(pooled).astype(bf16)
    h_ref[...] = h
    msg_ref[...] = jnp.dot(h, wmsg_ref[...], preferred_element_type=f32).astype(bf16)


def encode(cols, w_qkv, w_out, w_msg, tile=128):
    rows = cols.shape[0]
    e, et = head_mats()
    full = lambda a: pl.BlockSpec(a.shape, lambda t: (0, 0))
    return pl.pallas_call(
        encode_kernel,
        grid=(rows // tile,),
        in_specs=[
            pl.BlockSpec((tile, NCOL * H), lambda t: (t, 0)),
            full(w_qkv),
            full(w_out),
            full(w_msg),
            full(e),
            full(et),
        ],
        out_specs=[
            pl.BlockSpec((tile, H), lambda t: (t, 0)),
            pl.BlockSpec((tile, 2 * H), lambda t: (t, 0)),
        ],
        out_shape=[
            jax.ShapeDtypeStruct((rows, H), bf16),
            jax.ShapeDtypeStruct((rows, 2 * H), bf16),
        ],
    )(cols, w_qkv, w_out, w_msg, e, et)


MESH = pl.DeviceIdType.MESH


def _coords(axes, sizes, t):
    out = {}
    for name, size in reversed(list(zip(axes, sizes))):
        out[name] = t % size
        t = t // size
    return out


def exchange_kernel(plan, *refs):
    total = sum(c for _, _, c in plan)
    ins, outs = refs[:total], refs[total:2 * total]
    sems = refs[2 * total:]
    groups = []
    at, s_at = 0, 0
    for axes, sizes, count in plan:
        n = int(np.prod(sizes))
        me = 0
        for name, size in zip(axes, sizes):
            me = me * size + lax.axis_index(name)
        groups.append(dict(axes=axes, sizes=sizes, n=n, me=me, ins=ins[at:at + count], outs=outs[at:at + count],
                           send=sems[s_at], recv=sems[s_at + 1], local=sems[s_at + 2]))
        at += count
        s_at += 3

    barrier = pltpu.get_barrier_semaphore()
    expected = 0
    for g in groups:
        n, me = g["n"], g["me"]
        def greet(o, carry, g=g, n=n, me=me):
            t = lax.rem(me + o, n)
            pl.semaphore_signal(barrier, inc=1, device_id=_coords(g["axes"], g["sizes"], t), device_id_type=MESH)
            return carry
        lax.fori_loop(1, n, greet, 0)
        expected += n - 1
    pl.semaphore_wait(barrier, expected)

    def remote(g, a, src, dst, t):
        if g["ins"][a].shape[0] == 1:
            src = 0
        return pltpu.make_async_remote_copy(
            src_ref=g["ins"][a].at[src], dst_ref=g["outs"][a].at[dst],
            send_sem=g["send"].at[a, src], recv_sem=g["recv"].at[a, dst],
            device_id=_coords(g["axes"], g["sizes"], t), device_id_type=MESH)

    def own(g, a):
        src = 0 if g["ins"][a].shape[0] == 1 else g["me"]
        return pltpu.make_async_copy(g["ins"][a].at[src], g["outs"][a].at[g["me"]], g["local"].at[a])

    for g in groups:
        for a in range(len(g["ins"])):
            own(g, a).start()
    for g in groups:
        n, me = g["n"], g["me"]
        def start(o, carry, g=g, n=n, me=me):
            t = lax.rem(me + o, n)
            for a in range(len(g["ins"])):
                remote(g, a, t, me, t).start()
            return carry
        lax.fori_loop(1, n, start, 0)
    for g in groups:
        n, me = g["n"], g["me"]
        def finish(o, carry, g=g, n=n, me=me):
            t = lax.rem(me + o, n)
            s = lax.rem(me + n - o, n)
            for a in range(len(g["ins"])):
                remote(g, a, t, me, t).wait_send()
                remote(g, a, me, s, s).wait_recv()
            return carry
        lax.fori_loop(1, n, finish, 0)
        for a in range(len(g["ins"])):
            own(g, a).wait()


def exchange(groups, collective_id):
    plan, arrays, scratch, n_of = [], [], [], []
    for axes, arrs in groups:
        axes = tuple(axes)
        sizes = tuple(lax.axis_size(a) for a in axes)
        n = int(np.prod(sizes))
        plan.append((axes, sizes, len(arrs)))
        arrays.extend(arrs)
        n_of.extend([n] * len(arrs))
        scratch += [pltpu.SemaphoreType.DMA((len(arrs), n)), pltpu.SemaphoreType.DMA((len(arrs), n)),
                    pltpu.SemaphoreType.DMA((len(arrs),))]
    vmem = pl.BlockSpec(memory_space=pltpu.VMEM)
    return pl.pallas_call(
        functools.partial(exchange_kernel, tuple(plan)),
        out_shape=[jax.ShapeDtypeStruct((n_of[i],) + a.shape[1:], a.dtype) for i, a in enumerate(arrays)],
        in_specs=[vmem] * len(arrays),
        out_specs=[vmem] * len(arrays),
        scratch_shapes=scratch,
        compiler_params=pltpu.CompilerParams(has_side_effects=True, collective_id=collective_id),
    )(*arrays)


def refresh(totals, counts, states, weight):
    normed_sum = (totals / jnp.sqrt(jnp.maximum(counts, 1.0))[:, None]).astype(bf16)
    update = jax.nn.silu(jnp.dot(normed_sum, weight, preferred_element_type=f32))
    return rms_norm(states.astype(f32) + update).astype(bf16)


def pick_back(picker, states):
    return lax.dot_general(
        picker, states, (((0,), (0,)), ((), ())), preferred_element_type=f32
    ).astype(bf16)


def one_hot_rows(ids, rows):
    return (ids.reshape(1, -1) == jnp.arange(rows, dtype=jnp.int32)[:, None]).astype(bf16)


def on_device(
    review_cols,
    cust_state,
    prod_state,
    w_qkv,
    w_out,
    w_msg,
    w_cust_up,
    w_prod_up,
    w_back,
    cust_slot,
    prod_slot,
    prod_pos,
    live_count,
):
    review_rows = review_cols.shape[0]
    rev_size = lax.axis_size("rev")
    cust_size = lax.axis_size("cust")
    prod_size = lax.axis_size("prod")
    cust_owners = rev_size * cust_size
    cust_slots = review_rows // cust_owners
    prod_owners = cust_size * prod_size
    prod_slots = review_rows // prod_owners
    cust_rows = cust_state.shape[0]
    prod_rows = prod_state.shape[0]
    own_rows = prod_rows // rev_size

    review_h, message = encode(review_cols, w_qkv, w_out, w_msg)
    to_cust = message[:, :H]
    to_prod = message[:, H:]
    filled = jnp.arange(cust_slots, dtype=jnp.int32)[None, :] < live_count.reshape(cust_owners, 1)
    live = filled.reshape(review_rows)
    cust_ids = jnp.where(filled, cust_slot.reshape(cust_owners, cust_slots), -1)
    position = prod_pos.reshape(review_rows)
    perm = one_hot_rows(position, review_rows)
    id_plus = jnp.where(live, prod_slot + 1, 0)
    id_lane = jnp.arange(LANES, dtype=jnp.int32)[None, :]
    id_cols = jnp.where(
        id_lane == 0, (id_plus // 32)[:, None], jnp.where(id_lane == 1, (id_plus % 32)[:, None], 0)
    ).astype(bf16)
    sorted_all = jnp.dot(perm, jnp.concatenate([to_prod, id_cols], axis=1), preferred_element_type=f32)
    prod_msgs = sorted_all[:, :H].astype(bf16)
    prod_ids = (sorted_all[:, H] * 32.0 + sorted_all[:, H + 1]).astype(jnp.int32) - 1

    cust_run = cust_size * cust_slots
    stage_rows = rev_size * cust_slots
    sent1, ids1, prod_got, prod_got_ids = exchange(
        [
            (("rev",), [to_cust.reshape(rev_size, cust_run, H), cust_ids.reshape(rev_size, 1, cust_run)]),
            (("cust", "prod"), [prod_msgs.reshape(prod_owners, prod_slots, H),
                                prod_ids.reshape(prod_owners, 1, prod_slots)]),
        ],
        0,
    )
    prod_pick = one_hot_rows(prod_got_ids, prod_rows)
    prod_part = jnp.dot(prod_pick, prod_got.reshape(review_rows, H), preferred_element_type=f32)
    prod_cnt = jnp.sum(prod_pick, axis=1, dtype=f32)
    cnt_hi = jnp.floor(prod_cnt * (1.0 / 64.0))
    cnt_lo = prod_cnt - 64.0 * cnt_hi
    lane = jnp.arange(LANES, dtype=jnp.int32)[None, :]
    cnt_block = jnp.where(lane == 0, cnt_hi[:, None], jnp.where(lane == 1, cnt_lo[:, None], 0.0))
    prod_pack = jnp.concatenate([prod_part, cnt_block], axis=1).astype(bf16)
    stage2 = sent1.reshape(rev_size, cust_size, cust_slots, H).transpose(1, 0, 2, 3)
    ids2 = ids1.reshape(rev_size, cust_size, cust_slots).transpose(1, 0, 2)
    got_rows, got_ids, spread = exchange(
        [
            (("cust",), [stage2.reshape(cust_size, stage_rows, H), ids2.reshape(cust_size, 1, stage_rows)]),
            (("rev",), [prod_pack.reshape(rev_size, own_rows, H + LANES)]),
        ],
        1,
    )
    cust_pick = one_hot_rows(got_ids, cust_rows)
    cust_part = jnp.dot(cust_pick, got_rows.reshape(review_rows, H), preferred_element_type=f32)
    cust_cnt = jnp.sum(cust_pick, axis=1, dtype=f32)
    cust_pack = jnp.concatenate(
        [cust_part, jnp.broadcast_to(cust_cnt[:, None], (cust_rows, LANES))], axis=1
    )
    whole = jnp.sum(spread.astype(f32), axis=0)
    whole_cnt = whole[:, H] * 64.0 + whole[:, H + 1]
    me = lax.axis_index("rev")
    own_state = lax.dynamic_slice_in_dim(prod_state, me * own_rows, own_rows, axis=0)
    own_new = refresh(whole[:, :H], whole_cnt, own_state, w_prod_up)

    cust_both, new_prod = exchange(
        [
            (("prod",), [cust_pack[None]]),
            (("rev",), [own_new[None]]),
        ],
        2,
    )
    cust_tot = cust_both[0] + cust_both[1]
    new_cust = refresh(cust_tot[:, :H], cust_tot[:, H], cust_state, w_cust_up)
    new_prod = new_prod.reshape(prod_rows, H)

    reply = pick_back(cust_pick, new_cust).reshape(cust_size, rev_size, cust_slots, H).transpose(1, 0, 2, 3)
    back1, ret_sorted = exchange(
        [
            (("rev",), [reply.reshape(rev_size, cust_run, H)]),
            (("cust", "prod"), [pick_back(prod_pick, new_prod).reshape(prod_owners, prod_slots, H)]),
        ],
        3,
    )
    back2 = back1.reshape(rev_size, cust_size, cust_slots, H).transpose(1, 0, 2, 3)
    (ret_cust,) = exchange([(("cust",), [back2.reshape(cust_size, stage_rows, H)])], 4)
    ret_cust = ret_cust.reshape(cust_size, rev_size, cust_slots, H).transpose(1, 0, 2, 3).reshape(review_rows, H)
    ret_prod = pick_back(perm, ret_sorted.reshape(review_rows, H))

    back_proj = jnp.dot(
        jnp.concatenate([ret_cust, ret_prod], axis=1), w_back, preferred_element_type=f32
    )
    review_out = rms_norm(review_h.astype(f32) + back_proj).astype(bf16)
    return (review_out, new_cust, new_prod)


def solution(mesh):
    in_specs = (
        P(("rev", "cust", "prod"), None),
        P(("rev", "cust"), None),
        P(("cust", "prod"), None),
        P(),
        P(),
        P(),
        P(),
        P(),
        P(),
        P(("rev", "cust", "prod")),
        P(("rev", "cust", "prod")),
        P(("rev", "cust", "prod"), None),
        P(("rev", "cust", "prod"), None),
    )
    out_specs = (
        P(("rev", "cust", "prod"), None),
        P(("rev", "cust"), None),
        P(("cust", "prod"), None),
    )
    return jax.shard_map(
        on_device, mesh=mesh, in_specs=in_specs, out_specs=out_specs, check_vma=False
    )
```

```python
import math

import jax
import jax.numpy as jnp
from jax import lax
import functools

import numpy as np
from jax.experimental import pallas as pl
from jax.experimental.pallas import tpu as pltpu
from jax.sharding import PartitionSpec as P

H = 512
HEADS = 8
NCOL = 4
HD = 64
LANES = 128
f32 = jnp.float32
bf16 = jnp.bfloat16


def rms_norm(vector):
    return vector * lax.rsqrt(jnp.mean(vector * vector, axis=-1, keepdims=True) + 1e-06)


def head_mats():
    lane = jnp.arange(H, dtype=jnp.int32)[:, None] // HD
    col = jnp.arange(LANES, dtype=jnp.int32)[None, :]
    e = (lane == col).astype(bf16)
    return e, e.T


def encode_kernel(x_ref, wqkv_ref, wout_ref, wmsg_ref, e_ref, et_ref, h_ref, msg_ref):
    e = e_ref[...]
    et = et_ref[...]
    xs = [x_ref[:, i * H:(i + 1) * H] for i in range(NCOL)]
    q, k, v = [], [], []
    for i in range(NCOL):
        qkv = jnp.dot(xs[i], wqkv_ref[...], preferred_element_type=f32).astype(bf16)
        q.append(qkv[:, :H].astype(f32))
        k.append(qkv[:, H:2 * H].astype(f32))
        v.append(qkv[:, 2 * H:].astype(f32))
    pooled = None
    for i in range(NCOL):
        scores = []
        for j in range(NCOL):
            prod = q[i] * k[j]
            hi = prod.astype(bf16)
            lo = (prod - hi.astype(f32)).astype(bf16)
            s = jnp.dot(hi, e, preferred_element_type=f32) + jnp.dot(lo, e, preferred_element_type=f32)
            scores.append(s * (1.0 / math.sqrt(HD)))
        top = jnp.maximum(jnp.maximum(scores[0], scores[1]), jnp.maximum(scores[2], scores[3]))
        expon = [jnp.exp(s - top) for s in scores]
        total = (expon[0] + expon[1]) + (expon[2] + expon[3])
        att = None
        for j in range(NCOL):
            a = (expon[j] / total).astype(bf16)
            term = jnp.dot(a, et, preferred_element_type=f32) * v[j]
            att = term if att is None else att + term
        mixed = xs[i].astype(f32) + jnp.dot(att.astype(bf16), wout_ref[...], preferred_element_type=f32)
        pooled = mixed if pooled is None else pooled + mixed
    pooled = pooled * (1.0 / NCOL)
    h = rms_norm(pooled).astype(bf16)
    h_ref[...] = h
    msg_ref[...] = jnp.dot(h, wmsg_ref[...], preferred_element_type=f32).astype(bf16)


def encode(cols, w_qkv, w_out, w_msg, tile=128):
    rows = cols.shape[0]
    e, et = head_mats()
    full = lambda a: pl.BlockSpec(a.shape, lambda t: (0, 0))
    return pl.pallas_call(
        encode_kernel,
        grid=(rows // tile,),
        in_specs=[
            pl.BlockSpec((tile, NCOL * H), lambda t: (t, 0)),
            full(w_qkv),
            full(w_out),
            full(w_msg),
            full(e),
            full(et),
        ],
        out_specs=[
            pl.BlockSpec((tile, H), lambda t: (t, 0)),
            pl.BlockSpec((tile, 2 * H), lambda t: (t, 0)),
        ],
        out_shape=[
            jax.ShapeDtypeStruct((rows, H), bf16),
            jax.ShapeDtypeStruct((rows, 2 * H), bf16),
        ],
    )(cols, w_qkv, w_out, w_msg, e, et)


MESH = pl.DeviceIdType.MESH


def _coords(axes, sizes, t):
    out = {}
    for name, size in reversed(list(zip(axes, sizes))):
        out[name] = t % size
        t = t // size
    return out


def _step(o):
    return ((o + 1) // 2) * (2 * (o % 2) - 1)


def exchange_kernel(plan, *refs):
    total = sum(c for _, _, c in plan)
    ins, outs = refs[:total], refs[total:2 * total]
    sems = refs[2 * total:]
    groups = []
    at, s_at = 0, 0
    for axes, sizes, count in plan:
        n = int(np.prod(sizes))
        me = 0
        for name, size in zip(axes, sizes):
            me = me * size + lax.axis_index(name)
        groups.append(dict(axes=axes, sizes=sizes, n=n, me=me, ins=ins[at:at + count], outs=outs[at:at + count],
                           send=sems[s_at], recv=sems[s_at + 1], local=sems[s_at + 2]))
        at += count
        s_at += 3

    barrier = pltpu.get_barrier_semaphore()
    expected = 0
    for g in groups:
        n, me = g["n"], g["me"]
        def greet(o, carry, g=g, n=n, me=me):
            t = lax.rem(me + o, n)
            pl.semaphore_signal(barrier, inc=1, device_id=_coords(g["axes"], g["sizes"], t), device_id_type=MESH)
            return carry
        lax.fori_loop(1, n, greet, 0)
        expected += n - 1
    pl.semaphore_wait(barrier, expected)

    def remote(g, a, src, dst, t):
        if g["ins"][a].shape[0] == 1:
            src = 0
        return pltpu.make_async_remote_copy(
            src_ref=g["ins"][a].at[src], dst_ref=g["outs"][a].at[dst],
            send_sem=g["send"].at[a, src], recv_sem=g["recv"].at[a, dst],
            device_id=_coords(g["axes"], g["sizes"], t), device_id_type=MESH)

    def own(g, a):
        src = 0 if g["ins"][a].shape[0] == 1 else g["me"]
        return pltpu.make_async_copy(g["ins"][a].at[src], g["outs"][a].at[g["me"]], g["local"].at[a])

    for g in groups:
        for a in range(len(g["ins"])):
            own(g, a).start()
    for g in groups:
        n, me = g["n"], g["me"]
        def start(o, carry, g=g, n=n, me=me):
            t = lax.rem(me + _step(o) + n, n)
            for a in range(len(g["ins"])):
                remote(g, a, t, me, t).start()
            return carry
        lax.fori_loop(1, n, start, 0)
    for g in groups:
        n, me = g["n"], g["me"]
        def finish(o, carry, g=g, n=n, me=me):
            t = lax.rem(me + _step(o) + n, n)
            s = lax.rem(me - _step(o) + n, n)
            for a in range(len(g["ins"])):
                remote(g, a, t, me, t).wait_send()
                remote(g, a, me, s, s).wait_recv()
            return carry
        lax.fori_loop(1, n, finish, 0)
        for a in range(len(g["ins"])):
            own(g, a).wait()


def exchange(groups, collective_id):
    plan, arrays, scratch, n_of = [], [], [], []
    for axes, arrs in groups:
        axes = tuple(axes)
        sizes = tuple(lax.axis_size(a) for a in axes)
        n = int(np.prod(sizes))
        plan.append((axes, sizes, len(arrs)))
        arrays.extend(arrs)
        n_of.extend([n] * len(arrs))
        scratch += [pltpu.SemaphoreType.DMA((len(arrs), n)), pltpu.SemaphoreType.DMA((len(arrs), n)),
                    pltpu.SemaphoreType.DMA((len(arrs),))]
    vmem = pl.BlockSpec(memory_space=pltpu.VMEM)
    return pl.pallas_call(
        functools.partial(exchange_kernel, tuple(plan)),
        out_shape=[jax.ShapeDtypeStruct((n_of[i],) + a.shape[1:], a.dtype) for i, a in enumerate(arrays)],
        in_specs=[vmem] * len(arrays),
        out_specs=[vmem] * len(arrays),
        scratch_shapes=scratch,
        compiler_params=pltpu.CompilerParams(has_side_effects=True, collective_id=collective_id),
    )(*arrays)


def refresh(totals, counts, states, weight):
    normed_sum = (totals / jnp.sqrt(jnp.maximum(counts, 1.0))[:, None]).astype(bf16)
    update = jax.nn.silu(jnp.dot(normed_sum, weight, preferred_element_type=f32))
    return rms_norm(states.astype(f32) + update).astype(bf16)


def pick_back(picker, states):
    return lax.dot_general(
        picker, states, (((0,), (0,)), ((), ())), preferred_element_type=f32
    ).astype(bf16)


def one_hot_rows(ids, rows):
    return (ids.reshape(1, -1) == jnp.arange(rows, dtype=jnp.int32)[:, None]).astype(bf16)


def on_device(
    review_cols,
    cust_state,
    prod_state,
    w_qkv,
    w_out,
    w_msg,
    w_cust_up,
    w_prod_up,
    w_back,
    cust_slot,
    prod_slot,
    prod_pos,
    live_count,
):
    review_rows = review_cols.shape[0]
    rev_size = lax.axis_size("rev")
    cust_size = lax.axis_size("cust")
    prod_size = lax.axis_size("prod")
    cust_owners = rev_size * cust_size
    cust_slots = review_rows // cust_owners
    prod_owners = cust_size * prod_size
    prod_slots = review_rows // prod_owners
    cust_rows = cust_state.shape[0]
    prod_rows = prod_state.shape[0]
    own_rows = prod_rows // rev_size

    review_h, message = encode(review_cols, w_qkv, w_out, w_msg)
    to_cust = message[:, :H]
    to_prod = message[:, H:]
    filled = jnp.arange(cust_slots, dtype=jnp.int32)[None, :] < live_count.reshape(cust_owners, 1)
    live = filled.reshape(review_rows)
    cust_ids = jnp.where(filled, cust_slot.reshape(cust_owners, cust_slots), -1)
    position = prod_pos.reshape(review_rows)
    perm = one_hot_rows(position, review_rows)
    id_plus = jnp.where(live, prod_slot + 1, 0)
    id_lane = jnp.arange(LANES, dtype=jnp.int32)[None, :]
    id_cols = jnp.where(
        id_lane == 0, (id_plus // 32)[:, None], jnp.where(id_lane == 1, (id_plus % 32)[:, None], 0)
    ).astype(bf16)
    sorted_all = jnp.dot(perm, jnp.concatenate([to_prod, id_cols], axis=1), preferred_element_type=f32)
    prod_msgs = sorted_all[:, :H].astype(bf16)
    prod_ids = (sorted_all[:, H] * 32.0 + sorted_all[:, H + 1]).astype(jnp.int32) - 1

    cust_run = cust_size * cust_slots
    stage_rows = rev_size * cust_slots
    sent1, ids1, prod_got, prod_got_ids = exchange(
        [
            (("rev",), [to_cust.reshape(rev_size, cust_run, H), cust_ids.reshape(rev_size, 1, cust_run)]),
            (("cust", "prod"), [prod_msgs.reshape(prod_owners, prod_slots, H),
                                prod_ids.reshape(prod_owners, 1, prod_slots)]),
        ],
        0,
    )
    prod_pick = one_hot_rows(prod_got_ids, prod_rows)
    prod_part = jnp.dot(prod_pick, prod_got.reshape(review_rows, H), preferred_element_type=f32)
    prod_cnt = jnp.sum(prod_pick, axis=1, dtype=f32)
    cnt_hi = jnp.floor(prod_cnt * (1.0 / 64.0))
    cnt_lo = prod_cnt - 64.0 * cnt_hi
    lane = jnp.arange(LANES, dtype=jnp.int32)[None, :]
    cnt_block = jnp.where(lane == 0, cnt_hi[:, None], jnp.where(lane == 1, cnt_lo[:, None], 0.0))
    prod_pack = jnp.concatenate([prod_part, cnt_block], axis=1).astype(bf16)
    stage2 = sent1.reshape(rev_size, cust_size, cust_slots, H).transpose(1, 0, 2, 3)
    ids2 = ids1.reshape(rev_size, cust_size, cust_slots).transpose(1, 0, 2)
    got_rows, got_ids, spread = exchange(
        [
            (("cust",), [stage2.reshape(cust_size, stage_rows, H), ids2.reshape(cust_size, 1, stage_rows)]),
            (("rev",), [prod_pack.reshape(rev_size, own_rows, H + LANES)]),
        ],
        1,
    )
    cust_pick = one_hot_rows(got_ids, cust_rows)
    cust_part = jnp.dot(cust_pick, got_rows.reshape(review_rows, H), preferred_element_type=f32)
    cust_cnt = jnp.sum(cust_pick, axis=1, dtype=f32)
    cust_pack = jnp.concatenate(
        [cust_part, jnp.broadcast_to(cust_cnt[:, None], (cust_rows, LANES))], axis=1
    )
    whole = jnp.sum(spread.astype(f32), axis=0)
    whole_cnt = whole[:, H] * 64.0 + whole[:, H + 1]
    me = lax.axis_index("rev")
    own_state = lax.dynamic_slice_in_dim(prod_state, me * own_rows, own_rows, axis=0)
    own_new = refresh(whole[:, :H], whole_cnt, own_state, w_prod_up)

    cust_both, new_prod = exchange(
        [
            (("prod",), [cust_pack[None]]),
            (("rev",), [own_new[None]]),
        ],
        2,
    )
    cust_tot = cust_both[0] + cust_both[1]
    new_cust = refresh(cust_tot[:, :H], cust_tot[:, H], cust_state, w_cust_up)
    new_prod = new_prod.reshape(prod_rows, H)

    reply = pick_back(cust_pick, new_cust).reshape(cust_size, rev_size, cust_slots, H).transpose(1, 0, 2, 3)
    back1, ret_sorted = exchange(
        [
            (("rev",), [reply.reshape(rev_size, cust_run, H)]),
            (("cust", "prod"), [pick_back(prod_pick, new_prod).reshape(prod_owners, prod_slots, H)]),
        ],
        3,
    )
    back2 = back1.reshape(rev_size, cust_size, cust_slots, H).transpose(1, 0, 2, 3)
    (ret_cust,) = exchange([(("cust",), [back2.reshape(cust_size, stage_rows, H)])], 4)
    ret_cust = ret_cust.reshape(cust_size, rev_size, cust_slots, H).transpose(1, 0, 2, 3).reshape(review_rows, H)
    ret_prod = pick_back(perm, ret_sorted.reshape(review_rows, H))

    back_proj = jnp.dot(
        jnp.concatenate([ret_cust, ret_prod], axis=1), w_back, preferred_element_type=f32
    )
    review_out = rms_norm(review_h.astype(f32) + back_proj).astype(bf16)
    return (review_out, new_cust, new_prod)


def solution(mesh):
    in_specs = (
        P(("rev", "cust", "prod"), None),
        P(("rev", "cust"), None),
        P(("cust", "prod"), None),
        P(),
        P(),
        P(),
        P(),
        P(),
        P(),
        P(("rev", "cust", "prod")),
        P(("rev", "cust", "prod")),
        P(("rev", "cust", "prod"), None),
        P(("rev", "cust", "prod"), None),
    )
    out_specs = (
        P(("rev", "cust", "prod"), None),
        P(("rev", "cust"), None),
        P(("cust", "prod"), None),
    )
    return jax.shard_map(
        on_device, mesh=mesh, in_specs=in_specs, out_specs=out_specs, check_vma=False
    )
```

```python
import math

import jax
import jax.numpy as jnp
from jax import lax
import functools

import numpy as np
from jax.experimental import pallas as pl
from jax.experimental.pallas import tpu as pltpu
from jax.sharding import PartitionSpec as P

H = 512
HEADS = 8
NCOL = 4
HD = 64
LANES = 128
f32 = jnp.float32
bf16 = jnp.bfloat16


def rms_norm(vector):
    return vector * lax.rsqrt(jnp.mean(vector * vector, axis=-1, keepdims=True) + 1e-06)


def head_mats():
    lane = jnp.arange(H, dtype=jnp.int32)[:, None] // HD
    col = jnp.arange(LANES, dtype=jnp.int32)[None, :]
    e = (lane == col).astype(bf16)
    return e, e.T


def encode_kernel(x_ref, wqkv_ref, wout_ref, wmsg_ref, e_ref, et_ref, h_ref, msg_ref):
    e = e_ref[...]
    et = et_ref[...]
    xs = [x_ref[:, i * H:(i + 1) * H] for i in range(NCOL)]
    q, k, v = [], [], []
    for i in range(NCOL):
        qkv = jnp.dot(xs[i], wqkv_ref[...], preferred_element_type=f32).astype(bf16)
        q.append(qkv[:, :H].astype(f32))
        k.append(qkv[:, H:2 * H].astype(f32))
        v.append(qkv[:, 2 * H:].astype(f32))
    pooled = None
    for i in range(NCOL):
        scores = []
        for j in range(NCOL):
            prod = q[i] * k[j]
            hi = prod.astype(bf16)
            lo = (prod - hi.astype(f32)).astype(bf16)
            s = jnp.dot(hi, e, preferred_element_type=f32) + jnp.dot(lo, e, preferred_element_type=f32)
            scores.append(s * (1.0 / math.sqrt(HD)))
        top = jnp.maximum(jnp.maximum(scores[0], scores[1]), jnp.maximum(scores[2], scores[3]))
        expon = [jnp.exp(s - top) for s in scores]
        total = (expon[0] + expon[1]) + (expon[2] + expon[3])
        att = None
        for j in range(NCOL):
            a = (expon[j] / total).astype(bf16)
            term = jnp.dot(a, et, preferred_element_type=f32) * v[j]
            att = term if att is None else att + term
        mixed = xs[i].astype(f32) + jnp.dot(att.astype(bf16), wout_ref[...], preferred_element_type=f32)
        pooled = mixed if pooled is None else pooled + mixed
    pooled = pooled * (1.0 / NCOL)
    h = rms_norm(pooled).astype(bf16)
    h_ref[...] = h
    msg_ref[...] = jnp.dot(h, wmsg_ref[...], preferred_element_type=f32).astype(bf16)


def encode(cols, w_qkv, w_out, w_msg, tile=256):
    rows = cols.shape[0]
    e, et = head_mats()
    full = lambda a: pl.BlockSpec(a.shape, lambda t: (0, 0))
    return pl.pallas_call(
        encode_kernel,
        grid=(rows // tile,),
        in_specs=[
            pl.BlockSpec((tile, NCOL * H), lambda t: (t, 0)),
            full(w_qkv),
            full(w_out),
            full(w_msg),
            full(e),
            full(et),
        ],
        out_specs=[
            pl.BlockSpec((tile, H), lambda t: (t, 0)),
            pl.BlockSpec((tile, 2 * H), lambda t: (t, 0)),
        ],
        out_shape=[
            jax.ShapeDtypeStruct((rows, H), bf16),
            jax.ShapeDtypeStruct((rows, 2 * H), bf16),
        ],
    )(cols, w_qkv, w_out, w_msg, e, et)


MESH = pl.DeviceIdType.MESH


def _coords(axes, sizes, t):
    out = {}
    for name, size in reversed(list(zip(axes, sizes))):
        out[name] = t % size
        t = t // size
    return out


def _step(o):
    return ((o + 1) // 2) * (2 * (o % 2) - 1)


def exchange_kernel(plan, *refs):
    total = sum(c for _, _, c in plan)
    ins, outs = refs[:total], refs[total:2 * total]
    sems = refs[2 * total:]
    groups = []
    at, s_at = 0, 0
    for axes, sizes, count in plan:
        n = int(np.prod(sizes))
        me = 0
        for name, size in zip(axes, sizes):
            me = me * size + lax.axis_index(name)
        groups.append(dict(axes=axes, sizes=sizes, n=n, me=me, ins=ins[at:at + count], outs=outs[at:at + count],
                           send=sems[s_at], recv=sems[s_at + 1], local=sems[s_at + 2]))
        at += count
        s_at += 3

    barrier = pltpu.get_barrier_semaphore()
    expected = 0
    for g in groups:
        n, me = g["n"], g["me"]
        def greet(o, carry, g=g, n=n, me=me):
            t = lax.rem(me + o, n)
            pl.semaphore_signal(barrier, inc=1, device_id=_coords(g["axes"], g["sizes"], t), device_id_type=MESH)
            return carry
        lax.fori_loop(1, n, greet, 0)
        expected += n - 1
    pl.semaphore_wait(barrier, expected)

    def remote(g, a, src, dst, t):
        if g["ins"][a].shape[0] == 1:
            src = 0
        return pltpu.make_async_remote_copy(
            src_ref=g["ins"][a].at[src], dst_ref=g["outs"][a].at[dst],
            send_sem=g["send"].at[a, src], recv_sem=g["recv"].at[a, dst],
            device_id=_coords(g["axes"], g["sizes"], t), device_id_type=MESH)

    def own(g, a):
        src = 0 if g["ins"][a].shape[0] == 1 else g["me"]
        return pltpu.make_async_copy(g["ins"][a].at[src], g["outs"][a].at[g["me"]], g["local"].at[a])

    for g in groups:
        for a in range(len(g["ins"])):
            own(g, a).start()
    for g in groups:
        n, me = g["n"], g["me"]
        def start(o, carry, g=g, n=n, me=me):
            t = lax.rem(me + _step(o) + n, n)
            for a in range(len(g["ins"])):
                remote(g, a, t, me, t).start()
            return carry
        lax.fori_loop(1, n, start, 0)
    for g in groups:
        n, me = g["n"], g["me"]
        def finish(o, carry, g=g, n=n, me=me):
            t = lax.rem(me + _step(o) + n, n)
            s = lax.rem(me - _step(o) + n, n)
            for a in range(len(g["ins"])):
                remote(g, a, t, me, t).wait_send()
                remote(g, a, me, s, s).wait_recv()
            return carry
        lax.fori_loop(1, n, finish, 0)
        for a in range(len(g["ins"])):
            own(g, a).wait()


def exchange(groups, collective_id):
    plan, arrays, scratch, n_of = [], [], [], []
    for axes, arrs in groups:
        axes = tuple(axes)
        sizes = tuple(lax.axis_size(a) for a in axes)
        n = int(np.prod(sizes))
        plan.append((axes, sizes, len(arrs)))
        arrays.extend(arrs)
        n_of.extend([n] * len(arrs))
        scratch += [pltpu.SemaphoreType.DMA((len(arrs), n)), pltpu.SemaphoreType.DMA((len(arrs), n)),
                    pltpu.SemaphoreType.DMA((len(arrs),))]
    vmem = pl.BlockSpec(memory_space=pltpu.VMEM)
    return pl.pallas_call(
        functools.partial(exchange_kernel, tuple(plan)),
        out_shape=[jax.ShapeDtypeStruct((n_of[i],) + a.shape[1:], a.dtype) for i, a in enumerate(arrays)],
        in_specs=[vmem] * len(arrays),
        out_specs=[vmem] * len(arrays),
        scratch_shapes=scratch,
        compiler_params=pltpu.CompilerParams(has_side_effects=True, collective_id=collective_id),
    )(*arrays)


def tail_kernel(h_ref, cust_ref, order_ref, sorted_ref, unperm_ref, wback_ref, out_ref):
    ret_cust = jnp.dot(order_ref[...], cust_ref[...], preferred_element_type=f32).astype(bf16)
    ret_prod = jnp.dot(unperm_ref[...], sorted_ref[...], preferred_element_type=f32).astype(bf16)
    back = jnp.dot(ret_cust, wback_ref[:H, :], preferred_element_type=f32) + jnp.dot(
        ret_prod, wback_ref[H:, :], preferred_element_type=f32
    )
    out_ref[...] = rms_norm(h_ref[...].astype(f32) + back).astype(bf16)


def tail(review_h, cust_rows, order, sorted_rows, unperm, w_back):
    vmem = pl.BlockSpec(memory_space=pltpu.VMEM)
    return pl.pallas_call(
        tail_kernel,
        out_shape=jax.ShapeDtypeStruct(review_h.shape, bf16),
        in_specs=[vmem] * 6,
        out_specs=vmem,
    )(review_h, cust_rows, order, sorted_rows, unperm, w_back)


def refresh(totals, counts, states, weight):
    normed_sum = (totals / jnp.sqrt(jnp.maximum(counts, 1.0))[:, None]).astype(bf16)
    update = jax.nn.silu(jnp.dot(normed_sum, weight, preferred_element_type=f32))
    return rms_norm(states.astype(f32) + update).astype(bf16)


def pick_back(picker, states):
    return lax.dot_general(
        picker, states, (((0,), (0,)), ((), ())), preferred_element_type=f32
    ).astype(bf16)


def one_hot_rows(ids, rows):
    return (ids.reshape(1, -1) == jnp.arange(rows, dtype=jnp.int32)[:, None]).astype(bf16)


def on_device(
    review_cols,
    cust_state,
    prod_state,
    w_qkv,
    w_out,
    w_msg,
    w_cust_up,
    w_prod_up,
    w_back,
    cust_slot,
    prod_slot,
    prod_pos,
    live_count,
):
    review_rows = review_cols.shape[0]
    rev_size = lax.axis_size("rev")
    cust_size = lax.axis_size("cust")
    prod_size = lax.axis_size("prod")
    cust_owners = rev_size * cust_size
    cust_slots = review_rows // cust_owners
    prod_owners = cust_size * prod_size
    prod_slots = review_rows // prod_owners
    cust_rows = cust_state.shape[0]
    prod_rows = prod_state.shape[0]
    own_rows = prod_rows // rev_size

    review_h, message = encode(review_cols, w_qkv, w_out, w_msg)
    to_cust = message[:, :H]
    to_prod = message[:, H:]
    filled = jnp.arange(cust_slots, dtype=jnp.int32)[None, :] < live_count.reshape(cust_owners, 1)
    live = filled.reshape(review_rows)
    cust_ids = jnp.where(filled, cust_slot.reshape(cust_owners, cust_slots), -1)
    position = prod_pos.reshape(review_rows)
    perm = one_hot_rows(position, review_rows)
    id_plus = jnp.where(live, prod_slot + 1, 0)
    id_lane = jnp.arange(LANES, dtype=jnp.int32)[None, :]
    id_cols = jnp.where(
        id_lane == 0, (id_plus // 32)[:, None], jnp.where(id_lane == 1, (id_plus % 32)[:, None], 0)
    ).astype(bf16)
    sorted_all = jnp.dot(perm, jnp.concatenate([to_prod, id_cols], axis=1), preferred_element_type=f32)
    prod_msgs = sorted_all[:, :H].astype(bf16)
    prod_ids = (sorted_all[:, H] * 32.0 + sorted_all[:, H + 1]).astype(jnp.int32) - 1

    cust_run = cust_size * cust_slots
    stage_rows = rev_size * cust_slots
    sent1, ids1, prod_got, prod_got_ids = exchange(
        [
            (("rev",), [to_cust.reshape(rev_size, cust_run, H), cust_ids.reshape(rev_size, 1, cust_run)]),
            (("cust", "prod"), [prod_msgs.reshape(prod_owners, prod_slots, H),
                                prod_ids.reshape(prod_owners, 1, prod_slots)]),
        ],
        0,
    )
    prod_pick = one_hot_rows(prod_got_ids, prod_rows)
    prod_part = jnp.dot(prod_pick, prod_got.reshape(review_rows, H), preferred_element_type=f32)
    prod_cnt = jnp.sum(prod_pick, axis=1, dtype=f32)
    cnt_hi = jnp.floor(prod_cnt * (1.0 / 64.0))
    cnt_lo = prod_cnt - 64.0 * cnt_hi
    lane = jnp.arange(LANES, dtype=jnp.int32)[None, :]
    cnt_block = jnp.where(lane == 0, cnt_hi[:, None], jnp.where(lane == 1, cnt_lo[:, None], 0.0))
    prod_pack = jnp.concatenate([prod_part, cnt_block], axis=1).astype(bf16)
    stage2 = sent1.reshape(rev_size, cust_size, cust_slots, H).transpose(1, 0, 2, 3)
    ids2 = ids1.reshape(rev_size, cust_size, cust_slots).transpose(1, 0, 2)
    got_rows, got_ids, spread = exchange(
        [
            (("cust",), [stage2.reshape(cust_size, stage_rows, H), ids2.reshape(cust_size, 1, stage_rows)]),
            (("rev",), [prod_pack.reshape(rev_size, own_rows, H + LANES)]),
        ],
        1,
    )
    cust_pick = one_hot_rows(got_ids, cust_rows)
    cust_part = jnp.dot(cust_pick, got_rows.reshape(review_rows, H), preferred_element_type=f32)
    cust_cnt = jnp.sum(cust_pick, axis=1, dtype=f32)
    cust_pack = jnp.concatenate(
        [cust_part, jnp.broadcast_to(cust_cnt[:, None], (cust_rows, LANES))], axis=1
    )
    whole = jnp.sum(spread.astype(f32), axis=0)
    whole_cnt = whole[:, H] * 64.0 + whole[:, H + 1]
    me = lax.axis_index("rev")
    own_state = lax.dynamic_slice_in_dim(prod_state, me * own_rows, own_rows, axis=0)
    own_new = refresh(whole[:, :H], whole_cnt, own_state, w_prod_up)

    cust_both, new_prod = exchange(
        [
            (("prod",), [cust_pack[None]]),
            (("rev",), [own_new[None]]),
        ],
        2,
    )
    cust_tot = cust_both[0] + cust_both[1]
    new_cust = refresh(cust_tot[:, :H], cust_tot[:, H], cust_state, w_cust_up)
    new_prod = new_prod.reshape(prod_rows, H)

    reply = pick_back(cust_pick, new_cust).reshape(cust_size, rev_size, cust_slots, H).transpose(1, 0, 2, 3)
    back1, ret_sorted = exchange(
        [
            (("rev",), [reply.reshape(rev_size, cust_run, H)]),
            (("cust", "prod"), [pick_back(prod_pick, new_prod).reshape(prod_owners, prod_slots, H)]),
        ],
        3,
    )
    back2 = back1.reshape(rev_size, cust_size, cust_slots, H).transpose(1, 0, 2, 3)
    (ret_cust,) = exchange([(("cust",), [back2.reshape(cust_size, stage_rows, H)])], 4)
    slot = jnp.arange(review_rows, dtype=jnp.int32)
    came_from = (
        ((slot // cust_slots) % cust_size) * stage_rows
        + (slot // cust_run) * cust_slots
        + slot % cust_slots
    )
    order = one_hot_rows(came_from, review_rows).T
    unperm = one_hot_rows(position, review_rows).T
    review_out = tail(
        review_h, ret_cust.reshape(review_rows, H), order, ret_sorted.reshape(review_rows, H), unperm, w_back
    )
    return (review_out, new_cust, new_prod)


def solution(mesh):
    in_specs = (
        P(("rev", "cust", "prod"), None),
        P(("rev", "cust"), None),
        P(("cust", "prod"), None),
        P(),
        P(),
        P(),
        P(),
        P(),
        P(),
        P(("rev", "cust", "prod")),
        P(("rev", "cust", "prod")),
        P(("rev", "cust", "prod"), None),
        P(("rev", "cust", "prod"), None),
    )
    out_specs = (
        P(("rev", "cust", "prod"), None),
        P(("rev", "cust"), None),
        P(("cust", "prod"), None),
    )
    return jax.shard_map(
        on_device, mesh=mesh, in_specs=in_specs, out_specs=out_specs, check_vma=False
    )
```

```python
import math

import jax
import jax.numpy as jnp
from jax import lax
import functools

import numpy as np
from jax.experimental import pallas as pl
from jax.experimental.pallas import tpu as pltpu
from jax.sharding import PartitionSpec as P

H = 512
HEADS = 8
NCOL = 4
HD = 64
LANES = 128
f32 = jnp.float32
bf16 = jnp.bfloat16


def rms_norm(vector):
    return vector * lax.rsqrt(jnp.mean(vector * vector, axis=-1, keepdims=True) + 1e-06)


def head_mats():
    lane = jnp.arange(H, dtype=jnp.int32)[:, None] // HD
    col = jnp.arange(LANES, dtype=jnp.int32)[None, :]
    e = (lane == col).astype(bf16)
    return e, e.T


def encode_kernel(x_ref, wqkv_ref, wout_ref, wmsg_ref, e_ref, et_ref, perm_ref, idc_ref, h_ref, cust_ref, prod_ref, ids_ref):
    e = e_ref[...]
    et = et_ref[...]
    xs = [x_ref[:, i * H:(i + 1) * H] for i in range(NCOL)]
    q, k, v = [], [], []
    for i in range(NCOL):
        qkv = jnp.dot(xs[i], wqkv_ref[...], preferred_element_type=f32).astype(bf16)
        q.append(qkv[:, :H].astype(f32))
        k.append(qkv[:, H:2 * H].astype(f32))
        v.append(qkv[:, 2 * H:].astype(f32))
    pooled = None
    for i in range(NCOL):
        scores = []
        for j in range(NCOL):
            prod = q[i] * k[j]
            hi = prod.astype(bf16)
            lo = (prod - hi.astype(f32)).astype(bf16)
            s = jnp.dot(hi, e, preferred_element_type=f32) + jnp.dot(lo, e, preferred_element_type=f32)
            scores.append(s * (1.0 / math.sqrt(HD)))
        top = jnp.maximum(jnp.maximum(scores[0], scores[1]), jnp.maximum(scores[2], scores[3]))
        expon = [jnp.exp(s - top) for s in scores]
        total = (expon[0] + expon[1]) + (expon[2] + expon[3])
        att = None
        for j in range(NCOL):
            a = (expon[j] / total).astype(bf16)
            term = jnp.dot(a, et, preferred_element_type=f32) * v[j]
            att = term if att is None else att + term
        mixed = xs[i].astype(f32) + jnp.dot(att.astype(bf16), wout_ref[...], preferred_element_type=f32)
        pooled = mixed if pooled is None else pooled + mixed
    pooled = pooled * (1.0 / NCOL)
    h = rms_norm(pooled).astype(bf16)
    h_ref[...] = h
    msg = jnp.dot(h, wmsg_ref[...], preferred_element_type=f32).astype(bf16)
    cust_ref[...] = msg[:, :H]
    prod_ref[...] = jnp.dot(perm_ref[...], msg[:, H:], preferred_element_type=f32).astype(bf16)
    ids_ref[...] = jnp.dot(perm_ref[...], idc_ref[...], preferred_element_type=f32)


def encode(cols, w_qkv, w_out, w_msg, perm, id_cols):
    rows = cols.shape[0]
    e, et = head_mats()
    vmem = pl.BlockSpec(memory_space=pltpu.VMEM)
    return pl.pallas_call(
        encode_kernel,
        in_specs=[vmem] * 8,
        out_specs=[vmem] * 4,
        out_shape=[
            jax.ShapeDtypeStruct((rows, H), bf16),
            jax.ShapeDtypeStruct((rows, H), bf16),
            jax.ShapeDtypeStruct((rows, H), bf16),
            jax.ShapeDtypeStruct((rows, LANES), f32),
        ],
    )(cols, w_qkv, w_out, w_msg, e, et, perm, id_cols)

MESH = pl.DeviceIdType.MESH


def _coords(axes, sizes, t):
    out = {}
    for name, size in reversed(list(zip(axes, sizes))):
        out[name] = t % size
        t = t // size
    return out


def _step(o):
    return ((o + 1) // 2) * (2 * (o % 2) - 1)


def exchange_kernel(plan, *refs):
    total = sum(c for _, _, c in plan)
    ins, outs = refs[:total], refs[total:2 * total]
    sems = refs[2 * total:]
    groups = []
    at, s_at = 0, 0
    for axes, sizes, count in plan:
        n = int(np.prod(sizes))
        me = 0
        for name, size in zip(axes, sizes):
            me = me * size + lax.axis_index(name)
        groups.append(dict(axes=axes, sizes=sizes, n=n, me=me, ins=ins[at:at + count], outs=outs[at:at + count],
                           send=sems[s_at], recv=sems[s_at + 1], local=sems[s_at + 2]))
        at += count
        s_at += 3

    barrier = pltpu.get_barrier_semaphore()
    expected = 0
    for g in groups:
        n, me = g["n"], g["me"]
        def greet(o, carry, g=g, n=n, me=me):
            t = lax.rem(me + o, n)
            pl.semaphore_signal(barrier, inc=1, device_id=_coords(g["axes"], g["sizes"], t), device_id_type=MESH)
            return carry
        lax.fori_loop(1, n, greet, 0)
        expected += n - 1
    pl.semaphore_wait(barrier, expected)

    def remote(g, a, src, dst, t):
        if g["ins"][a].shape[0] == 1:
            src = 0
        return pltpu.make_async_remote_copy(
            src_ref=g["ins"][a].at[src], dst_ref=g["outs"][a].at[dst],
            send_sem=g["send"].at[a, src], recv_sem=g["recv"].at[a, dst],
            device_id=_coords(g["axes"], g["sizes"], t), device_id_type=MESH)

    def own(g, a):
        src = 0 if g["ins"][a].shape[0] == 1 else g["me"]
        return pltpu.make_async_copy(g["ins"][a].at[src], g["outs"][a].at[g["me"]], g["local"].at[a])

    for g in groups:
        for a in range(len(g["ins"])):
            own(g, a).start()
    for g in groups:
        n, me = g["n"], g["me"]
        def start(o, carry, g=g, n=n, me=me):
            t = lax.rem(me + _step(o) + n, n)
            for a in range(len(g["ins"])):
                remote(g, a, t, me, t).start()
            return carry
        lax.fori_loop(1, n, start, 0)
    for g in groups:
        n, me = g["n"], g["me"]
        def finish(o, carry, g=g, n=n, me=me):
            t = lax.rem(me + _step(o) + n, n)
            s = lax.rem(me - _step(o) + n, n)
            for a in range(len(g["ins"])):
                remote(g, a, t, me, t).wait_send()
                remote(g, a, me, s, s).wait_recv()
            return carry
        lax.fori_loop(1, n, finish, 0)
        for a in range(len(g["ins"])):
            own(g, a).wait()


def exchange(groups, collective_id):
    plan, arrays, scratch, n_of = [], [], [], []
    for axes, arrs in groups:
        axes = tuple(axes)
        sizes = tuple(lax.axis_size(a) for a in axes)
        n = int(np.prod(sizes))
        plan.append((axes, sizes, len(arrs)))
        arrays.extend(arrs)
        n_of.extend([n] * len(arrs))
        scratch += [pltpu.SemaphoreType.DMA((len(arrs), n)), pltpu.SemaphoreType.DMA((len(arrs), n)),
                    pltpu.SemaphoreType.DMA((len(arrs),))]
    vmem = pl.BlockSpec(memory_space=pltpu.VMEM)
    return pl.pallas_call(
        functools.partial(exchange_kernel, tuple(plan)),
        out_shape=[jax.ShapeDtypeStruct((n_of[i],) + a.shape[1:], a.dtype) for i, a in enumerate(arrays)],
        in_specs=[vmem] * len(arrays),
        out_specs=[vmem] * len(arrays),
        scratch_shapes=scratch,
        compiler_params=pltpu.CompilerParams(has_side_effects=True, collective_id=collective_id),
    )(*arrays)


def tail_kernel(h_ref, cust_ref, order_ref, sorted_ref, unperm_ref, wback_ref, out_ref):
    ret_cust = jnp.dot(order_ref[...], cust_ref[...], preferred_element_type=f32).astype(bf16)
    ret_prod = jnp.dot(unperm_ref[...], sorted_ref[...], preferred_element_type=f32).astype(bf16)
    back = jnp.dot(ret_cust, wback_ref[:H, :], preferred_element_type=f32) + jnp.dot(
        ret_prod, wback_ref[H:, :], preferred_element_type=f32
    )
    out_ref[...] = rms_norm(h_ref[...].astype(f32) + back).astype(bf16)


def tail(review_h, cust_rows, order, sorted_rows, unperm, w_back):
    vmem = pl.BlockSpec(memory_space=pltpu.VMEM)
    return pl.pallas_call(
        tail_kernel,
        out_shape=jax.ShapeDtypeStruct(review_h.shape, bf16),
        in_specs=[vmem] * 6,
        out_specs=vmem,
    )(review_h, cust_rows, order, sorted_rows, unperm, w_back)


def refresh(totals, counts, states, weight):
    normed_sum = (totals / jnp.sqrt(jnp.maximum(counts, 1.0))[:, None]).astype(bf16)
    update = jax.nn.silu(jnp.dot(normed_sum, weight, preferred_element_type=f32))
    return rms_norm(states.astype(f32) + update).astype(bf16)


def pick_back(picker, states):
    return lax.dot_general(
        picker, states, (((0,), (0,)), ((), ())), preferred_element_type=f32
    ).astype(bf16)


def one_hot_rows(ids, rows):
    return (ids.reshape(1, -1) == jnp.arange(rows, dtype=jnp.int32)[:, None]).astype(bf16)


def on_device(
    review_cols,
    cust_state,
    prod_state,
    w_qkv,
    w_out,
    w_msg,
    w_cust_up,
    w_prod_up,
    w_back,
    cust_slot,
    prod_slot,
    prod_pos,
    live_count,
):
    review_rows = review_cols.shape[0]
    rev_size = lax.axis_size("rev")
    cust_size = lax.axis_size("cust")
    prod_size = lax.axis_size("prod")
    cust_owners = rev_size * cust_size
    cust_slots = review_rows // cust_owners
    prod_owners = cust_size * prod_size
    prod_slots = review_rows // prod_owners
    cust_rows = cust_state.shape[0]
    prod_rows = prod_state.shape[0]
    own_rows = prod_rows // rev_size

    filled = jnp.arange(cust_slots, dtype=jnp.int32)[None, :] < live_count.reshape(cust_owners, 1)
    live = filled.reshape(review_rows)
    cust_ids = jnp.where(filled, cust_slot.reshape(cust_owners, cust_slots), -1)
    position = prod_pos.reshape(review_rows)
    perm = one_hot_rows(position, review_rows)
    id_plus = jnp.where(live, prod_slot + 1, 0)
    id_lane = jnp.arange(LANES, dtype=jnp.int32)[None, :]
    id_cols = jnp.where(
        id_lane == 0, (id_plus // 32)[:, None], jnp.where(id_lane == 1, (id_plus % 32)[:, None], 0)
    ).astype(bf16)
    review_h, to_cust, prod_msgs, sorted_ids = encode(review_cols, w_qkv, w_out, w_msg, perm, id_cols)
    prod_ids = (sorted_ids[:, 0] * 32.0 + sorted_ids[:, 1]).astype(jnp.int32) - 1

    cust_run = cust_size * cust_slots
    stage_rows = rev_size * cust_slots
    sent1, ids1, prod_got, prod_got_ids = exchange(
        [
            (("rev",), [to_cust.reshape(rev_size, cust_run, H), cust_ids.reshape(rev_size, 1, cust_run)]),
            (("cust", "prod"), [prod_msgs.reshape(prod_owners, prod_slots, H),
                                prod_ids.reshape(prod_owners, 1, prod_slots)]),
        ],
        0,
    )
    prod_pick = one_hot_rows(prod_got_ids, prod_rows)
    prod_part = jnp.dot(prod_pick, prod_got.reshape(review_rows, H), preferred_element_type=f32)
    prod_cnt = jnp.sum(prod_pick, axis=1, dtype=f32)
    cnt_hi = jnp.floor(prod_cnt * (1.0 / 64.0))
    cnt_lo = prod_cnt - 64.0 * cnt_hi
    lane = jnp.arange(LANES, dtype=jnp.int32)[None, :]
    cnt_block = jnp.where(lane == 0, cnt_hi[:, None], jnp.where(lane == 1, cnt_lo[:, None], 0.0))
    prod_pack = jnp.concatenate([prod_part, cnt_block], axis=1).astype(bf16)
    stage2 = sent1.reshape(rev_size, cust_size, cust_slots, H).transpose(1, 0, 2, 3)
    ids2 = ids1.reshape(rev_size, cust_size, cust_slots).transpose(1, 0, 2)
    got_rows, got_ids, spread = exchange(
        [
            (("cust",), [stage2.reshape(cust_size, stage_rows, H), ids2.reshape(cust_size, 1, stage_rows)]),
            (("rev",), [prod_pack.reshape(rev_size, own_rows, H + LANES)]),
        ],
        1,
    )
    cust_pick = one_hot_rows(got_ids, cust_rows)
    cust_part = jnp.dot(cust_pick, got_rows.reshape(review_rows, H), preferred_element_type=f32)
    cust_cnt = jnp.sum(cust_pick, axis=1, dtype=f32)
    cust_pack = jnp.concatenate(
        [cust_part, jnp.broadcast_to(cust_cnt[:, None], (cust_rows, LANES))], axis=1
    )
    whole = jnp.sum(spread.astype(f32), axis=0)
    whole_cnt = whole[:, H] * 64.0 + whole[:, H + 1]
    me = lax.axis_index("rev")
    own_state = lax.dynamic_slice_in_dim(prod_state, me * own_rows, own_rows, axis=0)
    own_new = refresh(whole[:, :H], whole_cnt, own_state, w_prod_up)

    cust_both, new_prod = exchange(
        [
            (("prod",), [cust_pack[None]]),
            (("rev",), [own_new[None]]),
        ],
        2,
    )
    cust_tot = cust_both[0] + cust_both[1]
    new_cust = refresh(cust_tot[:, :H], cust_tot[:, H], cust_state, w_cust_up)
    new_prod = new_prod.reshape(prod_rows, H)

    reply = pick_back(cust_pick, new_cust).reshape(cust_size, rev_size, cust_slots, H).transpose(1, 0, 2, 3)
    back1, ret_sorted = exchange(
        [
            (("rev",), [reply.reshape(rev_size, cust_run, H)]),
            (("cust", "prod"), [pick_back(prod_pick, new_prod).reshape(prod_owners, prod_slots, H)]),
        ],
        3,
    )
    back2 = back1.reshape(rev_size, cust_size, cust_slots, H).transpose(1, 0, 2, 3)
    (ret_cust,) = exchange([(("cust",), [back2.reshape(cust_size, stage_rows, H)])], 4)
    slot = jnp.arange(review_rows, dtype=jnp.int32)
    came_from = (
        ((slot // cust_slots) % cust_size) * stage_rows
        + (slot // cust_run) * cust_slots
        + slot % cust_slots
    )
    order = one_hot_rows(came_from, review_rows).T
    unperm = one_hot_rows(position, review_rows).T
    review_out = tail(
        review_h, ret_cust.reshape(review_rows, H), order, ret_sorted.reshape(review_rows, H), unperm, w_back
    )
    return (review_out, new_cust, new_prod)


def solution(mesh):
    in_specs = (
        P(("rev", "cust", "prod"), None),
        P(("rev", "cust"), None),
        P(("cust", "prod"), None),
        P(),
        P(),
        P(),
        P(),
        P(),
        P(),
        P(("rev", "cust", "prod")),
        P(("rev", "cust", "prod")),
        P(("rev", "cust", "prod"), None),
        P(("rev", "cust", "prod"), None),
    )
    out_specs = (
        P(("rev", "cust", "prod"), None),
        P(("rev", "cust"), None),
        P(("cust", "prod"), None),
    )
    return jax.shard_map(
        on_device, mesh=mesh, in_specs=in_specs, out_specs=out_specs, check_vma=False
    )
```

```python
import math

import jax
import jax.numpy as jnp
from jax import lax
import functools

import numpy as np
from jax.experimental import pallas as pl
from jax.experimental.pallas import tpu as pltpu
from jax.sharding import PartitionSpec as P

H = 512
HEADS = 8
NCOL = 4
HD = 64
LANES = 128
f32 = jnp.float32
bf16 = jnp.bfloat16


def rms_norm(vector):
    return vector * lax.rsqrt(jnp.mean(vector * vector, axis=-1, keepdims=True) + 1e-06)


def encode_kernel(x_ref, wqkv_ref, wout_ref, wmsg_ref, pos_ref, idc_ref, h_ref, cust_ref, prod_ref, ids_ref):
    e = (lax.broadcasted_iota(jnp.int32, (H, LANES), 0) // HD == lax.broadcasted_iota(jnp.int32, (H, LANES), 1)).astype(bf16)
    et = (lax.broadcasted_iota(jnp.int32, (LANES, H), 1) // HD == lax.broadcasted_iota(jnp.int32, (LANES, H), 0)).astype(bf16)
    xs = [x_ref[:, i * H:(i + 1) * H] for i in range(NCOL)]
    q, k, v = [], [], []
    for i in range(NCOL):
        qkv = jnp.dot(xs[i], wqkv_ref[...], preferred_element_type=f32).astype(bf16)
        q.append(qkv[:, :H].astype(f32))
        k.append(qkv[:, H:2 * H].astype(f32))
        v.append(qkv[:, 2 * H:].astype(f32))
    pooled = None
    for i in range(NCOL):
        scores = []
        for j in range(NCOL):
            prod = q[i] * k[j]
            hi = prod.astype(bf16)
            lo = (prod - hi.astype(f32)).astype(bf16)
            s = jnp.dot(hi, e, preferred_element_type=f32) + jnp.dot(lo, e, preferred_element_type=f32)
            scores.append(s * (1.0 / math.sqrt(HD)))
        top = jnp.maximum(jnp.maximum(scores[0], scores[1]), jnp.maximum(scores[2], scores[3]))
        expon = [jnp.exp(s - top) for s in scores]
        total = (expon[0] + expon[1]) + (expon[2] + expon[3])
        att = None
        for j in range(NCOL):
            a = (expon[j] / total).astype(bf16)
            term = jnp.dot(a, et, preferred_element_type=f32) * v[j]
            att = term if att is None else att + term
        mixed = xs[i].astype(f32) + jnp.dot(att.astype(bf16), wout_ref[...], preferred_element_type=f32)
        pooled = mixed if pooled is None else pooled + mixed
    pooled = pooled * (1.0 / NCOL)
    h = rms_norm(pooled).astype(bf16)
    h_ref[...] = h
    msg = jnp.dot(h, wmsg_ref[...], preferred_element_type=f32).astype(bf16)
    cust_ref[...] = msg[:, :H]
    rows = pos_ref.shape[1]
    perm = (lax.broadcasted_iota(jnp.int32, (rows, rows), 0) == pos_ref[...]).astype(bf16)
    prod_ref[...] = jnp.dot(perm, msg[:, H:], preferred_element_type=f32).astype(bf16)
    ids_ref[...] = jnp.dot(perm, idc_ref[...], preferred_element_type=f32)


def encode(cols, w_qkv, w_out, w_msg, position, id_cols):
    rows = cols.shape[0]
    vmem = pl.BlockSpec(memory_space=pltpu.VMEM)
    return pl.pallas_call(
        encode_kernel,
        in_specs=[vmem] * 6,
        out_specs=[vmem] * 4,
        out_shape=[
            jax.ShapeDtypeStruct((rows, H), bf16),
            jax.ShapeDtypeStruct((rows, H), bf16),
            jax.ShapeDtypeStruct((rows, H), bf16),
            jax.ShapeDtypeStruct((rows, LANES), f32),
        ],
    )(cols, w_qkv, w_out, w_msg, position.reshape(1, rows), id_cols)

MESH = pl.DeviceIdType.MESH


def _coords(axes, sizes, t):
    out = {}
    for name, size in reversed(list(zip(axes, sizes))):
        out[name] = t % size
        t = t // size
    return out


def _step(o):
    return ((o + 1) // 2) * (2 * (o % 2) - 1)


def exchange_kernel(plan, *refs):
    total = sum(c for _, _, c in plan)
    ins, outs = refs[:total], refs[total:2 * total]
    sems = refs[2 * total:]
    groups = []
    at, s_at = 0, 0
    for axes, sizes, count in plan:
        n = int(np.prod(sizes))
        me = 0
        for name, size in zip(axes, sizes):
            me = me * size + lax.axis_index(name)
        groups.append(dict(axes=axes, sizes=sizes, n=n, me=me, ins=ins[at:at + count], outs=outs[at:at + count],
                           send=sems[s_at], recv=sems[s_at + 1], local=sems[s_at + 2]))
        at += count
        s_at += 3

    barrier = pltpu.get_barrier_semaphore()
    expected = 0
    for g in groups:
        n, me = g["n"], g["me"]
        def greet(o, carry, g=g, n=n, me=me):
            t = lax.rem(me + o, n)
            pl.semaphore_signal(barrier, inc=1, device_id=_coords(g["axes"], g["sizes"], t), device_id_type=MESH)
            return carry
        lax.fori_loop(1, n, greet, 0)
        expected += n - 1
    pl.semaphore_wait(barrier, expected)

    def remote(g, a, src, dst, t):
        if g["ins"][a].shape[0] == 1:
            src = 0
        return pltpu.make_async_remote_copy(
            src_ref=g["ins"][a].at[src], dst_ref=g["outs"][a].at[dst],
            send_sem=g["send"].at[a, src], recv_sem=g["recv"].at[a, dst],
            device_id=_coords(g["axes"], g["sizes"], t), device_id_type=MESH)

    def own(g, a):
        src = 0 if g["ins"][a].shape[0] == 1 else g["me"]
        return pltpu.make_async_copy(g["ins"][a].at[src], g["outs"][a].at[g["me"]], g["local"].at[a])

    for g in groups:
        for a in range(len(g["ins"])):
            own(g, a).start()
    for g in groups:
        n, me = g["n"], g["me"]
        def start(o, carry, g=g, n=n, me=me):
            t = lax.rem(me + _step(o) + n, n)
            for a in range(len(g["ins"])):
                remote(g, a, t, me, t).start()
            return carry
        lax.fori_loop(1, n, start, 0)
    for g in groups:
        n, me = g["n"], g["me"]
        def finish(o, carry, g=g, n=n, me=me):
            t = lax.rem(me + _step(o) + n, n)
            s = lax.rem(me - _step(o) + n, n)
            for a in range(len(g["ins"])):
                remote(g, a, t, me, t).wait_send()
                remote(g, a, me, s, s).wait_recv()
            return carry
        lax.fori_loop(1, n, finish, 0)
        for a in range(len(g["ins"])):
            own(g, a).wait()


def exchange(groups, collective_id):
    plan, arrays, scratch, n_of = [], [], [], []
    for axes, arrs in groups:
        axes = tuple(axes)
        sizes = tuple(lax.axis_size(a) for a in axes)
        n = int(np.prod(sizes))
        plan.append((axes, sizes, len(arrs)))
        arrays.extend(arrs)
        n_of.extend([n] * len(arrs))
        scratch += [pltpu.SemaphoreType.DMA((len(arrs), n)), pltpu.SemaphoreType.DMA((len(arrs), n)),
                    pltpu.SemaphoreType.DMA((len(arrs),))]
    vmem = pl.BlockSpec(memory_space=pltpu.VMEM)
    return pl.pallas_call(
        functools.partial(exchange_kernel, tuple(plan)),
        out_shape=[jax.ShapeDtypeStruct((n_of[i],) + a.shape[1:], a.dtype) for i, a in enumerate(arrays)],
        in_specs=[vmem] * len(arrays),
        out_specs=[vmem] * len(arrays),
        scratch_shapes=scratch,
        compiler_params=pltpu.CompilerParams(has_side_effects=True, collective_id=collective_id),
    )(*arrays)


def tail_kernel(h_ref, cust_ref, order_ref, sorted_ref, unperm_ref, wback_ref, out_ref):
    ret_cust = jnp.dot(order_ref[...], cust_ref[...], preferred_element_type=f32).astype(bf16)
    ret_prod = jnp.dot(unperm_ref[...], sorted_ref[...], preferred_element_type=f32).astype(bf16)
    back = jnp.dot(ret_cust, wback_ref[:H, :], preferred_element_type=f32) + jnp.dot(
        ret_prod, wback_ref[H:, :], preferred_element_type=f32
    )
    out_ref[...] = rms_norm(h_ref[...].astype(f32) + back).astype(bf16)


def tail(review_h, cust_rows, order, sorted_rows, unperm, w_back):
    vmem = pl.BlockSpec(memory_space=pltpu.VMEM)
    return pl.pallas_call(
        tail_kernel,
        out_shape=jax.ShapeDtypeStruct(review_h.shape, bf16),
        in_specs=[vmem] * 6,
        out_specs=vmem,
    )(review_h, cust_rows, order, sorted_rows, unperm, w_back)


def refresh(totals, counts, states, weight):
    normed_sum = (totals / jnp.sqrt(jnp.maximum(counts, 1.0))[:, None]).astype(bf16)
    update = jax.nn.silu(jnp.dot(normed_sum, weight, preferred_element_type=f32))
    return rms_norm(states.astype(f32) + update).astype(bf16)


def pick_back(picker, states):
    return lax.dot_general(
        picker, states, (((0,), (0,)), ((), ())), preferred_element_type=f32
    ).astype(bf16)


def one_hot_rows(ids, rows):
    return (ids.reshape(1, -1) == jnp.arange(rows, dtype=jnp.int32)[:, None]).astype(bf16)


def on_device(
    review_cols,
    cust_state,
    prod_state,
    w_qkv,
    w_out,
    w_msg,
    w_cust_up,
    w_prod_up,
    w_back,
    cust_slot,
    prod_slot,
    prod_pos,
    live_count,
):
    review_rows = review_cols.shape[0]
    rev_size = lax.axis_size("rev")
    cust_size = lax.axis_size("cust")
    prod_size = lax.axis_size("prod")
    cust_owners = rev_size * cust_size
    cust_slots = review_rows // cust_owners
    prod_owners = cust_size * prod_size
    prod_slots = review_rows // prod_owners
    cust_rows = cust_state.shape[0]
    prod_rows = prod_state.shape[0]
    own_rows = prod_rows // rev_size

    filled = jnp.arange(cust_slots, dtype=jnp.int32)[None, :] < live_count.reshape(cust_owners, 1)
    live = filled.reshape(review_rows)
    cust_ids = jnp.where(filled, cust_slot.reshape(cust_owners, cust_slots), -1)
    position = prod_pos.reshape(review_rows)
    id_plus = jnp.where(live, prod_slot + 1, 0)
    id_lane = jnp.arange(LANES, dtype=jnp.int32)[None, :]
    id_cols = jnp.where(
        id_lane == 0, (id_plus // 32)[:, None], jnp.where(id_lane == 1, (id_plus % 32)[:, None], 0)
    ).astype(bf16)
    review_h, to_cust, prod_msgs, sorted_ids = encode(review_cols, w_qkv, w_out, w_msg, position, id_cols)
    prod_ids = (sorted_ids[:, 0] * 32.0 + sorted_ids[:, 1]).astype(jnp.int32) - 1

    cust_run = cust_size * cust_slots
    stage_rows = rev_size * cust_slots
    sent1, ids1, prod_got, prod_got_ids = exchange(
        [
            (("rev",), [to_cust.reshape(rev_size, cust_run, H), cust_ids.reshape(rev_size, 1, cust_run)]),
            (("cust", "prod"), [prod_msgs.reshape(prod_owners, prod_slots, H),
                                prod_ids.reshape(prod_owners, 1, prod_slots)]),
        ],
        0,
    )
    prod_pick = one_hot_rows(prod_got_ids, prod_rows)
    prod_part = jnp.dot(prod_pick, prod_got.reshape(review_rows, H), preferred_element_type=f32)
    prod_cnt = jnp.sum(prod_pick, axis=1, dtype=f32)
    cnt_hi = jnp.floor(prod_cnt * (1.0 / 64.0))
    cnt_lo = prod_cnt - 64.0 * cnt_hi
    lane = jnp.arange(LANES, dtype=jnp.int32)[None, :]
    cnt_block = jnp.where(lane == 0, cnt_hi[:, None], jnp.where(lane == 1, cnt_lo[:, None], 0.0))
    prod_pack = jnp.concatenate([prod_part, cnt_block], axis=1).astype(bf16)
    stage2 = sent1.reshape(rev_size, cust_size, cust_slots, H).transpose(1, 0, 2, 3)
    ids2 = ids1.reshape(rev_size, cust_size, cust_slots).transpose(1, 0, 2)
    got_rows, got_ids, spread = exchange(
        [
            (("cust",), [stage2.reshape(cust_size, stage_rows, H), ids2.reshape(cust_size, 1, stage_rows)]),
            (("rev",), [prod_pack.reshape(rev_size, own_rows, H + LANES)]),
        ],
        1,
    )
    cust_pick = one_hot_rows(got_ids, cust_rows)
    cust_part = jnp.dot(cust_pick, got_rows.reshape(review_rows, H), preferred_element_type=f32)
    cust_cnt = jnp.sum(cust_pick, axis=1, dtype=f32)
    cust_pack = jnp.concatenate(
        [cust_part, jnp.broadcast_to(cust_cnt[:, None], (cust_rows, LANES))], axis=1
    )
    whole = jnp.sum(spread.astype(f32), axis=0)
    whole_cnt = whole[:, H] * 64.0 + whole[:, H + 1]
    me = lax.axis_index("rev")
    own_state = lax.dynamic_slice_in_dim(prod_state, me * own_rows, own_rows, axis=0)
    own_new = refresh(whole[:, :H], whole_cnt, own_state, w_prod_up)

    cust_both, new_prod = exchange(
        [
            (("prod",), [cust_pack[None]]),
            (("rev",), [own_new[None]]),
        ],
        2,
    )
    cust_tot = cust_both[0] + cust_both[1]
    new_cust = refresh(cust_tot[:, :H], cust_tot[:, H], cust_state, w_cust_up)
    new_prod = new_prod.reshape(prod_rows, H)

    reply = pick_back(cust_pick, new_cust).reshape(cust_size, rev_size, cust_slots, H).transpose(1, 0, 2, 3)
    back1, ret_sorted = exchange(
        [
            (("rev",), [reply.reshape(rev_size, cust_run, H)]),
            (("cust", "prod"), [pick_back(prod_pick, new_prod).reshape(prod_owners, prod_slots, H)]),
        ],
        3,
    )
    back2 = back1.reshape(rev_size, cust_size, cust_slots, H).transpose(1, 0, 2, 3)
    (ret_cust,) = exchange([(("cust",), [back2.reshape(cust_size, stage_rows, H)])], 4)
    slot = jnp.arange(review_rows, dtype=jnp.int32)
    came_from = (
        ((slot // cust_slots) % cust_size) * stage_rows
        + (slot // cust_run) * cust_slots
        + slot % cust_slots
    )
    order = one_hot_rows(came_from, review_rows).T
    unperm = one_hot_rows(position, review_rows).T
    review_out = tail(
        review_h, ret_cust.reshape(review_rows, H), order, ret_sorted.reshape(review_rows, H), unperm, w_back
    )
    return (review_out, new_cust, new_prod)


def solution(mesh):
    in_specs = (
        P(("rev", "cust", "prod"), None),
        P(("rev", "cust"), None),
        P(("cust", "prod"), None),
        P(),
        P(),
        P(),
        P(),
        P(),
        P(),
        P(("rev", "cust", "prod")),
        P(("rev", "cust", "prod")),
        P(("rev", "cust", "prod"), None),
        P(("rev", "cust", "prod"), None),
    )
    out_specs = (
        P(("rev", "cust", "prod"), None),
        P(("rev", "cust"), None),
        P(("cust", "prod"), None),
    )
    return jax.shard_map(
        on_device, mesh=mesh, in_specs=in_specs, out_specs=out_specs, check_vma=False
    )
```

```python
import math

import jax
import jax.numpy as jnp
from jax import lax
import functools

import numpy as np
from jax.experimental import pallas as pl
from jax.experimental.pallas import tpu as pltpu
from jax.sharding import PartitionSpec as P

H = 512
HEADS = 8
NCOL = 4
HD = 64
LANES = 128
f32 = jnp.float32
bf16 = jnp.bfloat16


def rms_norm(vector):
    return vector * lax.rsqrt(jnp.mean(vector * vector, axis=-1, keepdims=True) + 1e-06)


def encode_kernel(x_ref, wqkv_ref, wout_ref, wmsg_ref, pos_ref, idc_ref, h_ref, cust_ref, prod_ref, ids_ref):
    e = (lax.broadcasted_iota(jnp.int32, (H, LANES), 0) // HD == lax.broadcasted_iota(jnp.int32, (H, LANES), 1)).astype(bf16)
    et = (lax.broadcasted_iota(jnp.int32, (LANES, H), 1) // HD == lax.broadcasted_iota(jnp.int32, (LANES, H), 0)).astype(bf16)
    xs = [x_ref[:, i * H:(i + 1) * H] for i in range(NCOL)]
    q, k, v = [], [], []
    for i in range(NCOL):
        qkv = jnp.dot(xs[i], wqkv_ref[...], preferred_element_type=f32).astype(bf16)
        q.append(qkv[:, :H].astype(f32))
        k.append(qkv[:, H:2 * H].astype(f32))
        v.append(qkv[:, 2 * H:].astype(f32))
    pooled = None
    for i in range(NCOL):
        scores = []
        for j in range(NCOL):
            prod = q[i] * k[j]
            hi = prod.astype(bf16)
            lo = (prod - hi.astype(f32)).astype(bf16)
            s = jnp.dot(hi, e, preferred_element_type=f32) + jnp.dot(lo, e, preferred_element_type=f32)
            scores.append(s * (1.0 / math.sqrt(HD)))
        top = jnp.maximum(jnp.maximum(scores[0], scores[1]), jnp.maximum(scores[2], scores[3]))
        expon = [jnp.exp(s - top) for s in scores]
        total = (expon[0] + expon[1]) + (expon[2] + expon[3])
        att = None
        for j in range(NCOL):
            a = (expon[j] / total).astype(bf16)
            term = jnp.dot(a, et, preferred_element_type=f32) * v[j]
            att = term if att is None else att + term
        mixed = xs[i].astype(f32) + jnp.dot(att.astype(bf16), wout_ref[...], preferred_element_type=f32)
        pooled = mixed if pooled is None else pooled + mixed
    pooled = pooled * (1.0 / NCOL)
    h = rms_norm(pooled).astype(bf16)
    h_ref[...] = h
    msg = jnp.dot(h, wmsg_ref[...], preferred_element_type=f32).astype(bf16)
    cust_ref[...] = msg[:, :H]
    rows = pos_ref.shape[1]
    perm = (lax.broadcasted_iota(jnp.int32, (rows, rows), 0) == pos_ref[...]).astype(bf16)
    prod_ref[...] = jnp.dot(perm, msg[:, H:], preferred_element_type=f32).astype(bf16)
    ids_ref[...] = jnp.dot(perm, idc_ref[...], preferred_element_type=f32)


def encode(cols, w_qkv, w_out, w_msg, position, id_cols):
    rows = cols.shape[0]
    vmem = pl.BlockSpec(memory_space=pltpu.VMEM)
    return pl.pallas_call(
        encode_kernel,
        in_specs=[vmem] * 6,
        out_specs=[vmem] * 4,
        out_shape=[
            jax.ShapeDtypeStruct((rows, H), bf16),
            jax.ShapeDtypeStruct((rows, H), bf16),
            jax.ShapeDtypeStruct((rows, H), bf16),
            jax.ShapeDtypeStruct((rows, LANES), f32),
        ],
    )(cols, w_qkv, w_out, w_msg, position.reshape(1, rows), id_cols)

MESH = pl.DeviceIdType.MESH


def _coords(axes, sizes, t):
    out = {}
    for name, size in reversed(list(zip(axes, sizes))):
        out[name] = t % size
        t = t // size
    return out


def _step(o):
    return ((o + 1) // 2) * (2 * (o % 2) - 1)


def exchange_kernel(plan, *refs):
    total = sum(c for _, _, c in plan)
    ins, outs = refs[:total], refs[total:2 * total]
    sems = refs[2 * total:]
    groups = []
    at, s_at = 0, 0
    for axes, sizes, count in plan:
        n = int(np.prod(sizes))
        me = 0
        for name, size in zip(axes, sizes):
            me = me * size + lax.axis_index(name)
        groups.append(dict(axes=axes, sizes=sizes, n=n, me=me, ins=ins[at:at + count], outs=outs[at:at + count],
                           send=sems[s_at], recv=sems[s_at + 1], local=sems[s_at + 2]))
        at += count
        s_at += 3

    barrier = pltpu.get_barrier_semaphore()
    expected = 0
    for g in groups:
        n, me = g["n"], g["me"]
        def greet(o, carry, g=g, n=n, me=me):
            t = lax.rem(me + o, n)
            pl.semaphore_signal(barrier, inc=1, device_id=_coords(g["axes"], g["sizes"], t), device_id_type=MESH)
            return carry
        lax.fori_loop(1, n, greet, 0)
        expected += n - 1
    pl.semaphore_wait(barrier, expected)

    def remote(g, a, src, dst, t):
        if g["ins"][a].shape[0] == 1:
            src = 0
        return pltpu.make_async_remote_copy(
            src_ref=g["ins"][a].at[src], dst_ref=g["outs"][a].at[dst],
            send_sem=g["send"].at[a, src], recv_sem=g["recv"].at[a, dst],
            device_id=_coords(g["axes"], g["sizes"], t), device_id_type=MESH)

    def own(g, a):
        src = 0 if g["ins"][a].shape[0] == 1 else g["me"]
        return pltpu.make_async_copy(g["ins"][a].at[src], g["outs"][a].at[g["me"]], g["local"].at[a])

    for g in groups:
        for a in range(len(g["ins"])):
            own(g, a).start()
    for g in groups:
        n, me = g["n"], g["me"]
        def start(o, carry, g=g, n=n, me=me):
            t = lax.rem(me + _step(o) + n, n)
            for a in range(len(g["ins"])):
                remote(g, a, t, me, t).start()
            return carry
        lax.fori_loop(1, n, start, 0)
    for g in groups:
        n, me = g["n"], g["me"]
        def finish(o, carry, g=g, n=n, me=me):
            t = lax.rem(me + _step(o) + n, n)
            s = lax.rem(me - _step(o) + n, n)
            for a in range(len(g["ins"])):
                remote(g, a, t, me, t).wait_send()
                remote(g, a, me, s, s).wait_recv()
            return carry
        lax.fori_loop(1, n, finish, 0)
        for a in range(len(g["ins"])):
            own(g, a).wait()


def exchange(groups, collective_id):
    plan, arrays, scratch, n_of = [], [], [], []
    for axes, arrs in groups:
        axes = tuple(axes)
        sizes = tuple(lax.axis_size(a) for a in axes)
        n = int(np.prod(sizes))
        plan.append((axes, sizes, len(arrs)))
        arrays.extend(arrs)
        n_of.extend([n] * len(arrs))
        scratch += [pltpu.SemaphoreType.DMA((len(arrs), n)), pltpu.SemaphoreType.DMA((len(arrs), n)),
                    pltpu.SemaphoreType.DMA((len(arrs),))]
    vmem = pl.BlockSpec(memory_space=pltpu.VMEM)
    return pl.pallas_call(
        functools.partial(exchange_kernel, tuple(plan)),
        out_shape=[jax.ShapeDtypeStruct((n_of[i],) + a.shape[1:], a.dtype) for i, a in enumerate(arrays)],
        in_specs=[vmem] * len(arrays),
        out_specs=[vmem] * len(arrays),
        scratch_shapes=scratch,
        compiler_params=pltpu.CompilerParams(has_side_effects=True, collective_id=collective_id),
    )(*arrays)


def tail_kernel(h_ref, cust_ref, order_ref, sorted_ref, unperm_ref, wback_ref, out_ref):
    ret_cust = jnp.dot(order_ref[...], cust_ref[...], preferred_element_type=f32).astype(bf16)
    ret_prod = jnp.dot(unperm_ref[...], sorted_ref[...], preferred_element_type=f32).astype(bf16)
    back = jnp.dot(ret_cust, wback_ref[:H, :], preferred_element_type=f32) + jnp.dot(
        ret_prod, wback_ref[H:, :], preferred_element_type=f32
    )
    out_ref[...] = rms_norm(h_ref[...].astype(f32) + back).astype(bf16)


def tail(review_h, cust_rows, order, sorted_rows, unperm, w_back):
    vmem = pl.BlockSpec(memory_space=pltpu.VMEM)
    return pl.pallas_call(
        tail_kernel,
        out_shape=jax.ShapeDtypeStruct(review_h.shape, bf16),
        in_specs=[vmem] * 6,
        out_specs=vmem,
    )(review_h, cust_rows, order, sorted_rows, unperm, w_back)


def refresh_rows(sums, counts, states, weight):
    normed = (sums / jnp.sqrt(jnp.maximum(counts, 1.0))).astype(bf16)
    update = jax.nn.silu(jnp.dot(normed, weight, preferred_element_type=f32))
    return rms_norm(states.astype(f32) + update).astype(bf16)


def column_of(row_ref):
    return jnp.transpose(jnp.broadcast_to(row_ref[...], (8, row_ref.shape[1])))[:, 0:1]


def gather_kernel(rev_axis, gids_ref, grows_ref, spread_ref, pstate_ref, wpu_ref, pack_ref, pnew_ref):
    rows = pack_ref.shape[0]
    pick = (lax.broadcasted_iota(jnp.int32, (rows, gids_ref.shape[1]), 0) == gids_ref[...]).astype(bf16)
    pack_ref[:, :H] = jnp.dot(pick, grows_ref[...], preferred_element_type=f32)
    cnt = jnp.sum(pick.astype(f32), axis=1, keepdims=True)
    pack_ref[:, H:] = jnp.broadcast_to(cnt, (rows, LANES))
    whole = spread_ref[0].astype(f32)
    for i in range(1, spread_ref.shape[0]):
        whole = whole + spread_ref[i].astype(f32)
    own = pnew_ref.shape[0]
    counts = whole[:, H:H + 1] * 64.0 + whole[:, H + 1:H + 2]
    start = pl.multiple_of(lax.axis_index(rev_axis) * own, own)
    pnew_ref[...] = refresh_rows(whole[:, :H], counts, pstate_ref[pl.ds(start, own), :], wpu_ref[...])


def gather_step(got_ids, got_rows, spread, prod_state, w_prod_up, cust_rows):
    own = prod_state.shape[0] // spread.shape[0]
    vmem = pl.BlockSpec(memory_space=pltpu.VMEM)
    return pl.pallas_call(
        functools.partial(gather_kernel, "rev"),
        in_specs=[vmem] * 5,
        out_specs=[vmem] * 2,
        out_shape=[
            jax.ShapeDtypeStruct((cust_rows, H + LANES), f32),
            jax.ShapeDtypeStruct((own, H), bf16),
        ],
    )(got_ids.reshape(1, -1), got_rows, spread, prod_state, w_prod_up)


def reply_kernel(both_ref, cstate_ref, wcu_ref, gids_ref, order_ref, newprod_ref, pids_ref, newcust_ref, creply_ref, preply_ref):
    tot = both_ref[0] + both_ref[1]
    new_cust = refresh_rows(tot[:, :H], tot[:, H:H + 1], cstate_ref[...], wcu_ref[...])
    newcust_ref[...] = new_cust
    n = gids_ref.shape[1]
    pick_t = (column_of(gids_ref) == lax.broadcasted_iota(jnp.int32, (n, new_cust.shape[0]), 1)).astype(bf16)
    reply = jnp.dot(pick_t, new_cust, preferred_element_type=f32).astype(bf16)
    creply_ref[...] = jnp.dot(order_ref[...], reply, preferred_element_type=f32).astype(bf16)
    m = pids_ref.shape[1]
    ppick_t = (column_of(pids_ref) == lax.broadcasted_iota(jnp.int32, (m, newprod_ref.shape[0]), 1)).astype(bf16)
    preply_ref[...] = jnp.dot(ppick_t, newprod_ref[...], preferred_element_type=f32).astype(bf16)


def reply_step(cust_both, cust_state, w_cust_up, got_ids, order, new_prod, prod_got_ids):
    vmem = pl.BlockSpec(memory_space=pltpu.VMEM)
    n = got_ids.size
    return pl.pallas_call(
        reply_kernel,
        in_specs=[vmem] * 7,
        out_specs=[vmem] * 3,
        out_shape=[
            jax.ShapeDtypeStruct(cust_state.shape, bf16),
            jax.ShapeDtypeStruct((n, H), bf16),
            jax.ShapeDtypeStruct((prod_got_ids.size, H), bf16),
        ],
    )(cust_both, cust_state, w_cust_up, got_ids.reshape(1, -1), order, new_prod, prod_got_ids.reshape(1, -1))


def refresh(totals, counts, states, weight):
    normed_sum = (totals / jnp.sqrt(jnp.maximum(counts, 1.0))[:, None]).astype(bf16)
    update = jax.nn.silu(jnp.dot(normed_sum, weight, preferred_element_type=f32))
    return rms_norm(states.astype(f32) + update).astype(bf16)


def pick_back(picker, states):
    return lax.dot_general(
        picker, states, (((0,), (0,)), ((), ())), preferred_element_type=f32
    ).astype(bf16)


def one_hot_rows(ids, rows):
    return (ids.reshape(1, -1) == jnp.arange(rows, dtype=jnp.int32)[:, None]).astype(bf16)


def on_device(
    review_cols,
    cust_state,
    prod_state,
    w_qkv,
    w_out,
    w_msg,
    w_cust_up,
    w_prod_up,
    w_back,
    cust_slot,
    prod_slot,
    prod_pos,
    live_count,
):
    review_rows = review_cols.shape[0]
    rev_size = lax.axis_size("rev")
    cust_size = lax.axis_size("cust")
    prod_size = lax.axis_size("prod")
    cust_owners = rev_size * cust_size
    cust_slots = review_rows // cust_owners
    prod_owners = cust_size * prod_size
    prod_slots = review_rows // prod_owners
    cust_rows = cust_state.shape[0]
    prod_rows = prod_state.shape[0]
    own_rows = prod_rows // rev_size

    filled = jnp.arange(cust_slots, dtype=jnp.int32)[None, :] < live_count.reshape(cust_owners, 1)
    live = filled.reshape(review_rows)
    cust_ids = jnp.where(filled, cust_slot.reshape(cust_owners, cust_slots), -1)
    position = prod_pos.reshape(review_rows)
    id_plus = jnp.where(live, prod_slot + 1, 0)
    id_lane = jnp.arange(LANES, dtype=jnp.int32)[None, :]
    id_cols = jnp.where(
        id_lane == 0, (id_plus // 32)[:, None], jnp.where(id_lane == 1, (id_plus % 32)[:, None], 0)
    ).astype(bf16)
    review_h, to_cust, prod_msgs, sorted_ids = encode(review_cols, w_qkv, w_out, w_msg, position, id_cols)
    prod_ids = (sorted_ids[:, 0] * 32.0 + sorted_ids[:, 1]).astype(jnp.int32) - 1

    cust_run = cust_size * cust_slots
    stage_rows = rev_size * cust_slots
    sent1, ids1, prod_got, prod_got_ids = exchange(
        [
            (("rev",), [to_cust.reshape(rev_size, cust_run, H), cust_ids.reshape(rev_size, 1, cust_run)]),
            (("cust", "prod"), [prod_msgs.reshape(prod_owners, prod_slots, H),
                                prod_ids.reshape(prod_owners, 1, prod_slots)]),
        ],
        0,
    )
    prod_pick = one_hot_rows(prod_got_ids, prod_rows)
    prod_part = jnp.dot(prod_pick, prod_got.reshape(review_rows, H), preferred_element_type=f32)
    prod_cnt = jnp.sum(prod_pick, axis=1, dtype=f32)
    cnt_hi = jnp.floor(prod_cnt * (1.0 / 64.0))
    cnt_lo = prod_cnt - 64.0 * cnt_hi
    lane = jnp.arange(LANES, dtype=jnp.int32)[None, :]
    cnt_block = jnp.where(lane == 0, cnt_hi[:, None], jnp.where(lane == 1, cnt_lo[:, None], 0.0))
    prod_pack = jnp.concatenate([prod_part, cnt_block], axis=1).astype(bf16)
    stage2 = sent1.reshape(rev_size, cust_size, cust_slots, H).transpose(1, 0, 2, 3)
    ids2 = ids1.reshape(rev_size, cust_size, cust_slots).transpose(1, 0, 2)
    got_rows, got_ids, spread = exchange(
        [
            (("cust",), [stage2.reshape(cust_size, stage_rows, H), ids2.reshape(cust_size, 1, stage_rows)]),
            (("rev",), [prod_pack.reshape(rev_size, own_rows, H + LANES)]),
        ],
        1,
    )
    cust_pack, own_new = gather_step(
        got_ids, got_rows.reshape(review_rows, H), spread, prod_state, w_prod_up, cust_rows
    )

    cust_both, new_prod = exchange(
        [
            (("prod",), [cust_pack[None]]),
            (("rev",), [own_new[None]]),
        ],
        2,
    )
    new_prod = new_prod.reshape(prod_rows, H)
    slot = jnp.arange(review_rows, dtype=jnp.int32)
    came_from = (
        ((slot // cust_slots) % cust_size) * stage_rows
        + (slot // cust_run) * cust_slots
        + slot % cust_slots
    )
    order = one_hot_rows(came_from, review_rows).T
    new_cust, reply, prod_reply = reply_step(
        cust_both, cust_state, w_cust_up, got_ids, order, new_prod, prod_got_ids
    )
    back1, ret_sorted = exchange(
        [
            (("rev",), [reply.reshape(rev_size, cust_run, H)]),
            (("cust", "prod"), [prod_reply.reshape(prod_owners, prod_slots, H)]),
        ],
        3,
    )
    back2 = back1.reshape(rev_size, cust_size, cust_slots, H).transpose(1, 0, 2, 3)
    (ret_cust,) = exchange([(("cust",), [back2.reshape(cust_size, stage_rows, H)])], 4)
    unperm = one_hot_rows(position, review_rows).T
    review_out = tail(
        review_h, ret_cust.reshape(review_rows, H), order, ret_sorted.reshape(review_rows, H), unperm, w_back
    )
    return (review_out, new_cust, new_prod)


def solution(mesh):
    in_specs = (
        P(("rev", "cust", "prod"), None),
        P(("rev", "cust"), None),
        P(("cust", "prod"), None),
        P(),
        P(),
        P(),
        P(),
        P(),
        P(),
        P(("rev", "cust", "prod")),
        P(("rev", "cust", "prod")),
        P(("rev", "cust", "prod"), None),
        P(("rev", "cust", "prod"), None),
    )
    out_specs = (
        P(("rev", "cust", "prod"), None),
        P(("rev", "cust"), None),
        P(("cust", "prod"), None),
    )
    return jax.shard_map(
        on_device, mesh=mesh, in_specs=in_specs, out_specs=out_specs, check_vma=False
    )
```

```python
import math

import jax
import jax.numpy as jnp
from jax import lax
import functools

import numpy as np
from jax.experimental import pallas as pl
from jax.experimental.pallas import tpu as pltpu
from jax.sharding import PartitionSpec as P

H = 512
HEADS = 8
NCOL = 4
HD = 64
LANES = 128
f32 = jnp.float32
bf16 = jnp.bfloat16


def rms_norm(vector):
    return vector * lax.rsqrt(jnp.mean(vector * vector, axis=-1, keepdims=True) + 1e-06)


def encode_kernel(x_ref, wqkv_ref, wout_ref, wmsg_ref, pos_ref, idc_ref, h_ref, cust_ref, prod_ref, ids_ref):
    e = (lax.broadcasted_iota(jnp.int32, (H, LANES), 0) // HD == lax.broadcasted_iota(jnp.int32, (H, LANES), 1)).astype(bf16)
    et = (lax.broadcasted_iota(jnp.int32, (LANES, H), 1) // HD == lax.broadcasted_iota(jnp.int32, (LANES, H), 0)).astype(bf16)
    xs = [x_ref[:, i * H:(i + 1) * H] for i in range(NCOL)]
    q, k, v = [], [], []
    for i in range(NCOL):
        qkv = jnp.dot(xs[i], wqkv_ref[...], preferred_element_type=f32).astype(bf16)
        q.append(qkv[:, :H].astype(f32))
        k.append(qkv[:, H:2 * H].astype(f32))
        v.append(qkv[:, 2 * H:].astype(f32))
    pooled = None
    for i in range(NCOL):
        scores = []
        for j in range(NCOL):
            prod = q[i] * k[j]
            hi = prod.astype(bf16)
            lo = (prod - hi.astype(f32)).astype(bf16)
            s = jnp.dot(hi, e, preferred_element_type=f32) + jnp.dot(lo, e, preferred_element_type=f32)
            scores.append(s * (1.0 / math.sqrt(HD)))
        top = jnp.maximum(jnp.maximum(scores[0], scores[1]), jnp.maximum(scores[2], scores[3]))
        expon = [jnp.exp(s - top) for s in scores]
        total = (expon[0] + expon[1]) + (expon[2] + expon[3])
        att = None
        for j in range(NCOL):
            a = (expon[j] / total).astype(bf16)
            term = jnp.dot(a, et, preferred_element_type=f32) * v[j]
            att = term if att is None else att + term
        mixed = xs[i].astype(f32) + jnp.dot(att.astype(bf16), wout_ref[...], preferred_element_type=f32)
        pooled = mixed if pooled is None else pooled + mixed
    pooled = pooled * (1.0 / NCOL)
    h = rms_norm(pooled).astype(bf16)
    h_ref[...] = h
    msg = jnp.dot(h, wmsg_ref[...], preferred_element_type=f32).astype(bf16)
    cust_ref[...] = msg[:, :H]
    rows = pos_ref.shape[1]
    perm = (lax.broadcasted_iota(jnp.int32, (rows, rows), 0) == pos_ref[...]).astype(bf16)
    prod_ref[...] = jnp.dot(perm, msg[:, H:], preferred_element_type=f32).astype(bf16)
    ids_ref[...] = jnp.dot(perm, idc_ref[...], preferred_element_type=f32)


def encode(cols, w_qkv, w_out, w_msg, position, id_cols):
    rows = cols.shape[0]
    vmem = pl.BlockSpec(memory_space=pltpu.VMEM)
    return pl.pallas_call(
        encode_kernel,
        in_specs=[vmem] * 6,
        out_specs=[vmem] * 4,
        out_shape=[
            jax.ShapeDtypeStruct((rows, H), bf16),
            jax.ShapeDtypeStruct((rows, H), bf16),
            jax.ShapeDtypeStruct((rows, H), bf16),
            jax.ShapeDtypeStruct((rows, LANES), f32),
        ],
    )(cols, w_qkv, w_out, w_msg, position.reshape(1, rows), id_cols)

MESH = pl.DeviceIdType.MESH


def _coords(axes, sizes, t):
    out = {}
    for name, size in reversed(list(zip(axes, sizes))):
        out[name] = t % size
        t = t // size
    return out


def _step(o):
    return ((o + 1) // 2) * (2 * (o % 2) - 1)


def exchange_kernel(plan, *refs):
    total = sum(c for _, _, c in plan)
    ins, outs = refs[:total], refs[total:2 * total]
    sems = refs[2 * total:]
    groups = []
    at, s_at = 0, 0
    for axes, sizes, count in plan:
        n = int(np.prod(sizes))
        me = 0
        for name, size in zip(axes, sizes):
            me = me * size + lax.axis_index(name)
        groups.append(dict(axes=axes, sizes=sizes, n=n, me=me, ins=ins[at:at + count], outs=outs[at:at + count],
                           send=sems[s_at], recv=sems[s_at + 1], local=sems[s_at + 2]))
        at += count
        s_at += 3

    barrier = pltpu.get_barrier_semaphore()
    expected = 0
    for g in groups:
        n, me = g["n"], g["me"]
        def greet(o, carry, g=g, n=n, me=me):
            t = lax.rem(me + o, n)
            pl.semaphore_signal(barrier, inc=1, device_id=_coords(g["axes"], g["sizes"], t), device_id_type=MESH)
            return carry
        lax.fori_loop(1, n, greet, 0)
        expected += n - 1
    pl.semaphore_wait(barrier, expected)

    def remote(g, a, src, dst, t):
        if g["ins"][a].shape[0] == 1:
            src = 0
        return pltpu.make_async_remote_copy(
            src_ref=g["ins"][a].at[src], dst_ref=g["outs"][a].at[dst],
            send_sem=g["send"].at[a, src], recv_sem=g["recv"].at[a, dst],
            device_id=_coords(g["axes"], g["sizes"], t), device_id_type=MESH)

    def own(g, a):
        src = 0 if g["ins"][a].shape[0] == 1 else g["me"]
        return pltpu.make_async_copy(g["ins"][a].at[src], g["outs"][a].at[g["me"]], g["local"].at[a])

    for g in groups:
        for a in range(len(g["ins"])):
            own(g, a).start()
    for g in groups:
        n, me = g["n"], g["me"]
        def start(o, carry, g=g, n=n, me=me):
            t = lax.rem(me + _step(o) + n, n)
            for a in range(len(g["ins"])):
                remote(g, a, t, me, t).start()
            return carry
        lax.fori_loop(1, n, start, 0)
    for g in groups:
        n, me = g["n"], g["me"]
        def finish(o, carry, g=g, n=n, me=me):
            t = lax.rem(me + _step(o) + n, n)
            s = lax.rem(me - _step(o) + n, n)
            for a in range(len(g["ins"])):
                remote(g, a, t, me, t).wait_send()
                remote(g, a, me, s, s).wait_recv()
            return carry
        lax.fori_loop(1, n, finish, 0)
        for a in range(len(g["ins"])):
            own(g, a).wait()


def exchange(groups, collective_id):
    plan, arrays, scratch, n_of = [], [], [], []
    for axes, arrs in groups:
        axes = tuple(axes)
        sizes = tuple(lax.axis_size(a) for a in axes)
        n = int(np.prod(sizes))
        plan.append((axes, sizes, len(arrs)))
        arrays.extend(arrs)
        n_of.extend([n] * len(arrs))
        scratch += [pltpu.SemaphoreType.DMA((len(arrs), n)), pltpu.SemaphoreType.DMA((len(arrs), n)),
                    pltpu.SemaphoreType.DMA((len(arrs),))]
    vmem = pl.BlockSpec(memory_space=pltpu.VMEM)
    return pl.pallas_call(
        functools.partial(exchange_kernel, tuple(plan)),
        out_shape=[jax.ShapeDtypeStruct((n_of[i],) + a.shape[1:], a.dtype) for i, a in enumerate(arrays)],
        in_specs=[vmem] * len(arrays),
        out_specs=[vmem] * len(arrays),
        scratch_shapes=scratch,
        compiler_params=pltpu.CompilerParams(has_side_effects=True, collective_id=collective_id),
    )(*arrays)


def tail_kernel(shape, h_ref, cust_ref, sorted_ref, pos_ref, wback_ref, out_ref):
    rows = h_ref.shape[0]
    ret_cust = jnp.dot(order_matrix(rows, *shape), cust_ref[...], preferred_element_type=f32).astype(bf16)
    unperm = (column_of(pos_ref) == lax.broadcasted_iota(jnp.int32, (rows, rows), 1)).astype(bf16)
    ret_prod = jnp.dot(unperm, sorted_ref[...], preferred_element_type=f32).astype(bf16)
    back = jnp.dot(ret_cust, wback_ref[:H, :], preferred_element_type=f32) + jnp.dot(
        ret_prod, wback_ref[H:, :], preferred_element_type=f32
    )
    out_ref[...] = rms_norm(h_ref[...].astype(f32) + back).astype(bf16)


def tail(review_h, cust_rows, shape, sorted_rows, position, w_back):
    vmem = pl.BlockSpec(memory_space=pltpu.VMEM)
    return pl.pallas_call(
        functools.partial(tail_kernel, shape),
        out_shape=jax.ShapeDtypeStruct(review_h.shape, bf16),
        in_specs=[vmem] * 5,
        out_specs=vmem,
    )(review_h, cust_rows, sorted_rows, position.reshape(1, -1), w_back)


def order_matrix(rows, cust_slots, cust_size, stage_rows, cust_run):
    s = lax.broadcasted_iota(jnp.int32, (rows, rows), 0)
    src = ((s // cust_slots) % cust_size) * stage_rows + (s // cust_run) * cust_slots + s % cust_slots
    return (src == lax.broadcasted_iota(jnp.int32, (rows, rows), 1)).astype(bf16)


def route_kernel(rev_size, cust_slots, sent_ref, pgot_ref, pids_ref, stage_ref, pack_ref):
    rows = sent_ref.shape[0]
    s = lax.broadcasted_iota(jnp.int32, (rows, rows), 0)
    stage_rows = rev_size * cust_slots
    cust_run = rows // rev_size
    src = (s % stage_rows) // cust_slots * cust_run + (s // stage_rows) * cust_slots + s % cust_slots
    move = (src == lax.broadcasted_iota(jnp.int32, (rows, rows), 1)).astype(bf16)
    stage_ref[...] = jnp.dot(move, sent_ref[...], preferred_element_type=f32).astype(bf16)
    prows = pack_ref.shape[0]
    pick = (lax.broadcasted_iota(jnp.int32, (prows, pids_ref.shape[1]), 0) == pids_ref[...]).astype(bf16)
    pack_ref[:, :H] = jnp.dot(pick, pgot_ref[...], preferred_element_type=f32).astype(bf16)
    cnt = jnp.sum(pick.astype(f32), axis=1, keepdims=True)
    hi = jnp.floor(cnt * (1.0 / 64.0))
    lo = cnt - 64.0 * hi
    lane = lax.broadcasted_iota(jnp.int32, (prows, LANES), 1)
    pack_ref[:, H:] = jnp.where(lane == 0, hi, jnp.where(lane == 1, lo, 0.0)).astype(bf16)


def route_step(sent1, prod_got, prod_got_ids, rev_size, cust_slots, prod_rows):
    rows = sent1.shape[0]
    vmem = pl.BlockSpec(memory_space=pltpu.VMEM)
    return pl.pallas_call(
        functools.partial(route_kernel, rev_size, cust_slots),
        in_specs=[vmem] * 3,
        out_specs=[vmem] * 2,
        out_shape=[
            jax.ShapeDtypeStruct((rows, H), bf16),
            jax.ShapeDtypeStruct((prod_rows, H + LANES), bf16),
        ],
    )(sent1, prod_got, prod_got_ids.reshape(1, -1))


def refresh_rows(sums, counts, states, weight):
    normed = (sums / jnp.sqrt(jnp.maximum(counts, 1.0))).astype(bf16)
    update = jax.nn.silu(jnp.dot(normed, weight, preferred_element_type=f32))
    return rms_norm(states.astype(f32) + update).astype(bf16)


def column_of(row_ref):
    return jnp.transpose(jnp.broadcast_to(row_ref[...], (8, row_ref.shape[1])))[:, 0:1]


def gather_kernel(rev_axis, gids_ref, grows_ref, spread_ref, pstate_ref, wpu_ref, pack_ref, pnew_ref):
    rows = pack_ref.shape[0]
    pick = (lax.broadcasted_iota(jnp.int32, (rows, gids_ref.shape[1]), 0) == gids_ref[...]).astype(bf16)
    pack_ref[:, :H] = jnp.dot(pick, grows_ref[...], preferred_element_type=f32)
    cnt = jnp.sum(pick.astype(f32), axis=1, keepdims=True)
    pack_ref[:, H:] = jnp.broadcast_to(cnt, (rows, LANES))
    whole = spread_ref[0].astype(f32)
    for i in range(1, spread_ref.shape[0]):
        whole = whole + spread_ref[i].astype(f32)
    own = pnew_ref.shape[0]
    counts = whole[:, H:H + 1] * 64.0 + whole[:, H + 1:H + 2]
    start = pl.multiple_of(lax.axis_index(rev_axis) * own, own)
    pnew_ref[...] = refresh_rows(whole[:, :H], counts, pstate_ref[pl.ds(start, own), :], wpu_ref[...])


def gather_step(got_ids, got_rows, spread, prod_state, w_prod_up, cust_rows):
    own = prod_state.shape[0] // spread.shape[0]
    vmem = pl.BlockSpec(memory_space=pltpu.VMEM)
    return pl.pallas_call(
        functools.partial(gather_kernel, "rev"),
        in_specs=[vmem] * 5,
        out_specs=[vmem] * 2,
        out_shape=[
            jax.ShapeDtypeStruct((cust_rows, H + LANES), f32),
            jax.ShapeDtypeStruct((own, H), bf16),
        ],
    )(got_ids.reshape(1, -1), got_rows, spread, prod_state, w_prod_up)


def reply_kernel(shape, both_ref, cstate_ref, wcu_ref, gids_ref, newprod_ref, pids_ref, newcust_ref, creply_ref, preply_ref):
    tot = both_ref[0] + both_ref[1]
    new_cust = refresh_rows(tot[:, :H], tot[:, H:H + 1], cstate_ref[...], wcu_ref[...])
    newcust_ref[...] = new_cust
    n = gids_ref.shape[1]
    pick_t = (column_of(gids_ref) == lax.broadcasted_iota(jnp.int32, (n, new_cust.shape[0]), 1)).astype(bf16)
    reply = jnp.dot(pick_t, new_cust, preferred_element_type=f32).astype(bf16)
    creply_ref[...] = jnp.dot(order_matrix(n, *shape), reply, preferred_element_type=f32).astype(bf16)
    m = pids_ref.shape[1]
    ppick_t = (column_of(pids_ref) == lax.broadcasted_iota(jnp.int32, (m, newprod_ref.shape[0]), 1)).astype(bf16)
    preply_ref[...] = jnp.dot(ppick_t, newprod_ref[...], preferred_element_type=f32).astype(bf16)


def reply_step(cust_both, cust_state, w_cust_up, got_ids, shape, new_prod, prod_got_ids):
    vmem = pl.BlockSpec(memory_space=pltpu.VMEM)
    n = got_ids.size
    return pl.pallas_call(
        functools.partial(reply_kernel, shape),
        in_specs=[vmem] * 6,
        out_specs=[vmem] * 3,
        out_shape=[
            jax.ShapeDtypeStruct(cust_state.shape, bf16),
            jax.ShapeDtypeStruct((n, H), bf16),
            jax.ShapeDtypeStruct((prod_got_ids.size, H), bf16),
        ],
    )(cust_both, cust_state, w_cust_up, got_ids.reshape(1, -1), new_prod, prod_got_ids.reshape(1, -1))


def refresh(totals, counts, states, weight):
    normed_sum = (totals / jnp.sqrt(jnp.maximum(counts, 1.0))[:, None]).astype(bf16)
    update = jax.nn.silu(jnp.dot(normed_sum, weight, preferred_element_type=f32))
    return rms_norm(states.astype(f32) + update).astype(bf16)


def pick_back(picker, states):
    return lax.dot_general(
        picker, states, (((0,), (0,)), ((), ())), preferred_element_type=f32
    ).astype(bf16)


def one_hot_rows(ids, rows):
    return (ids.reshape(1, -1) == jnp.arange(rows, dtype=jnp.int32)[:, None]).astype(bf16)


def on_device(
    review_cols,
    cust_state,
    prod_state,
    w_qkv,
    w_out,
    w_msg,
    w_cust_up,
    w_prod_up,
    w_back,
    cust_slot,
    prod_slot,
    prod_pos,
    live_count,
):
    review_rows = review_cols.shape[0]
    rev_size = lax.axis_size("rev")
    cust_size = lax.axis_size("cust")
    prod_size = lax.axis_size("prod")
    cust_owners = rev_size * cust_size
    cust_slots = review_rows // cust_owners
    prod_owners = cust_size * prod_size
    prod_slots = review_rows // prod_owners
    cust_rows = cust_state.shape[0]
    prod_rows = prod_state.shape[0]
    own_rows = prod_rows // rev_size

    filled = jnp.arange(cust_slots, dtype=jnp.int32)[None, :] < live_count.reshape(cust_owners, 1)
    live = filled.reshape(review_rows)
    cust_ids = jnp.where(filled, cust_slot.reshape(cust_owners, cust_slots), -1)
    position = prod_pos.reshape(review_rows)
    id_plus = jnp.where(live, prod_slot + 1, 0)
    id_lane = jnp.arange(LANES, dtype=jnp.int32)[None, :]
    id_cols = jnp.where(
        id_lane == 0, (id_plus // 32)[:, None], jnp.where(id_lane == 1, (id_plus % 32)[:, None], 0)
    ).astype(bf16)
    review_h, to_cust, prod_msgs, sorted_ids = encode(review_cols, w_qkv, w_out, w_msg, position, id_cols)
    prod_ids = (sorted_ids[:, 0] * 32.0 + sorted_ids[:, 1]).astype(jnp.int32) - 1

    cust_run = cust_size * cust_slots
    stage_rows = rev_size * cust_slots
    sent1, ids1, prod_got, prod_got_ids = exchange(
        [
            (("rev",), [to_cust.reshape(rev_size, cust_run, H), cust_ids.reshape(rev_size, 1, cust_run)]),
            (("cust", "prod"), [prod_msgs.reshape(prod_owners, prod_slots, H),
                                prod_ids.reshape(prod_owners, 1, prod_slots)]),
        ],
        0,
    )
    stage2, prod_pack = route_step(
        sent1.reshape(review_rows, H), prod_got.reshape(review_rows, H), prod_got_ids, rev_size, cust_slots, prod_rows
    )
    ids2 = ids1.reshape(rev_size, cust_size, cust_slots).transpose(1, 0, 2)
    got_rows, got_ids, spread = exchange(
        [
            (("cust",), [stage2.reshape(cust_size, stage_rows, H), ids2.reshape(cust_size, 1, stage_rows)]),
            (("rev",), [prod_pack.reshape(rev_size, own_rows, H + LANES)]),
        ],
        1,
    )
    cust_pack, own_new = gather_step(
        got_ids, got_rows.reshape(review_rows, H), spread, prod_state, w_prod_up, cust_rows
    )

    cust_both, new_prod = exchange(
        [
            (("prod",), [cust_pack[None]]),
            (("rev",), [own_new[None]]),
        ],
        2,
    )
    new_prod = new_prod.reshape(prod_rows, H)
    shape = (cust_slots, cust_size, stage_rows, cust_run)
    new_cust, reply, prod_reply = reply_step(
        cust_both, cust_state, w_cust_up, got_ids, shape, new_prod, prod_got_ids
    )
    back1, ret_sorted = exchange(
        [
            (("rev",), [reply.reshape(rev_size, cust_run, H)]),
            (("cust", "prod"), [prod_reply.reshape(prod_owners, prod_slots, H)]),
        ],
        3,
    )
    back2 = back1.reshape(rev_size, cust_size, cust_slots, H).transpose(1, 0, 2, 3)
    (ret_cust,) = exchange([(("cust",), [back2.reshape(cust_size, stage_rows, H)])], 4)
    review_out = tail(
        review_h, ret_cust.reshape(review_rows, H), shape, ret_sorted.reshape(review_rows, H), position, w_back
    )
    return (review_out, new_cust, new_prod)


def solution(mesh):
    in_specs = (
        P(("rev", "cust", "prod"), None),
        P(("rev", "cust"), None),
        P(("cust", "prod"), None),
        P(),
        P(),
        P(),
        P(),
        P(),
        P(),
        P(("rev", "cust", "prod")),
        P(("rev", "cust", "prod")),
        P(("rev", "cust", "prod"), None),
        P(("rev", "cust", "prod"), None),
    )
    out_specs = (
        P(("rev", "cust", "prod"), None),
        P(("rev", "cust"), None),
        P(("cust", "prod"), None),
    )
    return jax.shard_map(
        on_device, mesh=mesh, in_specs=in_specs, out_specs=out_specs, check_vma=False
    )
```

```python
import math

import jax
import jax.numpy as jnp
from jax import lax
import functools

import numpy as np
from jax.experimental import pallas as pl
from jax.experimental.pallas import tpu as pltpu
from jax.sharding import PartitionSpec as P

H = 512
HEADS = 8
NCOL = 4
HD = 64
LANES = 128
f32 = jnp.float32
bf16 = jnp.bfloat16


def rms_norm(vector):
    return vector * lax.rsqrt(jnp.mean(vector * vector, axis=-1, keepdims=True) + 1e-06)


def encode_kernel(x_ref, wqkv_ref, wout_ref, wmsg_ref, pos_ref, idc_ref, h_ref, cust_ref, prod_ref, ids_ref):
    e = (lax.broadcasted_iota(jnp.int32, (H, LANES), 0) // HD == lax.broadcasted_iota(jnp.int32, (H, LANES), 1)).astype(bf16)
    et = (lax.broadcasted_iota(jnp.int32, (LANES, H), 1) // HD == lax.broadcasted_iota(jnp.int32, (LANES, H), 0)).astype(bf16)
    xs = [x_ref[:, i * H:(i + 1) * H] for i in range(NCOL)]
    q, k, v = [], [], []
    for i in range(NCOL):
        qkv = jnp.dot(xs[i], wqkv_ref[...], preferred_element_type=f32).astype(bf16)
        q.append(qkv[:, :H].astype(f32))
        k.append(qkv[:, H:2 * H].astype(f32))
        v.append(qkv[:, 2 * H:].astype(f32))
    pooled = None
    for i in range(NCOL):
        scores = []
        for j in range(NCOL):
            s = jnp.dot((q[i] * k[j]).astype(bf16), e, preferred_element_type=f32)
            scores.append(s * (1.0 / math.sqrt(HD)))
        top = jnp.maximum(jnp.maximum(scores[0], scores[1]), jnp.maximum(scores[2], scores[3]))
        expon = [jnp.exp(s - top) for s in scores]
        total = (expon[0] + expon[1]) + (expon[2] + expon[3])
        att = None
        for j in range(NCOL):
            a = (expon[j] / total).astype(bf16)
            term = jnp.dot(a, et, preferred_element_type=f32) * v[j]
            att = term if att is None else att + term
        mixed = xs[i].astype(f32) + jnp.dot(att.astype(bf16), wout_ref[...], preferred_element_type=f32)
        pooled = mixed if pooled is None else pooled + mixed
    pooled = pooled * (1.0 / NCOL)
    h = rms_norm(pooled).astype(bf16)
    h_ref[...] = h
    msg = jnp.dot(h, wmsg_ref[...], preferred_element_type=f32).astype(bf16)
    cust_ref[...] = msg[:, :H]
    rows = pos_ref.shape[1]
    perm = (lax.broadcasted_iota(jnp.int32, (rows, rows), 0) == pos_ref[...]).astype(bf16)
    prod_ref[...] = jnp.dot(perm, msg[:, H:], preferred_element_type=f32).astype(bf16)
    ids_ref[...] = jnp.dot(perm, idc_ref[...], preferred_element_type=f32)


def encode(cols, w_qkv, w_out, w_msg, position, id_cols):
    rows = cols.shape[0]
    vmem = pl.BlockSpec(memory_space=pltpu.VMEM)
    return pl.pallas_call(
        encode_kernel,
        in_specs=[vmem] * 6,
        out_specs=[vmem] * 4,
        out_shape=[
            jax.ShapeDtypeStruct((rows, H), bf16),
            jax.ShapeDtypeStruct((rows, H), bf16),
            jax.ShapeDtypeStruct((rows, H), bf16),
            jax.ShapeDtypeStruct((rows, LANES), f32),
        ],
    )(cols, w_qkv, w_out, w_msg, position.reshape(1, rows), id_cols)

MESH = pl.DeviceIdType.MESH


def _coords(axes, sizes, t):
    out = {}
    for name, size in reversed(list(zip(axes, sizes))):
        out[name] = t % size
        t = t // size
    return out


def _step(o):
    return ((o + 1) // 2) * (2 * (o % 2) - 1)


def exchange_kernel(plan, *refs):
    total = sum(c for _, _, c in plan)
    ins, outs = refs[:total], refs[total:2 * total]
    sems = refs[2 * total:]
    groups = []
    at, s_at = 0, 0
    for axes, sizes, count in plan:
        n = int(np.prod(sizes))
        me = 0
        for name, size in zip(axes, sizes):
            me = me * size + lax.axis_index(name)
        groups.append(dict(axes=axes, sizes=sizes, n=n, me=me, ins=ins[at:at + count], outs=outs[at:at + count],
                           send=sems[s_at], recv=sems[s_at + 1], local=sems[s_at + 2]))
        at += count
        s_at += 3

    barrier = pltpu.get_barrier_semaphore()
    expected = 0
    for g in groups:
        n, me = g["n"], g["me"]
        def greet(o, carry, g=g, n=n, me=me):
            t = lax.rem(me + o, n)
            pl.semaphore_signal(barrier, inc=1, device_id=_coords(g["axes"], g["sizes"], t), device_id_type=MESH)
            return carry
        lax.fori_loop(1, n, greet, 0)
        expected += n - 1
    pl.semaphore_wait(barrier, expected)

    def remote(g, a, src, dst, t):
        if g["ins"][a].shape[0] == 1:
            src = 0
        return pltpu.make_async_remote_copy(
            src_ref=g["ins"][a].at[src], dst_ref=g["outs"][a].at[dst],
            send_sem=g["send"].at[a, src], recv_sem=g["recv"].at[a, dst],
            device_id=_coords(g["axes"], g["sizes"], t), device_id_type=MESH)

    def own(g, a):
        src = 0 if g["ins"][a].shape[0] == 1 else g["me"]
        return pltpu.make_async_copy(g["ins"][a].at[src], g["outs"][a].at[g["me"]], g["local"].at[a])

    for g in groups:
        for a in range(len(g["ins"])):
            own(g, a).start()
    for g in groups:
        n, me = g["n"], g["me"]
        def start(o, carry, g=g, n=n, me=me):
            t = lax.rem(me + _step(o) + n, n)
            for a in range(len(g["ins"])):
                remote(g, a, t, me, t).start()
            return carry
        lax.fori_loop(1, n, start, 0)
    for g in groups:
        n, me = g["n"], g["me"]
        def finish(o, carry, g=g, n=n, me=me):
            t = lax.rem(me + _step(o) + n, n)
            s = lax.rem(me - _step(o) + n, n)
            for a in range(len(g["ins"])):
                remote(g, a, t, me, t).wait_send()
                remote(g, a, me, s, s).wait_recv()
            return carry
        lax.fori_loop(1, n, finish, 0)
        for a in range(len(g["ins"])):
            own(g, a).wait()


def exchange(groups, collective_id):
    plan, arrays, scratch, n_of = [], [], [], []
    for axes, arrs in groups:
        axes = tuple(axes)
        sizes = tuple(lax.axis_size(a) for a in axes)
        n = int(np.prod(sizes))
        plan.append((axes, sizes, len(arrs)))
        arrays.extend(arrs)
        n_of.extend([n] * len(arrs))
        scratch += [pltpu.SemaphoreType.DMA((len(arrs), n)), pltpu.SemaphoreType.DMA((len(arrs), n)),
                    pltpu.SemaphoreType.DMA((len(arrs),))]
    vmem = pl.BlockSpec(memory_space=pltpu.VMEM)
    return pl.pallas_call(
        functools.partial(exchange_kernel, tuple(plan)),
        out_shape=[jax.ShapeDtypeStruct((n_of[i],) + a.shape[1:], a.dtype) for i, a in enumerate(arrays)],
        in_specs=[vmem] * len(arrays),
        out_specs=[vmem] * len(arrays),
        scratch_shapes=scratch,
        compiler_params=pltpu.CompilerParams(has_side_effects=True, collective_id=collective_id),
    )(*arrays)


def tail_kernel(shape, h_ref, cust_ref, sorted_ref, pos_ref, wback_ref, out_ref):
    rows = h_ref.shape[0]
    ret_cust = jnp.dot(order_matrix(rows, *shape), cust_ref[...], preferred_element_type=f32).astype(bf16)
    unperm = (column_of(pos_ref) == lax.broadcasted_iota(jnp.int32, (rows, rows), 1)).astype(bf16)
    ret_prod = jnp.dot(unperm, sorted_ref[...], preferred_element_type=f32).astype(bf16)
    back = jnp.dot(ret_cust, wback_ref[:H, :], preferred_element_type=f32) + jnp.dot(
        ret_prod, wback_ref[H:, :], preferred_element_type=f32
    )
    out_ref[...] = rms_norm(h_ref[...].astype(f32) + back).astype(bf16)


def tail(review_h, cust_rows, shape, sorted_rows, position, w_back):
    vmem = pl.BlockSpec(memory_space=pltpu.VMEM)
    return pl.pallas_call(
        functools.partial(tail_kernel, shape),
        out_shape=jax.ShapeDtypeStruct(review_h.shape, bf16),
        in_specs=[vmem] * 5,
        out_specs=vmem,
    )(review_h, cust_rows, sorted_rows, position.reshape(1, -1), w_back)


def order_matrix(rows, cust_slots, cust_size, stage_rows, cust_run):
    s = lax.broadcasted_iota(jnp.int32, (rows, rows), 0)
    src = ((s // cust_slots) % cust_size) * stage_rows + (s // cust_run) * cust_slots + s % cust_slots
    return (src == lax.broadcasted_iota(jnp.int32, (rows, rows), 1)).astype(bf16)


def route_kernel(rev_size, cust_slots, sent_ref, pgot_ref, pids_ref, stage_ref, pack_ref):
    rows = sent_ref.shape[0]
    s = lax.broadcasted_iota(jnp.int32, (rows, rows), 0)
    stage_rows = rev_size * cust_slots
    cust_run = rows // rev_size
    src = (s % stage_rows) // cust_slots * cust_run + (s // stage_rows) * cust_slots + s % cust_slots
    move = (src == lax.broadcasted_iota(jnp.int32, (rows, rows), 1)).astype(bf16)
    stage_ref[...] = jnp.dot(move, sent_ref[...], preferred_element_type=f32).astype(bf16)
    prows = pack_ref.shape[0]
    pick = (lax.broadcasted_iota(jnp.int32, (prows, pids_ref.shape[1]), 0) == pids_ref[...]).astype(bf16)
    pack_ref[:, :H] = jnp.dot(pick, pgot_ref[...], preferred_element_type=f32).astype(bf16)
    cnt = jnp.sum(pick.astype(f32), axis=1, keepdims=True)
    hi = jnp.floor(cnt * (1.0 / 64.0))
    lo = cnt - 64.0 * hi
    lane = lax.broadcasted_iota(jnp.int32, (prows, LANES), 1)
    pack_ref[:, H:] = jnp.where(lane == 0, hi, jnp.where(lane == 1, lo, 0.0)).astype(bf16)


def route_step(sent1, prod_got, prod_got_ids, rev_size, cust_slots, prod_rows):
    rows = sent1.shape[0]
    vmem = pl.BlockSpec(memory_space=pltpu.VMEM)
    return pl.pallas_call(
        functools.partial(route_kernel, rev_size, cust_slots),
        in_specs=[vmem] * 3,
        out_specs=[vmem] * 2,
        out_shape=[
            jax.ShapeDtypeStruct((rows, H), bf16),
            jax.ShapeDtypeStruct((prod_rows, H + LANES), bf16),
        ],
    )(sent1, prod_got, prod_got_ids.reshape(1, -1))


def refresh_rows(sums, counts, states, weight):
    normed = (sums / jnp.sqrt(jnp.maximum(counts, 1.0))).astype(bf16)
    update = jax.nn.silu(jnp.dot(normed, weight, preferred_element_type=f32))
    return rms_norm(states.astype(f32) + update).astype(bf16)


def column_of(row_ref):
    return jnp.transpose(jnp.broadcast_to(row_ref[...], (8, row_ref.shape[1])))[:, 0:1]


def gather_kernel(rev_axis, gids_ref, grows_ref, spread_ref, pstate_ref, wpu_ref, pack_ref, pnew_ref):
    rows = pack_ref.shape[0]
    pick = (lax.broadcasted_iota(jnp.int32, (rows, gids_ref.shape[1]), 0) == gids_ref[...]).astype(bf16)
    pack_ref[:, :H] = jnp.dot(pick, grows_ref[...], preferred_element_type=f32)
    cnt = jnp.sum(pick.astype(f32), axis=1, keepdims=True)
    pack_ref[:, H:] = jnp.broadcast_to(cnt, (rows, LANES))
    whole = spread_ref[0].astype(f32)
    for i in range(1, spread_ref.shape[0]):
        whole = whole + spread_ref[i].astype(f32)
    own = pnew_ref.shape[0]
    counts = whole[:, H:H + 1] * 64.0 + whole[:, H + 1:H + 2]
    start = pl.multiple_of(lax.axis_index(rev_axis) * own, own)
    pnew_ref[...] = refresh_rows(whole[:, :H], counts, pstate_ref[pl.ds(start, own), :], wpu_ref[...])


def gather_step(got_ids, got_rows, spread, prod_state, w_prod_up, cust_rows):
    own = prod_state.shape[0] // spread.shape[0]
    vmem = pl.BlockSpec(memory_space=pltpu.VMEM)
    return pl.pallas_call(
        functools.partial(gather_kernel, "rev"),
        in_specs=[vmem] * 5,
        out_specs=[vmem] * 2,
        out_shape=[
            jax.ShapeDtypeStruct((cust_rows, H + LANES), f32),
            jax.ShapeDtypeStruct((own, H), bf16),
        ],
    )(got_ids.reshape(1, -1), got_rows, spread, prod_state, w_prod_up)


def reply_kernel(shape, both_ref, cstate_ref, wcu_ref, gids_ref, newprod_ref, pids_ref, newcust_ref, creply_ref, preply_ref):
    tot = both_ref[0] + both_ref[1]
    new_cust = refresh_rows(tot[:, :H], tot[:, H:H + 1], cstate_ref[...], wcu_ref[...])
    newcust_ref[...] = new_cust
    n = gids_ref.shape[1]
    pick_t = (column_of(gids_ref) == lax.broadcasted_iota(jnp.int32, (n, new_cust.shape[0]), 1)).astype(bf16)
    reply = jnp.dot(pick_t, new_cust, preferred_element_type=f32).astype(bf16)
    creply_ref[...] = jnp.dot(order_matrix(n, *shape), reply, preferred_element_type=f32).astype(bf16)
    m = pids_ref.shape[1]
    ppick_t = (column_of(pids_ref) == lax.broadcasted_iota(jnp.int32, (m, newprod_ref.shape[0]), 1)).astype(bf16)
    preply_ref[...] = jnp.dot(ppick_t, newprod_ref[...], preferred_element_type=f32).astype(bf16)


def reply_step(cust_both, cust_state, w_cust_up, got_ids, shape, new_prod, prod_got_ids):
    vmem = pl.BlockSpec(memory_space=pltpu.VMEM)
    n = got_ids.size
    return pl.pallas_call(
        functools.partial(reply_kernel, shape),
        in_specs=[vmem] * 6,
        out_specs=[vmem] * 3,
        out_shape=[
            jax.ShapeDtypeStruct(cust_state.shape, bf16),
            jax.ShapeDtypeStruct((n, H), bf16),
            jax.ShapeDtypeStruct((prod_got_ids.size, H), bf16),
        ],
    )(cust_both, cust_state, w_cust_up, got_ids.reshape(1, -1), new_prod, prod_got_ids.reshape(1, -1))


def refresh(totals, counts, states, weight):
    normed_sum = (totals / jnp.sqrt(jnp.maximum(counts, 1.0))[:, None]).astype(bf16)
    update = jax.nn.silu(jnp.dot(normed_sum, weight, preferred_element_type=f32))
    return rms_norm(states.astype(f32) + update).astype(bf16)


def pick_back(picker, states):
    return lax.dot_general(
        picker, states, (((0,), (0,)), ((), ())), preferred_element_type=f32
    ).astype(bf16)


def one_hot_rows(ids, rows):
    return (ids.reshape(1, -1) == jnp.arange(rows, dtype=jnp.int32)[:, None]).astype(bf16)


def on_device(
    review_cols,
    cust_state,
    prod_state,
    w_qkv,
    w_out,
    w_msg,
    w_cust_up,
    w_prod_up,
    w_back,
    cust_slot,
    prod_slot,
    prod_pos,
    live_count,
):
    review_rows = review_cols.shape[0]
    rev_size = lax.axis_size("rev")
    cust_size = lax.axis_size("cust")
    prod_size = lax.axis_size("prod")
    cust_owners = rev_size * cust_size
    cust_slots = review_rows // cust_owners
    prod_owners = cust_size * prod_size
    prod_slots = review_rows // prod_owners
    cust_rows = cust_state.shape[0]
    prod_rows = prod_state.shape[0]
    own_rows = prod_rows // rev_size

    filled = jnp.arange(cust_slots, dtype=jnp.int32)[None, :] < live_count.reshape(cust_owners, 1)
    live = filled.reshape(review_rows)
    cust_ids = jnp.where(filled, cust_slot.reshape(cust_owners, cust_slots), -1)
    position = prod_pos.reshape(review_rows)
    id_plus = jnp.where(live, prod_slot + 1, 0)
    id_lane = jnp.arange(LANES, dtype=jnp.int32)[None, :]
    id_cols = jnp.where(
        id_lane == 0, (id_plus // 32)[:, None], jnp.where(id_lane == 1, (id_plus % 32)[:, None], 0)
    ).astype(bf16)
    review_h, to_cust, prod_msgs, sorted_ids = encode(review_cols, w_qkv, w_out, w_msg, position, id_cols)
    prod_ids = (sorted_ids[:, 0] * 32.0 + sorted_ids[:, 1]).astype(jnp.int32) - 1

    cust_run = cust_size * cust_slots
    stage_rows = rev_size * cust_slots
    sent1, ids1, prod_got, prod_got_ids = exchange(
        [
            (("rev",), [to_cust.reshape(rev_size, cust_run, H), cust_ids.reshape(rev_size, 1, cust_run)]),
            (("cust", "prod"), [prod_msgs.reshape(prod_owners, prod_slots, H),
                                prod_ids.reshape(prod_owners, 1, prod_slots)]),
        ],
        0,
    )
    stage2, prod_pack = route_step(
        sent1.reshape(review_rows, H), prod_got.reshape(review_rows, H), prod_got_ids, rev_size, cust_slots, prod_rows
    )
    ids2 = ids1.reshape(rev_size, cust_size, cust_slots).transpose(1, 0, 2)
    got_rows, got_ids, spread = exchange(
        [
            (("cust",), [stage2.reshape(cust_size, stage_rows, H), ids2.reshape(cust_size, 1, stage_rows)]),
            (("rev",), [prod_pack.reshape(rev_size, own_rows, H + LANES)]),
        ],
        1,
    )
    cust_pack, own_new = gather_step(
        got_ids, got_rows.reshape(review_rows, H), spread, prod_state, w_prod_up, cust_rows
    )

    cust_both, new_prod = exchange(
        [
            (("prod",), [cust_pack[None]]),
            (("rev",), [own_new[None]]),
        ],
        2,
    )
    new_prod = new_prod.reshape(prod_rows, H)
    shape = (cust_slots, cust_size, stage_rows, cust_run)
    new_cust, reply, prod_reply = reply_step(
        cust_both, cust_state, w_cust_up, got_ids, shape, new_prod, prod_got_ids
    )
    back1, ret_sorted = exchange(
        [
            (("rev",), [reply.reshape(rev_size, cust_run, H)]),
            (("cust", "prod"), [prod_reply.reshape(prod_owners, prod_slots, H)]),
        ],
        3,
    )
    back2 = back1.reshape(rev_size, cust_size, cust_slots, H).transpose(1, 0, 2, 3)
    (ret_cust,) = exchange([(("cust",), [back2.reshape(cust_size, stage_rows, H)])], 4)
    review_out = tail(
        review_h, ret_cust.reshape(review_rows, H), shape, ret_sorted.reshape(review_rows, H), position, w_back
    )
    return (review_out, new_cust, new_prod)


def solution(mesh):
    in_specs = (
        P(("rev", "cust", "prod"), None),
        P(("rev", "cust"), None),
        P(("cust", "prod"), None),
        P(),
        P(),
        P(),
        P(),
        P(),
        P(),
        P(("rev", "cust", "prod")),
        P(("rev", "cust", "prod")),
        P(("rev", "cust", "prod"), None),
        P(("rev", "cust", "prod"), None),
    )
    out_specs = (
        P(("rev", "cust", "prod"), None),
        P(("rev", "cust"), None),
        P(("cust", "prod"), None),
    )
    return jax.shard_map(
        on_device, mesh=mesh, in_specs=in_specs, out_specs=out_specs, check_vma=False
    )
```

```python
import math

import jax
import jax.numpy as jnp
from jax import lax
import functools

import numpy as np
from jax.experimental import pallas as pl
from jax.experimental.pallas import tpu as pltpu
from jax.sharding import PartitionSpec as P

H = 512
HEADS = 8
NCOL = 4
HD = 64
LANES = 128
f32 = jnp.float32
bf16 = jnp.bfloat16


def rms_norm(vector):
    return vector * lax.rsqrt(jnp.mean(vector * vector, axis=-1, keepdims=True) + 1e-06)


def encode_kernel(x_ref, wqkv_ref, wout_ref, wmsg_ref, pos_ref, idc_ref, h_ref, cust_ref, prod_ref, ids_ref):
    head = lax.broadcasted_iota(jnp.int32, (H, LANES), 0) // HD
    lane = lax.broadcasted_iota(jnp.int32, (H, LANES), 1)
    e = [(lane == i * HEADS + head).astype(bf16) for i in range(NCOL)]
    head_t = lax.broadcasted_iota(jnp.int32, (LANES, H), 1) // HD
    lane_t = lax.broadcasted_iota(jnp.int32, (LANES, H), 0)
    et = [(lane_t == i * HEADS + head_t).astype(bf16) for i in range(NCOL)]
    xs = [x_ref[:, i * H:(i + 1) * H] for i in range(NCOL)]
    q, k, v = [], [], []
    for i in range(NCOL):
        qkv = jnp.dot(xs[i], wqkv_ref[...], preferred_element_type=f32).astype(bf16)
        q.append(qkv[:, :H].astype(f32))
        k.append(qkv[:, H:2 * H].astype(f32))
        v.append(qkv[:, 2 * H:].astype(f32))
    scores = []
    for j in range(NCOL):
        s = None
        for i in range(NCOL):
            term = jnp.dot((q[i] * k[j]).astype(bf16), e[i], preferred_element_type=f32)
            s = term if s is None else s + term
        scores.append(s * (1.0 / math.sqrt(HD)))
    top = jnp.maximum(jnp.maximum(scores[0], scores[1]), jnp.maximum(scores[2], scores[3]))
    expon = [jnp.exp(s - top) for s in scores]
    total = (expon[0] + expon[1]) + (expon[2] + expon[3])
    weights = [(x / total).astype(bf16) for x in expon]
    pooled = None
    for i in range(NCOL):
        att = None
        for j in range(NCOL):
            term = jnp.dot(weights[j], et[i], preferred_element_type=f32) * v[j]
            att = term if att is None else att + term
        mixed = xs[i].astype(f32) + jnp.dot(att.astype(bf16), wout_ref[...], preferred_element_type=f32)
        pooled = mixed if pooled is None else pooled + mixed
    pooled = pooled * (1.0 / NCOL)
    h = rms_norm(pooled).astype(bf16)
    h_ref[...] = h
    msg = jnp.dot(h, wmsg_ref[...], preferred_element_type=f32).astype(bf16)
    cust_ref[...] = msg[:, :H]
    rows = pos_ref.shape[1]
    perm = (lax.broadcasted_iota(jnp.int32, (rows, rows), 0) == pos_ref[...]).astype(bf16)
    prod_ref[...] = jnp.dot(perm, msg[:, H:], preferred_element_type=f32).astype(bf16)
    ids_ref[...] = jnp.dot(perm, idc_ref[...], preferred_element_type=f32)


def encode(cols, w_qkv, w_out, w_msg, position, id_cols):
    rows = cols.shape[0]
    vmem = pl.BlockSpec(memory_space=pltpu.VMEM)
    return pl.pallas_call(
        encode_kernel,
        in_specs=[vmem] * 6,
        out_specs=[vmem] * 4,
        out_shape=[
            jax.ShapeDtypeStruct((rows, H), bf16),
            jax.ShapeDtypeStruct((rows, H), bf16),
            jax.ShapeDtypeStruct((rows, H), bf16),
            jax.ShapeDtypeStruct((rows, LANES), f32),
        ],
    )(cols, w_qkv, w_out, w_msg, position.reshape(1, rows), id_cols)

MESH = pl.DeviceIdType.MESH


def _coords(axes, sizes, t):
    out = {}
    for name, size in reversed(list(zip(axes, sizes))):
        out[name] = t % size
        t = t // size
    return out


def _step(o):
    return ((o + 1) // 2) * (2 * (o % 2) - 1)


def exchange_kernel(plan, *refs):
    total = sum(c for _, _, c in plan)
    ins, outs = refs[:total], refs[total:2 * total]
    sems = refs[2 * total:]
    groups = []
    at, s_at = 0, 0
    for axes, sizes, count in plan:
        n = int(np.prod(sizes))
        me = 0
        for name, size in zip(axes, sizes):
            me = me * size + lax.axis_index(name)
        groups.append(dict(axes=axes, sizes=sizes, n=n, me=me, ins=ins[at:at + count], outs=outs[at:at + count],
                           send=sems[s_at], recv=sems[s_at + 1], local=sems[s_at + 2]))
        at += count
        s_at += 3

    barrier = pltpu.get_barrier_semaphore()
    expected = 0
    for g in groups:
        n, me = g["n"], g["me"]
        def greet(o, carry, g=g, n=n, me=me):
            t = lax.rem(me + o, n)
            pl.semaphore_signal(barrier, inc=1, device_id=_coords(g["axes"], g["sizes"], t), device_id_type=MESH)
            return carry
        lax.fori_loop(1, n, greet, 0)
        expected += n - 1
    pl.semaphore_wait(barrier, expected)

    def remote(g, a, src, dst, t):
        if g["ins"][a].shape[0] == 1:
            src = 0
        return pltpu.make_async_remote_copy(
            src_ref=g["ins"][a].at[src], dst_ref=g["outs"][a].at[dst],
            send_sem=g["send"].at[a, src], recv_sem=g["recv"].at[a, dst],
            device_id=_coords(g["axes"], g["sizes"], t), device_id_type=MESH)

    def own(g, a):
        src = 0 if g["ins"][a].shape[0] == 1 else g["me"]
        return pltpu.make_async_copy(g["ins"][a].at[src], g["outs"][a].at[g["me"]], g["local"].at[a])

    for g in groups:
        for a in range(len(g["ins"])):
            own(g, a).start()
    for g in groups:
        n, me = g["n"], g["me"]
        def start(o, carry, g=g, n=n, me=me):
            t = lax.rem(me + _step(o) + n, n)
            for a in range(len(g["ins"])):
                remote(g, a, t, me, t).start()
            return carry
        lax.fori_loop(1, n, start, 0)
    for g in groups:
        n, me = g["n"], g["me"]
        def finish(o, carry, g=g, n=n, me=me):
            t = lax.rem(me + _step(o) + n, n)
            s = lax.rem(me - _step(o) + n, n)
            for a in range(len(g["ins"])):
                remote(g, a, t, me, t).wait_send()
                remote(g, a, me, s, s).wait_recv()
            return carry
        lax.fori_loop(1, n, finish, 0)
        for a in range(len(g["ins"])):
            own(g, a).wait()


def exchange(groups, collective_id):
    plan, arrays, scratch, n_of = [], [], [], []
    for axes, arrs in groups:
        axes = tuple(axes)
        sizes = tuple(lax.axis_size(a) for a in axes)
        n = int(np.prod(sizes))
        plan.append((axes, sizes, len(arrs)))
        arrays.extend(arrs)
        n_of.extend([n] * len(arrs))
        scratch += [pltpu.SemaphoreType.DMA((len(arrs), n)), pltpu.SemaphoreType.DMA((len(arrs), n)),
                    pltpu.SemaphoreType.DMA((len(arrs),))]
    vmem = pl.BlockSpec(memory_space=pltpu.VMEM)
    return pl.pallas_call(
        functools.partial(exchange_kernel, tuple(plan)),
        out_shape=[jax.ShapeDtypeStruct((n_of[i],) + a.shape[1:], a.dtype) for i, a in enumerate(arrays)],
        in_specs=[vmem] * len(arrays),
        out_specs=[vmem] * len(arrays),
        scratch_shapes=scratch,
        compiler_params=pltpu.CompilerParams(has_side_effects=True, collective_id=collective_id),
    )(*arrays)


def tail_kernel(shape, h_ref, cust_ref, sorted_ref, pos_ref, wback_ref, out_ref):
    rows = h_ref.shape[0]
    ret_cust = jnp.dot(order_matrix(rows, *shape), cust_ref[...], preferred_element_type=f32).astype(bf16)
    unperm = (column_of(pos_ref) == lax.broadcasted_iota(jnp.int32, (rows, rows), 1)).astype(bf16)
    ret_prod = jnp.dot(unperm, sorted_ref[...], preferred_element_type=f32).astype(bf16)
    back = jnp.dot(ret_cust, wback_ref[:H, :], preferred_element_type=f32) + jnp.dot(
        ret_prod, wback_ref[H:, :], preferred_element_type=f32
    )
    out_ref[...] = rms_norm(h_ref[...].astype(f32) + back).astype(bf16)


def tail(review_h, cust_rows, shape, sorted_rows, position, w_back):
    vmem = pl.BlockSpec(memory_space=pltpu.VMEM)
    return pl.pallas_call(
        functools.partial(tail_kernel, shape),
        out_shape=jax.ShapeDtypeStruct(review_h.shape, bf16),
        in_specs=[vmem] * 5,
        out_specs=vmem,
    )(review_h, cust_rows, sorted_rows, position.reshape(1, -1), w_back)


def order_matrix(rows, cust_slots, cust_size, stage_rows, cust_run):
    s = lax.broadcasted_iota(jnp.int32, (rows, rows), 0)
    src = ((s // cust_slots) % cust_size) * stage_rows + (s // cust_run) * cust_slots + s % cust_slots
    return (src == lax.broadcasted_iota(jnp.int32, (rows, rows), 1)).astype(bf16)


def route_kernel(rev_size, cust_slots, sent_ref, pgot_ref, pids_ref, stage_ref, pack_ref):
    rows = sent_ref.shape[0]
    s = lax.broadcasted_iota(jnp.int32, (rows, rows), 0)
    stage_rows = rev_size * cust_slots
    cust_run = rows // rev_size
    src = (s % stage_rows) // cust_slots * cust_run + (s // stage_rows) * cust_slots + s % cust_slots
    move = (src == lax.broadcasted_iota(jnp.int32, (rows, rows), 1)).astype(bf16)
    stage_ref[...] = jnp.dot(move, sent_ref[...], preferred_element_type=f32).astype(bf16)
    prows = pack_ref.shape[0]
    pick = (lax.broadcasted_iota(jnp.int32, (prows, pids_ref.shape[1]), 0) == pids_ref[...]).astype(bf16)
    pack_ref[:, :H] = jnp.dot(pick, pgot_ref[...], preferred_element_type=f32).astype(bf16)
    cnt = jnp.sum(pick.astype(f32), axis=1, keepdims=True)
    hi = jnp.floor(cnt * (1.0 / 64.0))
    lo = cnt - 64.0 * hi
    lane = lax.broadcasted_iota(jnp.int32, (prows, LANES), 1)
    pack_ref[:, H:] = jnp.where(lane == 0, hi, jnp.where(lane == 1, lo, 0.0)).astype(bf16)


def route_step(sent1, prod_got, prod_got_ids, rev_size, cust_slots, prod_rows):
    rows = sent1.shape[0]
    vmem = pl.BlockSpec(memory_space=pltpu.VMEM)
    return pl.pallas_call(
        functools.partial(route_kernel, rev_size, cust_slots),
        in_specs=[vmem] * 3,
        out_specs=[vmem] * 2,
        out_shape=[
            jax.ShapeDtypeStruct((rows, H), bf16),
            jax.ShapeDtypeStruct((prod_rows, H + LANES), bf16),
        ],
    )(sent1, prod_got, prod_got_ids.reshape(1, -1))


def refresh_rows(sums, counts, states, weight):
    normed = (sums / jnp.sqrt(jnp.maximum(counts, 1.0))).astype(bf16)
    update = jax.nn.silu(jnp.dot(normed, weight, preferred_element_type=f32))
    return rms_norm(states.astype(f32) + update).astype(bf16)


def column_of(row_ref):
    return jnp.transpose(jnp.broadcast_to(row_ref[...], (8, row_ref.shape[1])))[:, 0:1]


def gather_kernel(rev_axis, gids_ref, grows_ref, spread_ref, pstate_ref, wpu_ref, pack_ref, pnew_ref):
    rows = pack_ref.shape[0]
    pick = (lax.broadcasted_iota(jnp.int32, (rows, gids_ref.shape[1]), 0) == gids_ref[...]).astype(bf16)
    pack_ref[:, :H] = jnp.dot(pick, grows_ref[...], preferred_element_type=f32)
    cnt = jnp.sum(pick.astype(f32), axis=1, keepdims=True)
    pack_ref[:, H:] = jnp.broadcast_to(cnt, (rows, LANES))
    whole = spread_ref[0].astype(f32)
    for i in range(1, spread_ref.shape[0]):
        whole = whole + spread_ref[i].astype(f32)
    own = pnew_ref.shape[0]
    counts = whole[:, H:H + 1] * 64.0 + whole[:, H + 1:H + 2]
    start = pl.multiple_of(lax.axis_index(rev_axis) * own, own)
    pnew_ref[...] = refresh_rows(whole[:, :H], counts, pstate_ref[pl.ds(start, own), :], wpu_ref[...])


def gather_step(got_ids, got_rows, spread, prod_state, w_prod_up, cust_rows):
    own = prod_state.shape[0] // spread.shape[0]
    vmem = pl.BlockSpec(memory_space=pltpu.VMEM)
    return pl.pallas_call(
        functools.partial(gather_kernel, "rev"),
        in_specs=[vmem] * 5,
        out_specs=[vmem] * 2,
        out_shape=[
            jax.ShapeDtypeStruct((cust_rows, H + LANES), f32),
            jax.ShapeDtypeStruct((own, H), bf16),
        ],
    )(got_ids.reshape(1, -1), got_rows, spread, prod_state, w_prod_up)


def reply_kernel(shape, both_ref, cstate_ref, wcu_ref, gids_ref, newprod_ref, pids_ref, newcust_ref, creply_ref, preply_ref):
    tot = both_ref[0] + both_ref[1]
    new_cust = refresh_rows(tot[:, :H], tot[:, H:H + 1], cstate_ref[...], wcu_ref[...])
    newcust_ref[...] = new_cust
    n = gids_ref.shape[1]
    pick_t = (column_of(gids_ref) == lax.broadcasted_iota(jnp.int32, (n, new_cust.shape[0]), 1)).astype(bf16)
    reply = jnp.dot(pick_t, new_cust, preferred_element_type=f32).astype(bf16)
    creply_ref[...] = jnp.dot(order_matrix(n, *shape), reply, preferred_element_type=f32).astype(bf16)
    m = pids_ref.shape[1]
    ppick_t = (column_of(pids_ref) == lax.broadcasted_iota(jnp.int32, (m, newprod_ref.shape[0]), 1)).astype(bf16)
    preply_ref[...] = jnp.dot(ppick_t, newprod_ref[...], preferred_element_type=f32).astype(bf16)


def reply_step(cust_both, cust_state, w_cust_up, got_ids, shape, new_prod, prod_got_ids):
    vmem = pl.BlockSpec(memory_space=pltpu.VMEM)
    n = got_ids.size
    return pl.pallas_call(
        functools.partial(reply_kernel, shape),
        in_specs=[vmem] * 6,
        out_specs=[vmem] * 3,
        out_shape=[
            jax.ShapeDtypeStruct(cust_state.shape, bf16),
            jax.ShapeDtypeStruct((n, H), bf16),
            jax.ShapeDtypeStruct((prod_got_ids.size, H), bf16),
        ],
    )(cust_both, cust_state, w_cust_up, got_ids.reshape(1, -1), new_prod, prod_got_ids.reshape(1, -1))


def refresh(totals, counts, states, weight):
    normed_sum = (totals / jnp.sqrt(jnp.maximum(counts, 1.0))[:, None]).astype(bf16)
    update = jax.nn.silu(jnp.dot(normed_sum, weight, preferred_element_type=f32))
    return rms_norm(states.astype(f32) + update).astype(bf16)


def pick_back(picker, states):
    return lax.dot_general(
        picker, states, (((0,), (0,)), ((), ())), preferred_element_type=f32
    ).astype(bf16)


def one_hot_rows(ids, rows):
    return (ids.reshape(1, -1) == jnp.arange(rows, dtype=jnp.int32)[:, None]).astype(bf16)


def on_device(
    review_cols,
    cust_state,
    prod_state,
    w_qkv,
    w_out,
    w_msg,
    w_cust_up,
    w_prod_up,
    w_back,
    cust_slot,
    prod_slot,
    prod_pos,
    live_count,
):
    review_rows = review_cols.shape[0]
    rev_size = lax.axis_size("rev")
    cust_size = lax.axis_size("cust")
    prod_size = lax.axis_size("prod")
    cust_owners = rev_size * cust_size
    cust_slots = review_rows // cust_owners
    prod_owners = cust_size * prod_size
    prod_slots = review_rows // prod_owners
    cust_rows = cust_state.shape[0]
    prod_rows = prod_state.shape[0]
    own_rows = prod_rows // rev_size

    filled = jnp.arange(cust_slots, dtype=jnp.int32)[None, :] < live_count.reshape(cust_owners, 1)
    live = filled.reshape(review_rows)
    cust_ids = jnp.where(filled, cust_slot.reshape(cust_owners, cust_slots), -1)
    position = prod_pos.reshape(review_rows)
    id_plus = jnp.where(live, prod_slot + 1, 0)
    id_lane = jnp.arange(LANES, dtype=jnp.int32)[None, :]
    id_cols = jnp.where(
        id_lane == 0, (id_plus // 32)[:, None], jnp.where(id_lane == 1, (id_plus % 32)[:, None], 0)
    ).astype(bf16)
    review_h, to_cust, prod_msgs, sorted_ids = encode(review_cols, w_qkv, w_out, w_msg, position, id_cols)
    prod_ids = (sorted_ids[:, 0] * 32.0 + sorted_ids[:, 1]).astype(jnp.int32) - 1

    cust_run = cust_size * cust_slots
    stage_rows = rev_size * cust_slots
    sent1, ids1, prod_got, prod_got_ids = exchange(
        [
            (("rev",), [to_cust.reshape(rev_size, cust_run, H), cust_ids.reshape(rev_size, 1, cust_run)]),
            (("cust", "prod"), [prod_msgs.reshape(prod_owners, prod_slots, H),
                                prod_ids.reshape(prod_owners, 1, prod_slots)]),
        ],
        0,
    )
    stage2, prod_pack = route_step(
        sent1.reshape(review_rows, H), prod_got.reshape(review_rows, H), prod_got_ids, rev_size, cust_slots, prod_rows
    )
    ids2 = ids1.reshape(rev_size, cust_size, cust_slots).transpose(1, 0, 2)
    got_rows, got_ids, spread = exchange(
        [
            (("cust",), [stage2.reshape(cust_size, stage_rows, H), ids2.reshape(cust_size, 1, stage_rows)]),
            (("rev",), [prod_pack.reshape(rev_size, own_rows, H + LANES)]),
        ],
        1,
    )
    cust_pack, own_new = gather_step(
        got_ids, got_rows.reshape(review_rows, H), spread, prod_state, w_prod_up, cust_rows
    )

    cust_both, new_prod = exchange(
        [
            (("prod",), [cust_pack[None]]),
            (("rev",), [own_new[None]]),
        ],
        2,
    )
    new_prod = new_prod.reshape(prod_rows, H)
    shape = (cust_slots, cust_size, stage_rows, cust_run)
    new_cust, reply, prod_reply = reply_step(
        cust_both, cust_state, w_cust_up, got_ids, shape, new_prod, prod_got_ids
    )
    back1, ret_sorted = exchange(
        [
            (("rev",), [reply.reshape(rev_size, cust_run, H)]),
            (("cust", "prod"), [prod_reply.reshape(prod_owners, prod_slots, H)]),
        ],
        3,
    )
    back2 = back1.reshape(rev_size, cust_size, cust_slots, H).transpose(1, 0, 2, 3)
    (ret_cust,) = exchange([(("cust",), [back2.reshape(cust_size, stage_rows, H)])], 4)
    review_out = tail(
        review_h, ret_cust.reshape(review_rows, H), shape, ret_sorted.reshape(review_rows, H), position, w_back
    )
    return (review_out, new_cust, new_prod)


def solution(mesh):
    in_specs = (
        P(("rev", "cust", "prod"), None),
        P(("rev", "cust"), None),
        P(("cust", "prod"), None),
        P(),
        P(),
        P(),
        P(),
        P(),
        P(),
        P(("rev", "cust", "prod")),
        P(("rev", "cust", "prod")),
        P(("rev", "cust", "prod"), None),
        P(("rev", "cust", "prod"), None),
    )
    out_specs = (
        P(("rev", "cust", "prod"), None),
        P(("rev", "cust"), None),
        P(("cust", "prod"), None),
    )
    return jax.shard_map(
        on_device, mesh=mesh, in_specs=in_specs, out_specs=out_specs, check_vma=False
    )
```

```python
import math

import jax
import jax.numpy as jnp
from jax import lax
import functools

import numpy as np
from jax.experimental import pallas as pl
from jax.experimental.pallas import tpu as pltpu
from jax.sharding import PartitionSpec as P

H = 512
HEADS = 8
NCOL = 4
HD = 64
LANES = 128
f32 = jnp.float32
bf16 = jnp.bfloat16


def rms_norm(vector):
    return vector * lax.rsqrt(jnp.mean(vector * vector, axis=-1, keepdims=True) + 1e-06)


def encode_kernel(x_ref, wqkv_ref, wout_ref, wmsg_ref, pos_ref, idc_ref, h_ref, cust_ref, prod_ref, ids_ref):
    head = lax.broadcasted_iota(jnp.int32, (H, LANES), 0) // HD
    lane = lax.broadcasted_iota(jnp.int32, (H, LANES), 1)
    e = [(lane == i * HEADS + head).astype(bf16) for i in range(NCOL)]
    head_t = lax.broadcasted_iota(jnp.int32, (LANES, H), 1) // HD
    lane_t = lax.broadcasted_iota(jnp.int32, (LANES, H), 0)
    et = [(lane_t == i * HEADS + head_t).astype(bf16) for i in range(NCOL)]
    xs = [x_ref[:, i * H:(i + 1) * H] for i in range(NCOL)]
    q, k, v = [], [], []
    for i in range(NCOL):
        qkv = jnp.dot(xs[i], wqkv_ref[...], preferred_element_type=f32).astype(bf16)
        q.append(qkv[:, :H].astype(f32))
        k.append(qkv[:, H:2 * H].astype(f32))
        v.append(qkv[:, 2 * H:].astype(f32))
    scores = []
    for j in range(NCOL):
        s = None
        for i in range(NCOL):
            term = jnp.dot((q[i] * k[j]).astype(bf16), e[i], preferred_element_type=f32)
            s = term if s is None else s + term
        scores.append(s * (1.0 / math.sqrt(HD)))
    top = jnp.maximum(jnp.maximum(scores[0], scores[1]), jnp.maximum(scores[2], scores[3]))
    expon = [jnp.exp(s - top) for s in scores]
    total = (expon[0] + expon[1]) + (expon[2] + expon[3])
    weights = [(x / total).astype(bf16) for x in expon]
    pooled = None
    for i in range(NCOL):
        att = None
        for j in range(NCOL):
            term = jnp.dot(weights[j], et[i], preferred_element_type=f32) * v[j]
            att = term if att is None else att + term
        mixed = xs[i].astype(f32) + jnp.dot(att.astype(bf16), wout_ref[...], preferred_element_type=f32)
        pooled = mixed if pooled is None else pooled + mixed
    pooled = pooled * (1.0 / NCOL)
    h = rms_norm(pooled).astype(bf16)
    h_ref[...] = h
    msg = jnp.dot(h, wmsg_ref[...], preferred_element_type=f32).astype(bf16)
    cust_ref[...] = msg[:, :H]
    rows = pos_ref.shape[1]
    perm = (lax.broadcasted_iota(jnp.int32, (rows, rows), 0) == pos_ref[...]).astype(bf16)
    prod_ref[...] = jnp.dot(perm, msg[:, H:], preferred_element_type=f32).astype(bf16)
    ids_ref[...] = jnp.dot(perm, idc_ref[...], preferred_element_type=f32)


def encode(cols, w_qkv, w_out, w_msg, position, id_cols):
    rows = cols.shape[0]
    vmem = pl.BlockSpec(memory_space=pltpu.VMEM)
    return pl.pallas_call(
        encode_kernel,
        in_specs=[vmem] * 6,
        out_specs=[vmem] * 4,
        out_shape=[
            jax.ShapeDtypeStruct((rows, H), bf16),
            jax.ShapeDtypeStruct((rows, H), bf16),
            jax.ShapeDtypeStruct((rows, H), bf16),
            jax.ShapeDtypeStruct((rows, LANES), f32),
        ],
    )(cols, w_qkv, w_out, w_msg, position.reshape(1, rows), id_cols)

MESH = pl.DeviceIdType.MESH


def _coords(axes, sizes, t):
    out = {}
    for name, size in reversed(list(zip(axes, sizes))):
        out[name] = t % size
        t = t // size
    return out


def _step(o):
    return ((o + 1) // 2) * (2 * (o % 2) - 1)


def exchange_kernel(plan, *refs):
    total = sum(c for _, _, c in plan)
    ins, outs = refs[:total], refs[total:2 * total]
    sems = refs[2 * total:]
    groups = []
    at, s_at = 0, 0
    for axes, sizes, count in plan:
        n = int(np.prod(sizes))
        me = 0
        for name, size in zip(axes, sizes):
            me = me * size + lax.axis_index(name)
        groups.append(dict(axes=axes, sizes=sizes, n=n, me=me, ins=ins[at:at + count], outs=outs[at:at + count],
                           send=sems[s_at], recv=sems[s_at + 1], local=sems[s_at + 2]))
        at += count
        s_at += 3

    barrier = pltpu.get_barrier_semaphore()
    expected = 0
    for g in groups:
        n, me = g["n"], g["me"]
        def greet(o, carry, g=g, n=n, me=me):
            t = lax.rem(me + o, n)
            pl.semaphore_signal(barrier, inc=1, device_id=_coords(g["axes"], g["sizes"], t), device_id_type=MESH)
            return carry
        lax.fori_loop(1, n, greet, 0)
        expected += n - 1
    pl.semaphore_wait(barrier, expected)

    def remote(g, a, src, dst, t):
        if g["ins"][a].shape[0] == 1:
            src = 0
        return pltpu.make_async_remote_copy(
            src_ref=g["ins"][a].at[src], dst_ref=g["outs"][a].at[dst],
            send_sem=g["send"].at[a, src], recv_sem=g["recv"].at[a, dst],
            device_id=_coords(g["axes"], g["sizes"], t), device_id_type=MESH)

    def own(g, a):
        src = 0 if g["ins"][a].shape[0] == 1 else g["me"]
        return pltpu.make_async_copy(g["ins"][a].at[src], g["outs"][a].at[g["me"]], g["local"].at[a])

    for g in groups:
        for a in range(len(g["ins"])):
            own(g, a).start()
    for g in groups:
        n, me = g["n"], g["me"]
        def start(o, carry, g=g, n=n, me=me):
            t = lax.rem(me + _step(o) + n, n)
            for a in range(len(g["ins"])):
                remote(g, a, t, me, t).start()
            return carry
        lax.fori_loop(1, n, start, 0)
    for g in groups:
        n, me = g["n"], g["me"]
        def finish(o, carry, g=g, n=n, me=me):
            t = lax.rem(me + _step(o) + n, n)
            s = lax.rem(me - _step(o) + n, n)
            for a in range(len(g["ins"])):
                remote(g, a, t, me, t).wait_send()
                remote(g, a, me, s, s).wait_recv()
            return carry
        lax.fori_loop(1, n, finish, 0)
        for a in range(len(g["ins"])):
            own(g, a).wait()


def exchange(groups, collective_id):
    plan, arrays, scratch, n_of = [], [], [], []
    for axes, arrs in groups:
        axes = tuple(axes)
        sizes = tuple(lax.axis_size(a) for a in axes)
        n = int(np.prod(sizes))
        plan.append((axes, sizes, len(arrs)))
        arrays.extend(arrs)
        n_of.extend([n] * len(arrs))
        scratch += [pltpu.SemaphoreType.DMA((len(arrs), n)), pltpu.SemaphoreType.DMA((len(arrs), n)),
                    pltpu.SemaphoreType.DMA((len(arrs),))]
    vmem = pl.BlockSpec(memory_space=pltpu.VMEM)
    return pl.pallas_call(
        functools.partial(exchange_kernel, tuple(plan)),
        out_shape=[jax.ShapeDtypeStruct((n_of[i],) + a.shape[1:], a.dtype) for i, a in enumerate(arrays)],
        in_specs=[vmem] * len(arrays),
        out_specs=[vmem] * len(arrays),
        scratch_shapes=scratch,
        compiler_params=pltpu.CompilerParams(has_side_effects=True, collective_id=collective_id),
    )(*arrays)


def tail_kernel(shape, h_ref, cust_ref, sorted_ref, pos_ref, wback_ref, out_ref):
    rows = h_ref.shape[0]
    ret_cust = jnp.dot(order_matrix(rows, *shape), cust_ref[...], preferred_element_type=f32).astype(bf16)
    unperm = (column_of(pos_ref) == lax.broadcasted_iota(jnp.int32, (rows, rows), 1)).astype(bf16)
    ret_prod = jnp.dot(unperm, sorted_ref[...], preferred_element_type=f32).astype(bf16)
    back = jnp.dot(ret_cust, wback_ref[:H, :], preferred_element_type=f32) + jnp.dot(
        ret_prod, wback_ref[H:, :], preferred_element_type=f32
    )
    out_ref[...] = rms_norm(h_ref[...].astype(f32) + back).astype(bf16)


def tail(review_h, cust_rows, shape, sorted_rows, position, w_back):
    vmem = pl.BlockSpec(memory_space=pltpu.VMEM)
    return pl.pallas_call(
        functools.partial(tail_kernel, shape),
        out_shape=jax.ShapeDtypeStruct(review_h.shape, bf16),
        in_specs=[vmem] * 5,
        out_specs=vmem,
    )(review_h, cust_rows, sorted_rows, position.reshape(1, -1), w_back)


def order_matrix(rows, cust_slots, cust_size, stage_rows, cust_run):
    s = lax.broadcasted_iota(jnp.int32, (rows, rows), 0)
    src = ((s // cust_slots) % cust_size) * stage_rows + (s // cust_run) * cust_slots + s % cust_slots
    return (src == lax.broadcasted_iota(jnp.int32, (rows, rows), 1)).astype(bf16)


def route_kernel(rev_size, cust_slots, sent_ref, pgot_ref, pids_ref, stage_ref, pack_ref):
    rows = sent_ref.shape[0]
    s = lax.broadcasted_iota(jnp.int32, (rows, rows), 0)
    stage_rows = rev_size * cust_slots
    cust_run = rows // rev_size
    src = (s % stage_rows) // cust_slots * cust_run + (s // stage_rows) * cust_slots + s % cust_slots
    move = (src == lax.broadcasted_iota(jnp.int32, (rows, rows), 1)).astype(bf16)
    stage_ref[...] = jnp.dot(move, sent_ref[...], preferred_element_type=f32).astype(bf16)
    prows = pack_ref.shape[0]
    pick = (lax.broadcasted_iota(jnp.int32, (prows, pids_ref.shape[1]), 0) == pids_ref[...]).astype(bf16)
    pack_ref[:, :H] = jnp.dot(pick, pgot_ref[...], preferred_element_type=f32).astype(bf16)
    cnt = jnp.sum(pick.astype(f32), axis=1, keepdims=True)
    hi = jnp.floor(cnt * (1.0 / 64.0))
    lo = cnt - 64.0 * hi
    lane = lax.broadcasted_iota(jnp.int32, (prows, LANES), 1)
    pack_ref[:, H:] = jnp.where(lane == 0, hi, jnp.where(lane == 1, lo, 0.0)).astype(bf16)


def route_step(sent1, prod_got, prod_got_ids, rev_size, cust_slots, prod_rows):
    rows = sent1.shape[0]
    vmem = pl.BlockSpec(memory_space=pltpu.VMEM)
    return pl.pallas_call(
        functools.partial(route_kernel, rev_size, cust_slots),
        in_specs=[vmem] * 3,
        out_specs=[vmem] * 2,
        out_shape=[
            jax.ShapeDtypeStruct((rows, H), bf16),
            jax.ShapeDtypeStruct((prod_rows, H + LANES), bf16),
        ],
    )(sent1, prod_got, prod_got_ids.reshape(1, -1))


def refresh_rows(sums, counts, states, weight):
    normed = (sums / jnp.sqrt(jnp.maximum(counts, 1.0))).astype(bf16)
    update = jax.nn.silu(jnp.dot(normed, weight, preferred_element_type=f32))
    return rms_norm(states.astype(f32) + update).astype(bf16)


def column_of(row_ref):
    return jnp.transpose(jnp.broadcast_to(row_ref[...], (8, row_ref.shape[1])))[:, 0:1]


def gather_kernel(rev_axis, gids_ref, grows_ref, spread_ref, pstate_ref, wpu_ref, pack_ref, pnew_ref):
    rows = pack_ref.shape[0]
    pick = (lax.broadcasted_iota(jnp.int32, (rows, gids_ref.shape[1]), 0) == gids_ref[...]).astype(bf16)
    pack_ref[:, :H] = jnp.dot(pick, grows_ref[...], preferred_element_type=f32)
    cnt = jnp.sum(pick.astype(f32), axis=1, keepdims=True)
    pack_ref[:, H:] = jnp.broadcast_to(cnt, (rows, LANES))
    whole = spread_ref[0].astype(f32)
    for i in range(1, spread_ref.shape[0]):
        whole = whole + spread_ref[i].astype(f32)
    own = pnew_ref.shape[0]
    counts = whole[:, H:H + 1] * 64.0 + whole[:, H + 1:H + 2]
    start = pl.multiple_of(lax.axis_index(rev_axis) * own, own)
    pnew_ref[...] = refresh_rows(whole[:, :H], counts, pstate_ref[pl.ds(start, own), :], wpu_ref[...])


def gather_step(got_ids, got_rows, spread, prod_state, w_prod_up, cust_rows):
    own = prod_state.shape[0] // spread.shape[0]
    vmem = pl.BlockSpec(memory_space=pltpu.VMEM)
    return pl.pallas_call(
        functools.partial(gather_kernel, "rev"),
        in_specs=[vmem] * 5,
        out_specs=[vmem] * 2,
        out_shape=[
            jax.ShapeDtypeStruct((cust_rows, H + LANES), f32),
            jax.ShapeDtypeStruct((own, H), bf16),
        ],
    )(got_ids.reshape(1, -1), got_rows, spread, prod_state, w_prod_up)


def reply_kernel(shape, both_ref, cstate_ref, wcu_ref, gids_ref, newprod_ref, pids_ref, newcust_ref, creply_ref, preply_ref):
    tot = both_ref[0] + both_ref[1]
    new_cust = refresh_rows(tot[:, :H], tot[:, H:H + 1], cstate_ref[...], wcu_ref[...])
    newcust_ref[...] = new_cust
    n = gids_ref.shape[1]
    pick_t = (column_of(gids_ref) == lax.broadcasted_iota(jnp.int32, (n, new_cust.shape[0]), 1)).astype(bf16)
    reply = jnp.dot(pick_t, new_cust, preferred_element_type=f32).astype(bf16)
    creply_ref[...] = jnp.dot(order_matrix(n, *shape), reply, preferred_element_type=f32).astype(bf16)
    m = pids_ref.shape[1]
    ppick_t = (column_of(pids_ref) == lax.broadcasted_iota(jnp.int32, (m, newprod_ref.shape[0]), 1)).astype(bf16)
    preply_ref[...] = jnp.dot(ppick_t, newprod_ref[...], preferred_element_type=f32).astype(bf16)


def reply_step(cust_both, cust_state, w_cust_up, got_ids, shape, new_prod, prod_got_ids):
    vmem = pl.BlockSpec(memory_space=pltpu.VMEM)
    n = got_ids.size
    return pl.pallas_call(
        functools.partial(reply_kernel, shape),
        in_specs=[vmem] * 6,
        out_specs=[vmem] * 3,
        out_shape=[
            jax.ShapeDtypeStruct(cust_state.shape, bf16),
            jax.ShapeDtypeStruct((n, H), bf16),
            jax.ShapeDtypeStruct((prod_got_ids.size, H), bf16),
        ],
    )(cust_both, cust_state, w_cust_up, got_ids.reshape(1, -1), new_prod, prod_got_ids.reshape(1, -1))


def refresh(totals, counts, states, weight):
    normed_sum = (totals / jnp.sqrt(jnp.maximum(counts, 1.0))[:, None]).astype(bf16)
    update = jax.nn.silu(jnp.dot(normed_sum, weight, preferred_element_type=f32))
    return rms_norm(states.astype(f32) + update).astype(bf16)


def pick_back(picker, states):
    return lax.dot_general(
        picker, states, (((0,), (0,)), ((), ())), preferred_element_type=f32
    ).astype(bf16)


def one_hot_rows(ids, rows):
    return (ids.reshape(1, -1) == jnp.arange(rows, dtype=jnp.int32)[:, None]).astype(bf16)


def on_device(
    review_cols,
    cust_state,
    prod_state,
    w_qkv,
    w_out,
    w_msg,
    w_cust_up,
    w_prod_up,
    w_back,
    cust_slot,
    prod_slot,
    prod_pos,
    live_count,
):
    review_rows = review_cols.shape[0]
    rev_size = lax.axis_size("rev")
    cust_size = lax.axis_size("cust")
    prod_size = lax.axis_size("prod")
    cust_owners = rev_size * cust_size
    cust_slots = review_rows // cust_owners
    prod_owners = cust_size * prod_size
    prod_slots = review_rows // prod_owners
    cust_rows = cust_state.shape[0]
    prod_rows = prod_state.shape[0]
    own_rows = prod_rows // rev_size

    filled = jnp.arange(cust_slots, dtype=jnp.int32)[None, :] < live_count.reshape(cust_owners, 1)
    live = filled.reshape(review_rows)
    cust_ids = jnp.where(filled, cust_slot.reshape(cust_owners, cust_slots), -1)
    position = prod_pos.reshape(review_rows)
    id_plus = jnp.where(live, prod_slot + 1, 0)
    id_lane = jnp.arange(LANES, dtype=jnp.int32)[None, :]
    id_cols = jnp.where(
        id_lane == 0, (id_plus // 32)[:, None], jnp.where(id_lane == 1, (id_plus % 32)[:, None], 0)
    ).astype(bf16)
    review_h, to_cust, prod_msgs, sorted_ids = encode(review_cols, w_qkv, w_out, w_msg, position, id_cols)
    prod_ids = (sorted_ids[:, 0] * 32.0 + sorted_ids[:, 1]).astype(jnp.int32) - 1

    cust_run = cust_size * cust_slots
    stage_rows = rev_size * cust_slots
    prod_got, prod_got_ids, sent1, ids1 = exchange(
        [
            (("cust", "prod"), [prod_msgs.reshape(prod_owners, prod_slots, H),
                                prod_ids.reshape(prod_owners, 1, prod_slots)]),
            (("rev",), [to_cust.reshape(rev_size, cust_run, H), cust_ids.reshape(rev_size, 1, cust_run)]),
        ],
        0,
    )
    stage2, prod_pack = route_step(
        sent1.reshape(review_rows, H), prod_got.reshape(review_rows, H), prod_got_ids, rev_size, cust_slots, prod_rows
    )
    ids2 = ids1.reshape(rev_size, cust_size, cust_slots).transpose(1, 0, 2)
    got_rows, got_ids, spread = exchange(
        [
            (("cust",), [stage2.reshape(cust_size, stage_rows, H), ids2.reshape(cust_size, 1, stage_rows)]),
            (("rev",), [prod_pack.reshape(rev_size, own_rows, H + LANES)]),
        ],
        1,
    )
    cust_pack, own_new = gather_step(
        got_ids, got_rows.reshape(review_rows, H), spread, prod_state, w_prod_up, cust_rows
    )

    cust_both, new_prod = exchange(
        [
            (("prod",), [cust_pack[None]]),
            (("rev",), [own_new[None]]),
        ],
        2,
    )
    new_prod = new_prod.reshape(prod_rows, H)
    shape = (cust_slots, cust_size, stage_rows, cust_run)
    new_cust, reply, prod_reply = reply_step(
        cust_both, cust_state, w_cust_up, got_ids, shape, new_prod, prod_got_ids
    )
    ret_sorted, back1 = exchange(
        [
            (("cust", "prod"), [prod_reply.reshape(prod_owners, prod_slots, H)]),
            (("rev",), [reply.reshape(rev_size, cust_run, H)]),
        ],
        3,
    )
    back2 = back1.reshape(rev_size, cust_size, cust_slots, H).transpose(1, 0, 2, 3)
    (ret_cust,) = exchange([(("cust",), [back2.reshape(cust_size, stage_rows, H)])], 4)
    review_out = tail(
        review_h, ret_cust.reshape(review_rows, H), shape, ret_sorted.reshape(review_rows, H), position, w_back
    )
    return (review_out, new_cust, new_prod)


def solution(mesh):
    in_specs = (
        P(("rev", "cust", "prod"), None),
        P(("rev", "cust"), None),
        P(("cust", "prod"), None),
        P(),
        P(),
        P(),
        P(),
        P(),
        P(),
        P(("rev", "cust", "prod")),
        P(("rev", "cust", "prod")),
        P(("rev", "cust", "prod"), None),
        P(("rev", "cust", "prod"), None),
    )
    out_specs = (
        P(("rev", "cust", "prod"), None),
        P(("rev", "cust"), None),
        P(("cust", "prod"), None),
    )
    return jax.shard_map(
        on_device, mesh=mesh, in_specs=in_specs, out_specs=out_specs, check_vma=False
    )
```

```python
import math

import jax
import jax.numpy as jnp
from jax import lax
import functools

import numpy as np
from jax.experimental import pallas as pl
from jax.experimental.pallas import tpu as pltpu
from jax.sharding import PartitionSpec as P

H = 512
HEADS = 8
NCOL = 4
HD = 64
LANES = 128
f32 = jnp.float32
bf16 = jnp.bfloat16


def rms_norm(vector):
    return vector * lax.rsqrt(jnp.mean(vector * vector, axis=-1, keepdims=True) + 1e-06)


def encode_kernel(x_ref, wqkv_ref, wout_ref, wmsg_ref, pos_ref, idc_ref, h_ref, cust_ref, prod_ref, ids_ref):
    head = lax.broadcasted_iota(jnp.int32, (H, LANES), 0) // HD
    lane = lax.broadcasted_iota(jnp.int32, (H, LANES), 1)
    e = [(lane == i * HEADS + head).astype(bf16) for i in range(NCOL)]
    head_t = lax.broadcasted_iota(jnp.int32, (LANES, H), 1) // HD
    lane_t = lax.broadcasted_iota(jnp.int32, (LANES, H), 0)
    et = [(lane_t == i * HEADS + head_t).astype(bf16) for i in range(NCOL)]
    xs = [x_ref[:, i * H:(i + 1) * H] for i in range(NCOL)]
    q, k, v = [], [], []
    for i in range(NCOL):
        qkv = jnp.dot(xs[i], wqkv_ref[...], preferred_element_type=f32).astype(bf16)
        q.append(qkv[:, :H].astype(f32))
        k.append(qkv[:, H:2 * H].astype(f32))
        v.append(qkv[:, 2 * H:].astype(f32))
    scores = []
    for j in range(NCOL):
        s = None
        for i in range(NCOL):
            term = jnp.dot((q[i] * k[j]).astype(bf16), e[i], preferred_element_type=f32)
            s = term if s is None else s + term
        scores.append(s * (1.0 / math.sqrt(HD)))
    top = jnp.maximum(jnp.maximum(scores[0], scores[1]), jnp.maximum(scores[2], scores[3]))
    expon = [jnp.exp(s - top) for s in scores]
    total = (expon[0] + expon[1]) + (expon[2] + expon[3])
    weights = [(x / total).astype(bf16) for x in expon]
    pooled = None
    for i in range(NCOL):
        att = None
        for j in range(NCOL):
            term = jnp.dot(weights[j], et[i], preferred_element_type=f32) * v[j]
            att = term if att is None else att + term
        mixed = xs[i].astype(f32) + jnp.dot(att.astype(bf16), wout_ref[...], preferred_element_type=f32)
        pooled = mixed if pooled is None else pooled + mixed
    pooled = pooled * (1.0 / NCOL)
    h = rms_norm(pooled).astype(bf16)
    h_ref[...] = h
    msg = jnp.dot(h, wmsg_ref[...], preferred_element_type=f32).astype(bf16)
    cust_ref[...] = msg[:, :H]
    rows = pos_ref.shape[1]
    perm = (lax.broadcasted_iota(jnp.int32, (rows, rows), 0) == pos_ref[...]).astype(bf16)
    prod_ref[...] = jnp.dot(perm, msg[:, H:], preferred_element_type=f32).astype(bf16)
    ids_ref[...] = jnp.dot(perm, idc_ref[...], preferred_element_type=f32)


def encode(cols, w_qkv, w_out, w_msg, position, id_cols):
    rows = cols.shape[0]
    vmem = pl.BlockSpec(memory_space=pltpu.VMEM)
    return pl.pallas_call(
        encode_kernel,
        in_specs=[vmem] * 6,
        out_specs=[vmem] * 4,
        out_shape=[
            jax.ShapeDtypeStruct((rows, H), bf16),
            jax.ShapeDtypeStruct((rows, H), bf16),
            jax.ShapeDtypeStruct((rows, H), bf16),
            jax.ShapeDtypeStruct((rows, LANES), f32),
        ],
    )(cols, w_qkv, w_out, w_msg, position.reshape(1, rows), id_cols)

MESH = pl.DeviceIdType.MESH


def _coords(axes, sizes, t):
    out = {}
    for name, size in reversed(list(zip(axes, sizes))):
        out[name] = t % size
        t = t // size
    return out


def _step(o):
    return ((o + 1) // 2) * (2 * (o % 2) - 1)


def exchange_kernel(plan, *refs):
    total = sum(c for _, _, c in plan)
    ins, outs = refs[:total], refs[total:2 * total]
    sems = refs[2 * total:]
    groups = []
    at, s_at = 0, 0
    for axes, sizes, count in plan:
        n = int(np.prod(sizes))
        me = 0
        for name, size in zip(axes, sizes):
            me = me * size + lax.axis_index(name)
        groups.append(dict(axes=axes, sizes=sizes, n=n, me=me, ins=ins[at:at + count], outs=outs[at:at + count],
                           send=sems[s_at], recv=sems[s_at + 1], local=sems[s_at + 2]))
        at += count
        s_at += 3

    barrier = pltpu.get_barrier_semaphore()
    expected = 0
    for g in groups:
        n, me = g["n"], g["me"]
        def greet(o, carry, g=g, n=n, me=me):
            t = lax.rem(me + o, n)
            pl.semaphore_signal(barrier, inc=1, device_id=_coords(g["axes"], g["sizes"], t), device_id_type=MESH)
            return carry
        lax.fori_loop(1, n, greet, 0)
        expected += n - 1
    pl.semaphore_wait(barrier, expected)

    def remote(g, a, src, dst, t):
        if g["ins"][a].shape[0] == 1:
            src = 0
        return pltpu.make_async_remote_copy(
            src_ref=g["ins"][a].at[src], dst_ref=g["outs"][a].at[dst],
            send_sem=g["send"].at[a, src], recv_sem=g["recv"].at[a, dst],
            device_id=_coords(g["axes"], g["sizes"], t), device_id_type=MESH)

    def own(g, a):
        src = 0 if g["ins"][a].shape[0] == 1 else g["me"]
        return pltpu.make_async_copy(g["ins"][a].at[src], g["outs"][a].at[g["me"]], g["local"].at[a])

    for g in groups:
        for a in range(len(g["ins"])):
            own(g, a).start()
    for g in groups:
        n, me = g["n"], g["me"]
        def start(o, carry, g=g, n=n, me=me):
            t = lax.rem(me + _step(o) + n, n)
            for a in range(len(g["ins"])):
                remote(g, a, t, me, t).start()
            return carry
        lax.fori_loop(1, n, start, 0)
    for g in groups:
        n, me = g["n"], g["me"]
        def finish(o, carry, g=g, n=n, me=me):
            t = lax.rem(me + _step(o) + n, n)
            s = lax.rem(me - _step(o) + n, n)
            for a in range(len(g["ins"])):
                remote(g, a, t, me, t).wait_send()
                remote(g, a, me, s, s).wait_recv()
            return carry
        lax.fori_loop(1, n, finish, 0)
        for a in range(len(g["ins"])):
            own(g, a).wait()


def exchange(groups, collective_id):
    plan, arrays, scratch, n_of = [], [], [], []
    for axes, arrs in groups:
        axes = tuple(axes)
        sizes = tuple(lax.axis_size(a) for a in axes)
        n = int(np.prod(sizes))
        plan.append((axes, sizes, len(arrs)))
        arrays.extend(arrs)
        n_of.extend([n] * len(arrs))
        scratch += [pltpu.SemaphoreType.DMA((len(arrs), n)), pltpu.SemaphoreType.DMA((len(arrs), n)),
                    pltpu.SemaphoreType.DMA((len(arrs),))]
    vmem = pl.BlockSpec(memory_space=pltpu.VMEM)
    return pl.pallas_call(
        functools.partial(exchange_kernel, tuple(plan)),
        out_shape=[jax.ShapeDtypeStruct((n_of[i],) + a.shape[1:], a.dtype) for i, a in enumerate(arrays)],
        in_specs=[vmem] * len(arrays),
        out_specs=[vmem] * len(arrays),
        scratch_shapes=scratch,
        compiler_params=pltpu.CompilerParams(has_side_effects=True, collective_id=collective_id),
    )(*arrays)


def tail_kernel(shape, h_ref, cust_ref, sorted_ref, pos_ref, wback_ref, out_ref):
    rows = h_ref.shape[0]
    ret_cust = jnp.dot(order_matrix(rows, *shape), cust_ref[...], preferred_element_type=f32).astype(bf16)
    unperm = (column_of(pos_ref) == lax.broadcasted_iota(jnp.int32, (rows, rows), 1)).astype(bf16)
    ret_prod = jnp.dot(unperm, sorted_ref[...], preferred_element_type=f32).astype(bf16)
    back = jnp.dot(ret_cust, wback_ref[:H, :], preferred_element_type=f32) + jnp.dot(
        ret_prod, wback_ref[H:, :], preferred_element_type=f32
    )
    out_ref[...] = rms_norm(h_ref[...].astype(f32) + back).astype(bf16)


def tail(review_h, cust_rows, shape, sorted_rows, position, w_back):
    vmem = pl.BlockSpec(memory_space=pltpu.VMEM)
    return pl.pallas_call(
        functools.partial(tail_kernel, shape),
        out_shape=jax.ShapeDtypeStruct(review_h.shape, bf16),
        in_specs=[vmem] * 5,
        out_specs=vmem,
    )(review_h, cust_rows, sorted_rows, position.reshape(1, -1), w_back)


def order_matrix(rows, cust_slots, cust_size, stage_rows, cust_run):
    s = lax.broadcasted_iota(jnp.int32, (rows, rows), 0)
    src = ((s // cust_slots) % cust_size) * stage_rows + (s // cust_run) * cust_slots + s % cust_slots
    return (src == lax.broadcasted_iota(jnp.int32, (rows, rows), 1)).astype(bf16)


def route_kernel(rev_size, cust_slots, sent_ref, pgot_ref, pids_ref, stage_ref, pack_ref):
    rows = sent_ref.shape[0]
    s = lax.broadcasted_iota(jnp.int32, (rows, rows), 0)
    stage_rows = rev_size * cust_slots
    cust_run = rows // rev_size
    src = (s % stage_rows) // cust_slots * cust_run + (s // stage_rows) * cust_slots + s % cust_slots
    move = (src == lax.broadcasted_iota(jnp.int32, (rows, rows), 1)).astype(bf16)
    stage_ref[...] = jnp.dot(move, sent_ref[...], preferred_element_type=f32).astype(bf16)
    prows = pack_ref.shape[0]
    pick = (lax.broadcasted_iota(jnp.int32, (prows, pids_ref.shape[1]), 0) == pids_ref[...]).astype(bf16)
    pack_ref[:, :H] = jnp.dot(pick, pgot_ref[...], preferred_element_type=f32).astype(bf16)
    cnt = jnp.sum(pick.astype(f32), axis=1, keepdims=True)
    hi = jnp.floor(cnt * (1.0 / 64.0))
    lo = cnt - 64.0 * hi
    lane = lax.broadcasted_iota(jnp.int32, (prows, LANES), 1)
    pack_ref[:, H:] = jnp.where(lane == 0, hi, jnp.where(lane == 1, lo, 0.0)).astype(bf16)


def route_step(sent1, prod_got, prod_got_ids, rev_size, cust_slots, prod_rows):
    rows = sent1.shape[0]
    vmem = pl.BlockSpec(memory_space=pltpu.VMEM)
    return pl.pallas_call(
        functools.partial(route_kernel, rev_size, cust_slots),
        in_specs=[vmem] * 3,
        out_specs=[vmem] * 2,
        out_shape=[
            jax.ShapeDtypeStruct((rows, H), bf16),
            jax.ShapeDtypeStruct((prod_rows, H + LANES), bf16),
        ],
    )(sent1, prod_got, prod_got_ids.reshape(1, -1))


def refresh_rows(sums, counts, states, weight):
    normed = (sums / jnp.sqrt(jnp.maximum(counts, 1.0))).astype(bf16)
    update = jax.nn.silu(jnp.dot(normed, weight, preferred_element_type=f32))
    return rms_norm(states.astype(f32) + update).astype(bf16)


def column_of(row_ref):
    return jnp.transpose(jnp.broadcast_to(row_ref[...], (8, row_ref.shape[1])))[:, 0:1]


def gather_kernel(rev_axis, gids_ref, grows_ref, spread_ref, pstate_ref, wpu_ref, pack_ref, pnew_ref):
    rows = pack_ref.shape[0]
    pick = (lax.broadcasted_iota(jnp.int32, (rows, gids_ref.shape[1]), 0) == gids_ref[...]).astype(bf16)
    pack_ref[:, :H] = jnp.dot(pick, grows_ref[...], preferred_element_type=f32)
    cnt = jnp.sum(pick.astype(f32), axis=1, keepdims=True)
    pack_ref[:, H:] = jnp.broadcast_to(cnt, (rows, LANES))
    whole = spread_ref[0].astype(f32)
    for i in range(1, spread_ref.shape[0]):
        whole = whole + spread_ref[i].astype(f32)
    own = pnew_ref.shape[0]
    counts = whole[:, H:H + 1] * 64.0 + whole[:, H + 1:H + 2]
    start = pl.multiple_of(lax.axis_index(rev_axis) * own, own)
    pnew_ref[...] = refresh_rows(whole[:, :H], counts, pstate_ref[pl.ds(start, own), :], wpu_ref[...])


def gather_step(got_ids, got_rows, spread, prod_state, w_prod_up, cust_rows):
    own = prod_state.shape[0] // spread.shape[0]
    vmem = pl.BlockSpec(memory_space=pltpu.VMEM)
    return pl.pallas_call(
        functools.partial(gather_kernel, "rev"),
        in_specs=[vmem] * 5,
        out_specs=[vmem] * 2,
        out_shape=[
            jax.ShapeDtypeStruct((cust_rows, H + LANES), f32),
            jax.ShapeDtypeStruct((own, H), bf16),
        ],
    )(got_ids.reshape(1, -1), got_rows, spread, prod_state, w_prod_up)


def reply_kernel(shape, both_ref, cstate_ref, wcu_ref, gids_ref, newprod_ref, pids_ref, newcust_ref, creply_ref, preply_ref):
    tot = both_ref[0] + both_ref[1]
    new_cust = refresh_rows(tot[:, :H], tot[:, H:H + 1], cstate_ref[...], wcu_ref[...])
    newcust_ref[...] = new_cust
    n = gids_ref.shape[1]
    pick_t = (column_of(gids_ref) == lax.broadcasted_iota(jnp.int32, (n, new_cust.shape[0]), 1)).astype(bf16)
    reply = jnp.dot(pick_t, new_cust, preferred_element_type=f32).astype(bf16)
    creply_ref[...] = jnp.dot(order_matrix(n, *shape), reply, preferred_element_type=f32).astype(bf16)
    m = pids_ref.shape[1]
    ppick_t = (column_of(pids_ref) == lax.broadcasted_iota(jnp.int32, (m, newprod_ref.shape[0]), 1)).astype(bf16)
    preply_ref[...] = jnp.dot(ppick_t, newprod_ref[...], preferred_element_type=f32).astype(bf16)


def reply_step(cust_both, cust_state, w_cust_up, got_ids, shape, new_prod, prod_got_ids):
    vmem = pl.BlockSpec(memory_space=pltpu.VMEM)
    n = got_ids.size
    return pl.pallas_call(
        functools.partial(reply_kernel, shape),
        in_specs=[vmem] * 6,
        out_specs=[vmem] * 3,
        out_shape=[
            jax.ShapeDtypeStruct(cust_state.shape, bf16),
            jax.ShapeDtypeStruct((n, H), bf16),
            jax.ShapeDtypeStruct((prod_got_ids.size, H), bf16),
        ],
    )(cust_both, cust_state, w_cust_up, got_ids.reshape(1, -1), new_prod, prod_got_ids.reshape(1, -1))


def refresh(totals, counts, states, weight):
    normed_sum = (totals / jnp.sqrt(jnp.maximum(counts, 1.0))[:, None]).astype(bf16)
    update = jax.nn.silu(jnp.dot(normed_sum, weight, preferred_element_type=f32))
    return rms_norm(states.astype(f32) + update).astype(bf16)


def pick_back(picker, states):
    return lax.dot_general(
        picker, states, (((0,), (0,)), ((), ())), preferred_element_type=f32
    ).astype(bf16)


def one_hot_rows(ids, rows):
    return (ids.reshape(1, -1) == jnp.arange(rows, dtype=jnp.int32)[:, None]).astype(bf16)


def on_device(
    review_cols,
    cust_state,
    prod_state,
    w_qkv,
    w_out,
    w_msg,
    w_cust_up,
    w_prod_up,
    w_back,
    cust_slot,
    prod_slot,
    prod_pos,
    live_count,
):
    review_rows = review_cols.shape[0]
    rev_size = lax.axis_size("rev")
    cust_size = lax.axis_size("cust")
    prod_size = lax.axis_size("prod")
    cust_owners = rev_size * cust_size
    cust_slots = review_rows // cust_owners
    prod_owners = cust_size * prod_size
    prod_slots = review_rows // prod_owners
    cust_rows = cust_state.shape[0]
    prod_rows = prod_state.shape[0]
    own_rows = prod_rows // rev_size

    filled = jnp.arange(cust_slots, dtype=jnp.int32)[None, :] < live_count.reshape(cust_owners, 1)
    live = filled.reshape(review_rows)
    cust_ids = jnp.where(filled, cust_slot.reshape(cust_owners, cust_slots), -1)
    position = prod_pos.reshape(review_rows)
    id_plus = jnp.where(live, prod_slot + 1, 0)
    id_lane = jnp.arange(LANES, dtype=jnp.int32)[None, :]
    id_cols = jnp.where(
        id_lane == 0, (id_plus // 32)[:, None], jnp.where(id_lane == 1, (id_plus % 32)[:, None], 0)
    ).astype(bf16)
    review_h, to_cust, prod_msgs, sorted_ids = encode(review_cols, w_qkv, w_out, w_msg, position, id_cols)
    prod_ids = (sorted_ids[:, 0] * 32.0 + sorted_ids[:, 1]).astype(jnp.int32) - 1

    cust_run = cust_size * cust_slots
    stage_rows = rev_size * cust_slots
    prod_got, prod_got_ids, sent1, ids1 = exchange(
        [
            (("cust", "prod"), [prod_msgs.reshape(prod_owners, prod_slots, H),
                                prod_ids.reshape(prod_owners, 1, prod_slots)]),
            (("rev",), [to_cust.reshape(rev_size, cust_run, H), cust_ids.reshape(rev_size, 1, cust_run)]),
        ],
        0,
    )
    stage2, prod_pack = route_step(
        sent1.reshape(review_rows, H), prod_got.reshape(review_rows, H), prod_got_ids, rev_size, cust_slots, prod_rows
    )
    ids2 = ids1.reshape(rev_size, cust_size, cust_slots).transpose(1, 0, 2)
    got_rows, got_ids, spread = exchange(
        [
            (("cust",), [stage2.reshape(cust_size, stage_rows, H), ids2.reshape(cust_size, 1, stage_rows)]),
            (("rev",), [prod_pack.reshape(rev_size, own_rows, H + LANES)]),
        ],
        1,
    )
    cust_pack, own_new = gather_step(
        got_ids, got_rows.reshape(review_rows, H), spread, prod_state, w_prod_up, cust_rows
    )

    new_prod, cust_both = exchange(
        [
            (("rev",), [own_new[None]]),
            (("prod",), [cust_pack[None]]),
        ],
        2,
    )
    new_prod = new_prod.reshape(prod_rows, H)
    shape = (cust_slots, cust_size, stage_rows, cust_run)
    new_cust, reply, prod_reply = reply_step(
        cust_both, cust_state, w_cust_up, got_ids, shape, new_prod, prod_got_ids
    )
    ret_sorted, back1 = exchange(
        [
            (("cust", "prod"), [prod_reply.reshape(prod_owners, prod_slots, H)]),
            (("rev",), [reply.reshape(rev_size, cust_run, H)]),
        ],
        3,
    )
    back2 = back1.reshape(rev_size, cust_size, cust_slots, H).transpose(1, 0, 2, 3)
    (ret_cust,) = exchange([(("cust",), [back2.reshape(cust_size, stage_rows, H)])], 4)
    review_out = tail(
        review_h, ret_cust.reshape(review_rows, H), shape, ret_sorted.reshape(review_rows, H), position, w_back
    )
    return (review_out, new_cust, new_prod)


def solution(mesh):
    in_specs = (
        P(("rev", "cust", "prod"), None),
        P(("rev", "cust"), None),
        P(("cust", "prod"), None),
        P(),
        P(),
        P(),
        P(),
        P(),
        P(),
        P(("rev", "cust", "prod")),
        P(("rev", "cust", "prod")),
        P(("rev", "cust", "prod"), None),
        P(("rev", "cust", "prod"), None),
    )
    out_specs = (
        P(("rev", "cust", "prod"), None),
        P(("rev", "cust"), None),
        P(("cust", "prod"), None),
    )
    return jax.shard_map(
        on_device, mesh=mesh, in_specs=in_specs, out_specs=out_specs, check_vma=False
    )
```

```python
import math

import jax
import jax.numpy as jnp
from jax import lax
import functools

import numpy as np
from jax.experimental import pallas as pl
from jax.experimental.pallas import tpu as pltpu
from jax.sharding import PartitionSpec as P

H = 512
HEADS = 8
NCOL = 4
HD = 64
LANES = 128
f32 = jnp.float32
bf16 = jnp.bfloat16


def rms_norm(vector):
    return vector * lax.rsqrt(jnp.mean(vector * vector, axis=-1, keepdims=True) + 1e-06)


def encode_kernel(x_ref, wqkv_ref, wout_ref, wmsg_ref, pos_ref, idc_ref, h_ref, cust_ref, prod_ref, ids_ref):
    head = lax.broadcasted_iota(jnp.int32, (H, LANES), 0) // HD
    lane = lax.broadcasted_iota(jnp.int32, (H, LANES), 1)
    e = [(lane == i * HEADS + head).astype(bf16) for i in range(NCOL)]
    head_t = lax.broadcasted_iota(jnp.int32, (LANES, H), 1) // HD
    lane_t = lax.broadcasted_iota(jnp.int32, (LANES, H), 0)
    et = [(lane_t == i * HEADS + head_t).astype(bf16) for i in range(NCOL)]
    xs = [x_ref[:, i * H:(i + 1) * H] for i in range(NCOL)]
    q, k, v = [], [], []
    for i in range(NCOL):
        qkv = jnp.dot(xs[i], wqkv_ref[...], preferred_element_type=f32).astype(bf16)
        q.append(qkv[:, :H])
        k.append(qkv[:, H:2 * H])
        v.append(qkv[:, 2 * H:].astype(f32))
    scores = []
    for j in range(NCOL):
        s = None
        for i in range(NCOL):
            term = jnp.dot(q[i] * k[j], e[i], preferred_element_type=f32)
            s = term if s is None else s + term
        scores.append(s * (1.0 / math.sqrt(HD)))
    top = jnp.maximum(jnp.maximum(scores[0], scores[1]), jnp.maximum(scores[2], scores[3]))
    expon = [jnp.exp(s - top) for s in scores]
    total = (expon[0] + expon[1]) + (expon[2] + expon[3])
    weights = [(x / total).astype(bf16) for x in expon]
    pooled = None
    for i in range(NCOL):
        att = None
        for j in range(NCOL):
            term = jnp.dot(weights[j], et[i], preferred_element_type=f32) * v[j]
            att = term if att is None else att + term
        mixed = xs[i].astype(f32) + jnp.dot(att.astype(bf16), wout_ref[...], preferred_element_type=f32)
        pooled = mixed if pooled is None else pooled + mixed
    pooled = pooled * (1.0 / NCOL)
    h = rms_norm(pooled).astype(bf16)
    h_ref[...] = h
    msg = jnp.dot(h, wmsg_ref[...], preferred_element_type=f32).astype(bf16)
    cust_ref[...] = msg[:, :H]
    rows = pos_ref.shape[1]
    perm = (lax.broadcasted_iota(jnp.int32, (rows, rows), 0) == pos_ref[...]).astype(bf16)
    prod_ref[...] = jnp.dot(perm, msg[:, H:], preferred_element_type=f32).astype(bf16)
    ids_ref[...] = jnp.dot(perm, idc_ref[...], preferred_element_type=f32)


def encode(cols, w_qkv, w_out, w_msg, position, id_cols):
    rows = cols.shape[0]
    vmem = pl.BlockSpec(memory_space=pltpu.VMEM)
    return pl.pallas_call(
        encode_kernel,
        in_specs=[vmem] * 6,
        out_specs=[vmem] * 4,
        out_shape=[
            jax.ShapeDtypeStruct((rows, H), bf16),
            jax.ShapeDtypeStruct((rows, H), bf16),
            jax.ShapeDtypeStruct((rows, H), bf16),
            jax.ShapeDtypeStruct((rows, LANES), f32),
        ],
    )(cols, w_qkv, w_out, w_msg, position.reshape(1, rows), id_cols)

MESH = pl.DeviceIdType.MESH


def _coords(axes, sizes, t):
    out = {}
    for name, size in reversed(list(zip(axes, sizes))):
        out[name] = t % size
        t = t // size
    return out


def _step(o):
    return ((o + 1) // 2) * (2 * (o % 2) - 1)


def exchange_kernel(plan, *refs):
    total = sum(c for _, _, c in plan)
    ins, outs = refs[:total], refs[total:2 * total]
    sems = refs[2 * total:]
    groups = []
    at, s_at = 0, 0
    for axes, sizes, count in plan:
        n = int(np.prod(sizes))
        me = 0
        for name, size in zip(axes, sizes):
            me = me * size + lax.axis_index(name)
        groups.append(dict(axes=axes, sizes=sizes, n=n, me=me, ins=ins[at:at + count], outs=outs[at:at + count],
                           send=sems[s_at], recv=sems[s_at + 1], local=sems[s_at + 2]))
        at += count
        s_at += 3

    barrier = pltpu.get_barrier_semaphore()
    expected = 0
    for g in groups:
        n, me = g["n"], g["me"]
        def greet(o, carry, g=g, n=n, me=me):
            t = lax.rem(me + o, n)
            pl.semaphore_signal(barrier, inc=1, device_id=_coords(g["axes"], g["sizes"], t), device_id_type=MESH)
            return carry
        lax.fori_loop(1, n, greet, 0)
        expected += n - 1
    pl.semaphore_wait(barrier, expected)

    def remote(g, a, src, dst, t):
        if g["ins"][a].shape[0] == 1:
            src = 0
        return pltpu.make_async_remote_copy(
            src_ref=g["ins"][a].at[src], dst_ref=g["outs"][a].at[dst],
            send_sem=g["send"].at[a, src], recv_sem=g["recv"].at[a, dst],
            device_id=_coords(g["axes"], g["sizes"], t), device_id_type=MESH)

    def own(g, a):
        src = 0 if g["ins"][a].shape[0] == 1 else g["me"]
        return pltpu.make_async_copy(g["ins"][a].at[src], g["outs"][a].at[g["me"]], g["local"].at[a])

    for g in groups:
        for a in range(len(g["ins"])):
            own(g, a).start()
    for g in groups:
        n, me = g["n"], g["me"]
        def start(o, carry, g=g, n=n, me=me):
            t = lax.rem(me + _step(o) + n, n)
            for a in range(len(g["ins"])):
                remote(g, a, t, me, t).start()
            return carry
        lax.fori_loop(1, n, start, 0)
    for g in groups:
        n, me = g["n"], g["me"]
        def finish(o, carry, g=g, n=n, me=me):
            t = lax.rem(me + _step(o) + n, n)
            s = lax.rem(me - _step(o) + n, n)
            for a in range(len(g["ins"])):
                remote(g, a, t, me, t).wait_send()
                remote(g, a, me, s, s).wait_recv()
            return carry
        lax.fori_loop(1, n, finish, 0)
        for a in range(len(g["ins"])):
            own(g, a).wait()


def exchange(groups, collective_id):
    plan, arrays, scratch, n_of = [], [], [], []
    for axes, arrs in groups:
        axes = tuple(axes)
        sizes = tuple(lax.axis_size(a) for a in axes)
        n = int(np.prod(sizes))
        plan.append((axes, sizes, len(arrs)))
        arrays.extend(arrs)
        n_of.extend([n] * len(arrs))
        scratch += [pltpu.SemaphoreType.DMA((len(arrs), n)), pltpu.SemaphoreType.DMA((len(arrs), n)),
                    pltpu.SemaphoreType.DMA((len(arrs),))]
    vmem = pl.BlockSpec(memory_space=pltpu.VMEM)
    return pl.pallas_call(
        functools.partial(exchange_kernel, tuple(plan)),
        out_shape=[jax.ShapeDtypeStruct((n_of[i],) + a.shape[1:], a.dtype) for i, a in enumerate(arrays)],
        in_specs=[vmem] * len(arrays),
        out_specs=[vmem] * len(arrays),
        scratch_shapes=scratch,
        compiler_params=pltpu.CompilerParams(has_side_effects=True, collective_id=collective_id),
    )(*arrays)


def tail_kernel(shape, h_ref, cust_ref, sorted_ref, pos_ref, wback_ref, out_ref):
    rows = h_ref.shape[0]
    ret_cust = jnp.dot(order_matrix(rows, *shape), cust_ref[...], preferred_element_type=f32).astype(bf16)
    unperm = (column_of(pos_ref) == lax.broadcasted_iota(jnp.int32, (rows, rows), 1)).astype(bf16)
    ret_prod = jnp.dot(unperm, sorted_ref[...], preferred_element_type=f32).astype(bf16)
    back = jnp.dot(ret_cust, wback_ref[:H, :], preferred_element_type=f32) + jnp.dot(
        ret_prod, wback_ref[H:, :], preferred_element_type=f32
    )
    out_ref[...] = rms_norm(h_ref[...].astype(f32) + back).astype(bf16)


def tail(review_h, cust_rows, shape, sorted_rows, position, w_back):
    vmem = pl.BlockSpec(memory_space=pltpu.VMEM)
    return pl.pallas_call(
        functools.partial(tail_kernel, shape),
        out_shape=jax.ShapeDtypeStruct(review_h.shape, bf16),
        in_specs=[vmem] * 5,
        out_specs=vmem,
    )(review_h, cust_rows, sorted_rows, position.reshape(1, -1), w_back)


def order_matrix(rows, cust_slots, cust_size, stage_rows, cust_run):
    s = lax.broadcasted_iota(jnp.int32, (rows, rows), 0)
    src = ((s // cust_slots) % cust_size) * stage_rows + (s // cust_run) * cust_slots + s % cust_slots
    return (src == lax.broadcasted_iota(jnp.int32, (rows, rows), 1)).astype(bf16)


def route_kernel(rev_size, cust_slots, sent_ref, pgot_ref, pids_ref, stage_ref, pack_ref):
    rows = sent_ref.shape[0]
    s = lax.broadcasted_iota(jnp.int32, (rows, rows), 0)
    stage_rows = rev_size * cust_slots
    cust_run = rows // rev_size
    src = (s % stage_rows) // cust_slots * cust_run + (s // stage_rows) * cust_slots + s % cust_slots
    move = (src == lax.broadcasted_iota(jnp.int32, (rows, rows), 1)).astype(bf16)
    stage_ref[...] = jnp.dot(move, sent_ref[...], preferred_element_type=f32).astype(bf16)
    prows = pack_ref.shape[0]
    pick = (lax.broadcasted_iota(jnp.int32, (prows, pids_ref.shape[1]), 0) == pids_ref[...]).astype(bf16)
    pack_ref[:, :H] = jnp.dot(pick, pgot_ref[...], preferred_element_type=f32).astype(bf16)
    cnt = jnp.sum(pick.astype(f32), axis=1, keepdims=True)
    hi = jnp.floor(cnt * (1.0 / 64.0))
    lo = cnt - 64.0 * hi
    lane = lax.broadcasted_iota(jnp.int32, (prows, LANES), 1)
    pack_ref[:, H:] = jnp.where(lane == 0, hi, jnp.where(lane == 1, lo, 0.0)).astype(bf16)


def route_step(sent1, prod_got, prod_got_ids, rev_size, cust_slots, prod_rows):
    rows = sent1.shape[0]
    vmem = pl.BlockSpec(memory_space=pltpu.VMEM)
    return pl.pallas_call(
        functools.partial(route_kernel, rev_size, cust_slots),
        in_specs=[vmem] * 3,
        out_specs=[vmem] * 2,
        out_shape=[
            jax.ShapeDtypeStruct((rows, H), bf16),
            jax.ShapeDtypeStruct((prod_rows, H + LANES), bf16),
        ],
    )(sent1, prod_got, prod_got_ids.reshape(1, -1))


def refresh_rows(sums, counts, states, weight):
    normed = (sums / jnp.sqrt(jnp.maximum(counts, 1.0))).astype(bf16)
    update = jax.nn.silu(jnp.dot(normed, weight, preferred_element_type=f32))
    return rms_norm(states.astype(f32) + update).astype(bf16)


def column_of(row_ref):
    return jnp.transpose(jnp.broadcast_to(row_ref[...], (8, row_ref.shape[1])))[:, 0:1]


def gather_kernel(rev_axis, gids_ref, grows_ref, spread_ref, pstate_ref, wpu_ref, pack_ref, pnew_ref):
    rows = pack_ref.shape[0]
    pick = (lax.broadcasted_iota(jnp.int32, (rows, gids_ref.shape[1]), 0) == gids_ref[...]).astype(bf16)
    pack_ref[:, :H] = jnp.dot(pick, grows_ref[...], preferred_element_type=f32)
    cnt = jnp.sum(pick.astype(f32), axis=1, keepdims=True)
    pack_ref[:, H:] = jnp.broadcast_to(cnt, (rows, LANES))
    whole = spread_ref[0].astype(f32)
    for i in range(1, spread_ref.shape[0]):
        whole = whole + spread_ref[i].astype(f32)
    own = pnew_ref.shape[0]
    counts = whole[:, H:H + 1] * 64.0 + whole[:, H + 1:H + 2]
    start = pl.multiple_of(lax.axis_index(rev_axis) * own, own)
    pnew_ref[...] = refresh_rows(whole[:, :H], counts, pstate_ref[pl.ds(start, own), :], wpu_ref[...])


def gather_step(got_ids, got_rows, spread, prod_state, w_prod_up, cust_rows):
    own = prod_state.shape[0] // spread.shape[0]
    vmem = pl.BlockSpec(memory_space=pltpu.VMEM)
    return pl.pallas_call(
        functools.partial(gather_kernel, "rev"),
        in_specs=[vmem] * 5,
        out_specs=[vmem] * 2,
        out_shape=[
            jax.ShapeDtypeStruct((cust_rows, H + LANES), f32),
            jax.ShapeDtypeStruct((own, H), bf16),
        ],
    )(got_ids.reshape(1, -1), got_rows, spread, prod_state, w_prod_up)


def reply_kernel(shape, both_ref, cstate_ref, wcu_ref, gids_ref, newprod_ref, pids_ref, newcust_ref, creply_ref, preply_ref):
    tot = both_ref[0] + both_ref[1]
    new_cust = refresh_rows(tot[:, :H], tot[:, H:H + 1], cstate_ref[...], wcu_ref[...])
    newcust_ref[...] = new_cust
    n = gids_ref.shape[1]
    pick_t = (column_of(gids_ref) == lax.broadcasted_iota(jnp.int32, (n, new_cust.shape[0]), 1)).astype(bf16)
    reply = jnp.dot(pick_t, new_cust, preferred_element_type=f32).astype(bf16)
    creply_ref[...] = jnp.dot(order_matrix(n, *shape), reply, preferred_element_type=f32).astype(bf16)
    m = pids_ref.shape[1]
    ppick_t = (column_of(pids_ref) == lax.broadcasted_iota(jnp.int32, (m, newprod_ref.shape[0]), 1)).astype(bf16)
    preply_ref[...] = jnp.dot(ppick_t, newprod_ref[...], preferred_element_type=f32).astype(bf16)


def reply_step(cust_both, cust_state, w_cust_up, got_ids, shape, new_prod, prod_got_ids):
    vmem = pl.BlockSpec(memory_space=pltpu.VMEM)
    n = got_ids.size
    return pl.pallas_call(
        functools.partial(reply_kernel, shape),
        in_specs=[vmem] * 6,
        out_specs=[vmem] * 3,
        out_shape=[
            jax.ShapeDtypeStruct(cust_state.shape, bf16),
            jax.ShapeDtypeStruct((n, H), bf16),
            jax.ShapeDtypeStruct((prod_got_ids.size, H), bf16),
        ],
    )(cust_both, cust_state, w_cust_up, got_ids.reshape(1, -1), new_prod, prod_got_ids.reshape(1, -1))


def refresh(totals, counts, states, weight):
    normed_sum = (totals / jnp.sqrt(jnp.maximum(counts, 1.0))[:, None]).astype(bf16)
    update = jax.nn.silu(jnp.dot(normed_sum, weight, preferred_element_type=f32))
    return rms_norm(states.astype(f32) + update).astype(bf16)


def pick_back(picker, states):
    return lax.dot_general(
        picker, states, (((0,), (0,)), ((), ())), preferred_element_type=f32
    ).astype(bf16)


def one_hot_rows(ids, rows):
    return (ids.reshape(1, -1) == jnp.arange(rows, dtype=jnp.int32)[:, None]).astype(bf16)


def on_device(
    review_cols,
    cust_state,
    prod_state,
    w_qkv,
    w_out,
    w_msg,
    w_cust_up,
    w_prod_up,
    w_back,
    cust_slot,
    prod_slot,
    prod_pos,
    live_count,
):
    review_rows = review_cols.shape[0]
    rev_size = lax.axis_size("rev")
    cust_size = lax.axis_size("cust")
    prod_size = lax.axis_size("prod")
    cust_owners = rev_size * cust_size
    cust_slots = review_rows // cust_owners
    prod_owners = cust_size * prod_size
    prod_slots = review_rows // prod_owners
    cust_rows = cust_state.shape[0]
    prod_rows = prod_state.shape[0]
    own_rows = prod_rows // rev_size

    filled = jnp.arange(cust_slots, dtype=jnp.int32)[None, :] < live_count.reshape(cust_owners, 1)
    live = filled.reshape(review_rows)
    cust_ids = jnp.where(filled, cust_slot.reshape(cust_owners, cust_slots), -1)
    position = prod_pos.reshape(review_rows)
    id_plus = jnp.where(live, prod_slot + 1, 0)
    id_lane = jnp.arange(LANES, dtype=jnp.int32)[None, :]
    id_cols = jnp.where(
        id_lane == 0, (id_plus // 32)[:, None], jnp.where(id_lane == 1, (id_plus % 32)[:, None], 0)
    ).astype(bf16)
    review_h, to_cust, prod_msgs, sorted_ids = encode(review_cols, w_qkv, w_out, w_msg, position, id_cols)
    prod_ids = (sorted_ids[:, 0] * 32.0 + sorted_ids[:, 1]).astype(jnp.int32) - 1

    cust_run = cust_size * cust_slots
    stage_rows = rev_size * cust_slots
    prod_got, prod_got_ids, sent1, ids1 = exchange(
        [
            (("cust", "prod"), [prod_msgs.reshape(prod_owners, prod_slots, H),
                                prod_ids.reshape(prod_owners, 1, prod_slots)]),
            (("rev",), [to_cust.reshape(rev_size, cust_run, H), cust_ids.reshape(rev_size, 1, cust_run)]),
        ],
        0,
    )
    stage2, prod_pack = route_step(
        sent1.reshape(review_rows, H), prod_got.reshape(review_rows, H), prod_got_ids, rev_size, cust_slots, prod_rows
    )
    ids2 = ids1.reshape(rev_size, cust_size, cust_slots).transpose(1, 0, 2)
    got_rows, got_ids, spread = exchange(
        [
            (("cust",), [stage2.reshape(cust_size, stage_rows, H), ids2.reshape(cust_size, 1, stage_rows)]),
            (("rev",), [prod_pack.reshape(rev_size, own_rows, H + LANES)]),
        ],
        1,
    )
    cust_pack, own_new = gather_step(
        got_ids, got_rows.reshape(review_rows, H), spread, prod_state, w_prod_up, cust_rows
    )

    cust_both, new_prod = exchange(
        [
            (("prod",), [cust_pack[None]]),
            (("rev",), [own_new[None]]),
        ],
        2,
    )
    new_prod = new_prod.reshape(prod_rows, H)
    shape = (cust_slots, cust_size, stage_rows, cust_run)
    new_cust, reply, prod_reply = reply_step(
        cust_both, cust_state, w_cust_up, got_ids, shape, new_prod, prod_got_ids
    )
    ret_sorted, back1 = exchange(
        [
            (("cust", "prod"), [prod_reply.reshape(prod_owners, prod_slots, H)]),
            (("rev",), [reply.reshape(rev_size, cust_run, H)]),
        ],
        3,
    )
    back2 = back1.reshape(rev_size, cust_size, cust_slots, H).transpose(1, 0, 2, 3)
    (ret_cust,) = exchange([(("cust",), [back2.reshape(cust_size, stage_rows, H)])], 4)
    review_out = tail(
        review_h, ret_cust.reshape(review_rows, H), shape, ret_sorted.reshape(review_rows, H), position, w_back
    )
    return (review_out, new_cust, new_prod)


def solution(mesh):
    in_specs = (
        P(("rev", "cust", "prod"), None),
        P(("rev", "cust"), None),
        P(("cust", "prod"), None),
        P(),
        P(),
        P(),
        P(),
        P(),
        P(),
        P(("rev", "cust", "prod")),
        P(("rev", "cust", "prod")),
        P(("rev", "cust", "prod"), None),
        P(("rev", "cust", "prod"), None),
    )
    out_specs = (
        P(("rev", "cust", "prod"), None),
        P(("rev", "cust"), None),
        P(("cust", "prod"), None),
    )
    return jax.shard_map(
        on_device, mesh=mesh, in_specs=in_specs, out_specs=out_specs, check_vma=False
    )
```

```python
import math

import jax
import jax.numpy as jnp
from jax import lax
import functools

import numpy as np
from jax.experimental import pallas as pl
from jax.experimental.pallas import tpu as pltpu
from jax.sharding import PartitionSpec as P

H = 512
HEADS = 8
NCOL = 4
HD = 64
LANES = 128
f32 = jnp.float32
bf16 = jnp.bfloat16


def rms_norm(vector):
    return vector * lax.rsqrt(jnp.mean(vector * vector, axis=-1, keepdims=True) + 1e-06)


def encode_kernel(x_ref, wqkv_ref, wout_ref, wmsg_ref, pos_ref, idc_ref, h_ref, cust_ref, prod_ref, ids_ref):
    head = lax.broadcasted_iota(jnp.int32, (H, LANES), 0) // HD
    lane = lax.broadcasted_iota(jnp.int32, (H, LANES), 1)
    e = [(lane == i * HEADS + head).astype(bf16) for i in range(NCOL)]
    head_t = lax.broadcasted_iota(jnp.int32, (LANES, H), 1) // HD
    lane_t = lax.broadcasted_iota(jnp.int32, (LANES, H), 0)
    et = [(lane_t == i * HEADS + head_t).astype(bf16) for i in range(NCOL)]
    xs = [x_ref[:, i * H:(i + 1) * H] for i in range(NCOL)]
    q, k, v = [], [], []
    for i in range(NCOL):
        qkv = jnp.dot(xs[i], wqkv_ref[...], preferred_element_type=f32).astype(bf16)
        q.append(qkv[:, :H])
        k.append(qkv[:, H:2 * H])
        v.append(qkv[:, 2 * H:].astype(f32))
    scores = []
    for j in range(NCOL):
        s = None
        for i in range(NCOL):
            term = jnp.dot(q[i] * k[j], e[i], preferred_element_type=f32)
            s = term if s is None else s + term
        scores.append(s * (1.0 / math.sqrt(HD)))
    top = jnp.maximum(jnp.maximum(scores[0], scores[1]), jnp.maximum(scores[2], scores[3]))
    expon = [jnp.exp(s - top) for s in scores]
    total = (expon[0] + expon[1]) + (expon[2] + expon[3])
    weights = [(x / total).astype(bf16) for x in expon]
    pooled = None
    for i in range(NCOL):
        att = None
        for j in range(NCOL):
            term = jnp.dot(weights[j], et[i], preferred_element_type=f32) * v[j]
            att = term if att is None else att + term
        mixed = xs[i].astype(f32) + jnp.dot(att.astype(bf16), wout_ref[...], preferred_element_type=f32)
        pooled = mixed if pooled is None else pooled + mixed
    pooled = pooled * (1.0 / NCOL)
    h = rms_norm(pooled).astype(bf16)
    h_ref[...] = h
    msg = jnp.dot(h, wmsg_ref[...], preferred_element_type=f32).astype(bf16)
    cust_ref[...] = msg[:, :H]
    rows = pos_ref.shape[1]
    perm = (lax.broadcasted_iota(jnp.int32, (rows, rows), 0) == pos_ref[...]).astype(bf16)
    prod_ref[...] = jnp.dot(perm, msg[:, H:], preferred_element_type=f32).astype(bf16)
    ids_ref[...] = jnp.dot(perm, idc_ref[...], preferred_element_type=f32)


def encode(cols, w_qkv, w_out, w_msg, position, id_cols):
    rows = cols.shape[0]
    vmem = pl.BlockSpec(memory_space=pltpu.VMEM)
    return pl.pallas_call(
        encode_kernel,
        in_specs=[vmem] * 6,
        out_specs=[vmem] * 4,
        out_shape=[
            jax.ShapeDtypeStruct((rows, H), bf16),
            jax.ShapeDtypeStruct((rows, H), bf16),
            jax.ShapeDtypeStruct((rows, H), bf16),
            jax.ShapeDtypeStruct((rows, LANES), f32),
        ],
    )(cols, w_qkv, w_out, w_msg, position.reshape(1, rows), id_cols)

MESH = pl.DeviceIdType.MESH


def _coords(axes, sizes, t):
    out = {}
    for name, size in reversed(list(zip(axes, sizes))):
        out[name] = t % size
        t = t // size
    return out


def _step(o):
    return ((o + 1) // 2) * (2 * (o % 2) - 1)


def exchange_kernel(plan, *refs):
    total = sum(c for _, _, c in plan)
    ins, outs = refs[:total], refs[total:2 * total]
    sems = refs[2 * total:]
    groups = []
    at, s_at = 0, 0
    for axes, sizes, count in plan:
        n = int(np.prod(sizes))
        me = 0
        for name, size in zip(axes, sizes):
            me = me * size + lax.axis_index(name)
        groups.append(dict(axes=axes, sizes=sizes, n=n, me=me, ins=ins[at:at + count], outs=outs[at:at + count],
                           send=sems[s_at], recv=sems[s_at + 1], local=sems[s_at + 2]))
        at += count
        s_at += 3

    barrier = pltpu.get_barrier_semaphore()
    expected = 0
    for g in groups:
        n, me = g["n"], g["me"]
        def greet(o, carry, g=g, n=n, me=me):
            t = lax.rem(me + o, n)
            pl.semaphore_signal(barrier, inc=1, device_id=_coords(g["axes"], g["sizes"], t), device_id_type=MESH)
            return carry
        lax.fori_loop(1, n, greet, 0)
        expected += n - 1
    pl.semaphore_wait(barrier, expected)

    def remote(g, a, src, dst, t):
        if g["ins"][a].shape[0] == 1:
            src = 0
        return pltpu.make_async_remote_copy(
            src_ref=g["ins"][a].at[src], dst_ref=g["outs"][a].at[dst],
            send_sem=g["send"].at[a, src], recv_sem=g["recv"].at[a, dst],
            device_id=_coords(g["axes"], g["sizes"], t), device_id_type=MESH)

    def own(g, a):
        src = 0 if g["ins"][a].shape[0] == 1 else g["me"]
        return pltpu.make_async_copy(g["ins"][a].at[src], g["outs"][a].at[g["me"]], g["local"].at[a])

    for g in groups:
        n, me = g["n"], g["me"]
        def start(o, carry, g=g, n=n, me=me):
            t = lax.rem(me + _step(o) + n, n)
            for a in range(len(g["ins"])):
                remote(g, a, t, me, t).start()
            return carry
        lax.fori_loop(1, n, start, 0)
    for g in groups:
        for a in range(len(g["ins"])):
            own(g, a).start()
    for g in groups:
        n, me = g["n"], g["me"]
        def finish(o, carry, g=g, n=n, me=me):
            t = lax.rem(me + _step(o) + n, n)
            s = lax.rem(me - _step(o) + n, n)
            for a in range(len(g["ins"])):
                remote(g, a, t, me, t).wait_send()
                remote(g, a, me, s, s).wait_recv()
            return carry
        lax.fori_loop(1, n, finish, 0)
        for a in range(len(g["ins"])):
            own(g, a).wait()


def exchange(groups, collective_id):
    plan, arrays, scratch, n_of = [], [], [], []
    for axes, arrs in groups:
        axes = tuple(axes)
        sizes = tuple(lax.axis_size(a) for a in axes)
        n = int(np.prod(sizes))
        plan.append((axes, sizes, len(arrs)))
        arrays.extend(arrs)
        n_of.extend([n] * len(arrs))
        scratch += [pltpu.SemaphoreType.DMA((len(arrs), n)), pltpu.SemaphoreType.DMA((len(arrs), n)),
                    pltpu.SemaphoreType.DMA((len(arrs),))]
    vmem = pl.BlockSpec(memory_space=pltpu.VMEM)
    return pl.pallas_call(
        functools.partial(exchange_kernel, tuple(plan)),
        out_shape=[jax.ShapeDtypeStruct((n_of[i],) + a.shape[1:], a.dtype) for i, a in enumerate(arrays)],
        in_specs=[vmem] * len(arrays),
        out_specs=[vmem] * len(arrays),
        scratch_shapes=scratch,
        compiler_params=pltpu.CompilerParams(has_side_effects=True, collective_id=collective_id),
    )(*arrays)


def tail_kernel(shape, h_ref, cust_ref, sorted_ref, pos_ref, wback_ref, out_ref):
    rows = h_ref.shape[0]
    ret_cust = jnp.dot(order_matrix(rows, *shape), cust_ref[...], preferred_element_type=f32).astype(bf16)
    unperm = (column_of(pos_ref) == lax.broadcasted_iota(jnp.int32, (rows, rows), 1)).astype(bf16)
    ret_prod = jnp.dot(unperm, sorted_ref[...], preferred_element_type=f32).astype(bf16)
    back = jnp.dot(ret_cust, wback_ref[:H, :], preferred_element_type=f32) + jnp.dot(
        ret_prod, wback_ref[H:, :], preferred_element_type=f32
    )
    out_ref[...] = rms_norm(h_ref[...].astype(f32) + back).astype(bf16)


def tail(review_h, cust_rows, shape, sorted_rows, position, w_back):
    vmem = pl.BlockSpec(memory_space=pltpu.VMEM)
    return pl.pallas_call(
        functools.partial(tail_kernel, shape),
        out_shape=jax.ShapeDtypeStruct(review_h.shape, bf16),
        in_specs=[vmem] * 5,
        out_specs=vmem,
    )(review_h, cust_rows, sorted_rows, position.reshape(1, -1), w_back)


def order_matrix(rows, cust_slots, cust_size, stage_rows, cust_run):
    s = lax.broadcasted_iota(jnp.int32, (rows, rows), 0)
    src = ((s // cust_slots) % cust_size) * stage_rows + (s // cust_run) * cust_slots + s % cust_slots
    return (src == lax.broadcasted_iota(jnp.int32, (rows, rows), 1)).astype(bf16)


def route_kernel(rev_size, cust_slots, sent_ref, pgot_ref, pids_ref, stage_ref, pack_ref):
    rows = sent_ref.shape[0]
    s = lax.broadcasted_iota(jnp.int32, (rows, rows), 0)
    stage_rows = rev_size * cust_slots
    cust_run = rows // rev_size
    src = (s % stage_rows) // cust_slots * cust_run + (s // stage_rows) * cust_slots + s % cust_slots
    move = (src == lax.broadcasted_iota(jnp.int32, (rows, rows), 1)).astype(bf16)
    stage_ref[...] = jnp.dot(move, sent_ref[...], preferred_element_type=f32).astype(bf16)
    prows = pack_ref.shape[0]
    pick = (lax.broadcasted_iota(jnp.int32, (prows, pids_ref.shape[1]), 0) == pids_ref[...]).astype(bf16)
    pack_ref[:, :H] = jnp.dot(pick, pgot_ref[...], preferred_element_type=f32).astype(bf16)
    cnt = jnp.sum(pick.astype(f32), axis=1, keepdims=True)
    hi = jnp.floor(cnt * (1.0 / 64.0))
    lo = cnt - 64.0 * hi
    lane = lax.broadcasted_iota(jnp.int32, (prows, LANES), 1)
    pack_ref[:, H:] = jnp.where(lane == 0, hi, jnp.where(lane == 1, lo, 0.0)).astype(bf16)


def route_step(sent1, prod_got, prod_got_ids, rev_size, cust_slots, prod_rows):
    rows = sent1.shape[0]
    vmem = pl.BlockSpec(memory_space=pltpu.VMEM)
    return pl.pallas_call(
        functools.partial(route_kernel, rev_size, cust_slots),
        in_specs=[vmem] * 3,
        out_specs=[vmem] * 2,
        out_shape=[
            jax.ShapeDtypeStruct((rows, H), bf16),
            jax.ShapeDtypeStruct((prod_rows, H + LANES), bf16),
        ],
    )(sent1, prod_got, prod_got_ids.reshape(1, -1))


def refresh_rows(sums, counts, states, weight):
    normed = (sums / jnp.sqrt(jnp.maximum(counts, 1.0))).astype(bf16)
    update = jax.nn.silu(jnp.dot(normed, weight, preferred_element_type=f32))
    return rms_norm(states.astype(f32) + update).astype(bf16)


def column_of(row_ref):
    return jnp.transpose(jnp.broadcast_to(row_ref[...], (8, row_ref.shape[1])))[:, 0:1]


def gather_kernel(rev_axis, gids_ref, grows_ref, spread_ref, pstate_ref, wpu_ref, pack_ref, pnew_ref):
    rows = pack_ref.shape[0]
    pick = (lax.broadcasted_iota(jnp.int32, (rows, gids_ref.shape[1]), 0) == gids_ref[...]).astype(bf16)
    pack_ref[:, :H] = jnp.dot(pick, grows_ref[...], preferred_element_type=f32)
    cnt = jnp.sum(pick.astype(f32), axis=1, keepdims=True)
    pack_ref[:, H:] = jnp.broadcast_to(cnt, (rows, LANES))
    whole = spread_ref[0].astype(f32)
    for i in range(1, spread_ref.shape[0]):
        whole = whole + spread_ref[i].astype(f32)
    own = pnew_ref.shape[0]
    counts = whole[:, H:H + 1] * 64.0 + whole[:, H + 1:H + 2]
    start = pl.multiple_of(lax.axis_index(rev_axis) * own, own)
    pnew_ref[...] = refresh_rows(whole[:, :H], counts, pstate_ref[pl.ds(start, own), :], wpu_ref[...])


def gather_step(got_ids, got_rows, spread, prod_state, w_prod_up, cust_rows):
    own = prod_state.shape[0] // spread.shape[0]
    vmem = pl.BlockSpec(memory_space=pltpu.VMEM)
    return pl.pallas_call(
        functools.partial(gather_kernel, "rev"),
        in_specs=[vmem] * 5,
        out_specs=[vmem] * 2,
        out_shape=[
            jax.ShapeDtypeStruct((cust_rows, H + LANES), f32),
            jax.ShapeDtypeStruct((own, H), bf16),
        ],
    )(got_ids.reshape(1, -1), got_rows, spread, prod_state, w_prod_up)


def reply_kernel(shape, both_ref, cstate_ref, wcu_ref, gids_ref, newprod_ref, pids_ref, newcust_ref, creply_ref, preply_ref):
    tot = both_ref[0] + both_ref[1]
    new_cust = refresh_rows(tot[:, :H], tot[:, H:H + 1], cstate_ref[...], wcu_ref[...])
    newcust_ref[...] = new_cust
    n = gids_ref.shape[1]
    pick_t = (column_of(gids_ref) == lax.broadcasted_iota(jnp.int32, (n, new_cust.shape[0]), 1)).astype(bf16)
    reply = jnp.dot(pick_t, new_cust, preferred_element_type=f32).astype(bf16)
    creply_ref[...] = jnp.dot(order_matrix(n, *shape), reply, preferred_element_type=f32).astype(bf16)
    m = pids_ref.shape[1]
    ppick_t = (column_of(pids_ref) == lax.broadcasted_iota(jnp.int32, (m, newprod_ref.shape[0]), 1)).astype(bf16)
    preply_ref[...] = jnp.dot(ppick_t, newprod_ref[...], preferred_element_type=f32).astype(bf16)


def reply_step(cust_both, cust_state, w_cust_up, got_ids, shape, new_prod, prod_got_ids):
    vmem = pl.BlockSpec(memory_space=pltpu.VMEM)
    n = got_ids.size
    return pl.pallas_call(
        functools.partial(reply_kernel, shape),
        in_specs=[vmem] * 6,
        out_specs=[vmem] * 3,
        out_shape=[
            jax.ShapeDtypeStruct(cust_state.shape, bf16),
            jax.ShapeDtypeStruct((n, H), bf16),
            jax.ShapeDtypeStruct((prod_got_ids.size, H), bf16),
        ],
    )(cust_both, cust_state, w_cust_up, got_ids.reshape(1, -1), new_prod, prod_got_ids.reshape(1, -1))


def refresh(totals, counts, states, weight):
    normed_sum = (totals / jnp.sqrt(jnp.maximum(counts, 1.0))[:, None]).astype(bf16)
    update = jax.nn.silu(jnp.dot(normed_sum, weight, preferred_element_type=f32))
    return rms_norm(states.astype(f32) + update).astype(bf16)


def pick_back(picker, states):
    return lax.dot_general(
        picker, states, (((0,), (0,)), ((), ())), preferred_element_type=f32
    ).astype(bf16)


def one_hot_rows(ids, rows):
    return (ids.reshape(1, -1) == jnp.arange(rows, dtype=jnp.int32)[:, None]).astype(bf16)


def on_device(
    review_cols,
    cust_state,
    prod_state,
    w_qkv,
    w_out,
    w_msg,
    w_cust_up,
    w_prod_up,
    w_back,
    cust_slot,
    prod_slot,
    prod_pos,
    live_count,
):
    review_rows = review_cols.shape[0]
    rev_size = lax.axis_size("rev")
    cust_size = lax.axis_size("cust")
    prod_size = lax.axis_size("prod")
    cust_owners = rev_size * cust_size
    cust_slots = review_rows // cust_owners
    prod_owners = cust_size * prod_size
    prod_slots = review_rows // prod_owners
    cust_rows = cust_state.shape[0]
    prod_rows = prod_state.shape[0]
    own_rows = prod_rows // rev_size

    filled = jnp.arange(cust_slots, dtype=jnp.int32)[None, :] < live_count.reshape(cust_owners, 1)
    live = filled.reshape(review_rows)
    cust_ids = jnp.where(filled, cust_slot.reshape(cust_owners, cust_slots), -1)
    position = prod_pos.reshape(review_rows)
    id_plus = jnp.where(live, prod_slot + 1, 0)
    id_lane = jnp.arange(LANES, dtype=jnp.int32)[None, :]
    id_cols = jnp.where(
        id_lane == 0, (id_plus // 32)[:, None], jnp.where(id_lane == 1, (id_plus % 32)[:, None], 0)
    ).astype(bf16)
    review_h, to_cust, prod_msgs, sorted_ids = encode(review_cols, w_qkv, w_out, w_msg, position, id_cols)
    prod_ids = (sorted_ids[:, 0] * 32.0 + sorted_ids[:, 1]).astype(jnp.int32) - 1

    cust_run = cust_size * cust_slots
    stage_rows = rev_size * cust_slots
    prod_got, prod_got_ids, sent1, ids1 = exchange(
        [
            (("cust", "prod"), [prod_msgs.reshape(prod_owners, prod_slots, H),
                                prod_ids.reshape(prod_owners, 1, prod_slots)]),
            (("rev",), [to_cust.reshape(rev_size, cust_run, H), cust_ids.reshape(rev_size, 1, cust_run)]),
        ],
        0,
    )
    stage2, prod_pack = route_step(
        sent1.reshape(review_rows, H), prod_got.reshape(review_rows, H), prod_got_ids, rev_size, cust_slots, prod_rows
    )
    ids2 = ids1.reshape(rev_size, cust_size, cust_slots).transpose(1, 0, 2)
    got_rows, got_ids, spread = exchange(
        [
            (("cust",), [stage2.reshape(cust_size, stage_rows, H), ids2.reshape(cust_size, 1, stage_rows)]),
            (("rev",), [prod_pack.reshape(rev_size, own_rows, H + LANES)]),
        ],
        1,
    )
    cust_pack, own_new = gather_step(
        got_ids, got_rows.reshape(review_rows, H), spread, prod_state, w_prod_up, cust_rows
    )

    cust_both, new_prod = exchange(
        [
            (("prod",), [cust_pack[None]]),
            (("rev",), [own_new[None]]),
        ],
        2,
    )
    new_prod = new_prod.reshape(prod_rows, H)
    shape = (cust_slots, cust_size, stage_rows, cust_run)
    new_cust, reply, prod_reply = reply_step(
        cust_both, cust_state, w_cust_up, got_ids, shape, new_prod, prod_got_ids
    )
    ret_sorted, back1 = exchange(
        [
            (("cust", "prod"), [prod_reply.reshape(prod_owners, prod_slots, H)]),
            (("rev",), [reply.reshape(rev_size, cust_run, H)]),
        ],
        3,
    )
    back2 = back1.reshape(rev_size, cust_size, cust_slots, H).transpose(1, 0, 2, 3)
    (ret_cust,) = exchange([(("cust",), [back2.reshape(cust_size, stage_rows, H)])], 4)
    review_out = tail(
        review_h, ret_cust.reshape(review_rows, H), shape, ret_sorted.reshape(review_rows, H), position, w_back
    )
    return (review_out, new_cust, new_prod)


def solution(mesh):
    in_specs = (
        P(("rev", "cust", "prod"), None),
        P(("rev", "cust"), None),
        P(("cust", "prod"), None),
        P(),
        P(),
        P(),
        P(),
        P(),
        P(),
        P(("rev", "cust", "prod")),
        P(("rev", "cust", "prod")),
        P(("rev", "cust", "prod"), None),
        P(("rev", "cust", "prod"), None),
    )
    out_specs = (
        P(("rev", "cust", "prod"), None),
        P(("rev", "cust"), None),
        P(("cust", "prod"), None),
    )
    return jax.shard_map(
        on_device, mesh=mesh, in_specs=in_specs, out_specs=out_specs, check_vma=False
    )
```

```python
import math

import jax
import jax.numpy as jnp
from jax import lax
import functools

import numpy as np
from jax.experimental import pallas as pl
from jax.experimental.pallas import tpu as pltpu
from jax.sharding import PartitionSpec as P

H = 512
HEADS = 8
NCOL = 4
HD = 64
LANES = 128
f32 = jnp.float32
bf16 = jnp.bfloat16


def rms_norm(vector):
    return vector * lax.rsqrt(jnp.mean(vector * vector, axis=-1, keepdims=True) + 1e-06)


def encode_kernel(x_ref, wqkv_ref, wout_ref, wmsg_ref, pos_ref, idc_ref, h_ref, cust_ref, prod_ref, ids_ref):
    head = lax.broadcasted_iota(jnp.int32, (H, LANES), 0) // HD
    lane = lax.broadcasted_iota(jnp.int32, (H, LANES), 1)
    e = [(lane == i * HEADS + head).astype(bf16) for i in range(NCOL)]
    head_t = lax.broadcasted_iota(jnp.int32, (LANES, H), 1) // HD
    lane_t = lax.broadcasted_iota(jnp.int32, (LANES, H), 0)
    et = [(lane_t == i * HEADS + head_t).astype(bf16) for i in range(NCOL)]
    xs = [x_ref[:, i * H:(i + 1) * H] for i in range(NCOL)]
    q, k, v = [], [], []
    for i in range(NCOL):
        qkv = jnp.dot(xs[i], wqkv_ref[...], preferred_element_type=f32).astype(bf16)
        q.append(qkv[:, :H])
        k.append(qkv[:, H:2 * H])
        v.append(qkv[:, 2 * H:].astype(f32))
    scores = []
    for j in range(NCOL):
        s = None
        for i in range(NCOL):
            term = jnp.dot(q[i] * k[j], e[i], preferred_element_type=f32)
            s = term if s is None else s + term
        scores.append(s * (1.0 / math.sqrt(HD)))
    top = jnp.maximum(jnp.maximum(scores[0], scores[1]), jnp.maximum(scores[2], scores[3]))
    expon = [jnp.exp(s - top) for s in scores]
    total = (expon[0] + expon[1]) + (expon[2] + expon[3])
    weights = [(x / total).astype(bf16) for x in expon]
    pooled = None
    for i in range(NCOL):
        att = None
        for j in range(NCOL):
            term = jnp.dot(weights[j], et[i], preferred_element_type=f32) * v[j]
            att = term if att is None else att + term
        mixed = xs[i].astype(f32) + jnp.dot(att.astype(bf16), wout_ref[...], preferred_element_type=f32)
        pooled = mixed if pooled is None else pooled + mixed
    pooled = pooled * (1.0 / NCOL)
    h = rms_norm(pooled).astype(bf16)
    h_ref[...] = h
    msg = jnp.dot(h, wmsg_ref[...], preferred_element_type=f32).astype(bf16)
    cust_ref[...] = msg[:, :H]
    rows = pos_ref.shape[1]
    perm = (lax.broadcasted_iota(jnp.int32, (rows, rows), 0) == pos_ref[...]).astype(bf16)
    prod_ref[...] = jnp.dot(perm, msg[:, H:], preferred_element_type=f32).astype(bf16)
    ids_ref[...] = jnp.dot(perm, idc_ref[...], preferred_element_type=f32)


def encode(cols, w_qkv, w_out, w_msg, position, id_cols):
    rows = cols.shape[0]
    vmem = pl.BlockSpec(memory_space=pltpu.VMEM)
    return pl.pallas_call(
        encode_kernel,
        in_specs=[vmem] * 6,
        out_specs=[vmem] * 4,
        out_shape=[
            jax.ShapeDtypeStruct((rows, H), bf16),
            jax.ShapeDtypeStruct((rows, H), bf16),
            jax.ShapeDtypeStruct((rows, H), bf16),
            jax.ShapeDtypeStruct((rows, LANES), f32),
        ],
    )(cols, w_qkv, w_out, w_msg, position.reshape(1, rows), id_cols)

MESH = pl.DeviceIdType.MESH


def _coords(axes, sizes, t):
    out = {}
    for name, size in reversed(list(zip(axes, sizes))):
        out[name] = t % size
        t = t // size
    return out


def _step(o):
    return ((o + 1) // 2) * (2 * (o % 2) - 1)


def exchange_kernel(plan, *refs):
    total = sum(c for _, _, c in plan)
    ins, outs = refs[:total], refs[total:2 * total]
    sems = refs[2 * total:]
    groups = []
    at, s_at = 0, 0
    for axes, sizes, count in plan:
        n = int(np.prod(sizes))
        me = 0
        for name, size in zip(axes, sizes):
            me = me * size + lax.axis_index(name)
        groups.append(dict(axes=axes, sizes=sizes, n=n, me=me, ins=ins[at:at + count], outs=outs[at:at + count],
                           send=sems[s_at], recv=sems[s_at + 1], local=sems[s_at + 2]))
        at += count
        s_at += 3

    barrier = pltpu.get_barrier_semaphore()
    expected = 0
    for g in groups:
        n, me = g["n"], g["me"]
        def greet(o, carry, g=g, n=n, me=me):
            t = lax.rem(me + o, n)
            pl.semaphore_signal(barrier, inc=1, device_id=_coords(g["axes"], g["sizes"], t), device_id_type=MESH)
            return carry
        lax.fori_loop(1, n, greet, 0)
        expected += n - 1
    pl.semaphore_wait(barrier, expected)

    def remote(g, a, src, dst, t):
        if g["ins"][a].shape[0] == 1:
            src = 0
        return pltpu.make_async_remote_copy(
            src_ref=g["ins"][a].at[src], dst_ref=g["outs"][a].at[dst],
            send_sem=g["send"].at[a, src], recv_sem=g["recv"].at[a, dst],
            device_id=_coords(g["axes"], g["sizes"], t), device_id_type=MESH)

    def own(g, a):
        src = 0 if g["ins"][a].shape[0] == 1 else g["me"]
        return pltpu.make_async_copy(g["ins"][a].at[src], g["outs"][a].at[g["me"]], g["local"].at[a])

    for g in groups:
        for a in range(len(g["ins"])):
            own(g, a).start()
    for g in groups:
        n, me = g["n"], g["me"]
        def start(o, carry, g=g, n=n, me=me):
            t = lax.rem(me + _step(o) + n, n)
            for a in range(len(g["ins"])):
                remote(g, a, t, me, t).start()
            return carry
        lax.fori_loop(1, n, start, 0)
    for g in groups:
        n, me = g["n"], g["me"]
        def finish(o, carry, g=g, n=n, me=me):
            t = lax.rem(me + _step(o) + n, n)
            s = lax.rem(me - _step(o) + n, n)
            for a in range(len(g["ins"])):
                remote(g, a, t, me, t).wait_send()
                remote(g, a, me, s, s).wait_recv()
            return carry
        lax.fori_loop(1, n, finish, 0)
        for a in range(len(g["ins"])):
            own(g, a).wait()


def exchange(groups, collective_id):
    plan, arrays, scratch, n_of = [], [], [], []
    for axes, arrs in groups:
        axes = tuple(axes)
        sizes = tuple(lax.axis_size(a) for a in axes)
        n = int(np.prod(sizes))
        plan.append((axes, sizes, len(arrs)))
        arrays.extend(arrs)
        n_of.extend([n] * len(arrs))
        scratch += [pltpu.SemaphoreType.DMA((len(arrs), n)), pltpu.SemaphoreType.DMA((len(arrs), n)),
                    pltpu.SemaphoreType.DMA((len(arrs),))]
    vmem = pl.BlockSpec(memory_space=pltpu.VMEM)
    return pl.pallas_call(
        functools.partial(exchange_kernel, tuple(plan)),
        out_shape=[jax.ShapeDtypeStruct((n_of[i],) + a.shape[1:], a.dtype) for i, a in enumerate(arrays)],
        in_specs=[vmem] * len(arrays),
        out_specs=[vmem] * len(arrays),
        scratch_shapes=scratch,
        compiler_params=pltpu.CompilerParams(has_side_effects=True, collective_id=collective_id),
    )(*arrays)


def tail_kernel(shape, h_ref, cust_ref, sorted_ref, pos_ref, wback_ref, out_ref):
    rows = h_ref.shape[0]
    ret_cust = jnp.dot(order_matrix(rows, *shape), cust_ref[...], preferred_element_type=f32).astype(bf16)
    unperm = (column_of(pos_ref) == lax.broadcasted_iota(jnp.int32, (rows, rows), 1)).astype(bf16)
    ret_prod = jnp.dot(unperm, sorted_ref[...], preferred_element_type=f32).astype(bf16)
    back = jnp.dot(ret_cust, wback_ref[:H, :], preferred_element_type=f32) + jnp.dot(
        ret_prod, wback_ref[H:, :], preferred_element_type=f32
    )
    out_ref[...] = rms_norm(h_ref[...].astype(f32) + back).astype(bf16)


def tail(review_h, cust_rows, shape, sorted_rows, position, w_back):
    vmem = pl.BlockSpec(memory_space=pltpu.VMEM)
    return pl.pallas_call(
        functools.partial(tail_kernel, shape),
        out_shape=jax.ShapeDtypeStruct(review_h.shape, bf16),
        in_specs=[vmem] * 5,
        out_specs=vmem,
    )(review_h, cust_rows, sorted_rows, position.reshape(1, -1), w_back)


def order_matrix(rows, cust_slots, cust_size, stage_rows, cust_run):
    s = lax.broadcasted_iota(jnp.int32, (rows, rows), 0)
    src = ((s // cust_slots) % cust_size) * stage_rows + (s // cust_run) * cust_slots + s % cust_slots
    return (src == lax.broadcasted_iota(jnp.int32, (rows, rows), 1)).astype(bf16)


def route_kernel(rev_size, cust_slots, sent_ref, pgot_ref, pids_ref, stage_ref, pack_ref):
    rows = sent_ref.shape[0]
    s = lax.broadcasted_iota(jnp.int32, (rows, rows), 0)
    stage_rows = rev_size * cust_slots
    cust_run = rows // rev_size
    src = (s % stage_rows) // cust_slots * cust_run + (s // stage_rows) * cust_slots + s % cust_slots
    move = (src == lax.broadcasted_iota(jnp.int32, (rows, rows), 1)).astype(bf16)
    stage_ref[...] = jnp.dot(move, sent_ref[...], preferred_element_type=f32).astype(bf16)
    prows = pack_ref.shape[0]
    pick = (lax.broadcasted_iota(jnp.int32, (prows, pids_ref.shape[1]), 0) == pids_ref[...]).astype(bf16)
    pack_ref[:, :H] = jnp.dot(pick, pgot_ref[...], preferred_element_type=f32).astype(bf16)
    cnt = jnp.sum(pick.astype(f32), axis=1, keepdims=True)
    hi = jnp.floor(cnt * (1.0 / 64.0))
    lo = cnt - 64.0 * hi
    lane = lax.broadcasted_iota(jnp.int32, (prows, LANES), 1)
    pack_ref[:, H:] = jnp.where(lane == 0, hi, jnp.where(lane == 1, lo, 0.0)).astype(bf16)


def route_step(sent1, prod_got, prod_got_ids, rev_size, cust_slots, prod_rows):
    rows = sent1.shape[0]
    vmem = pl.BlockSpec(memory_space=pltpu.VMEM)
    return pl.pallas_call(
        functools.partial(route_kernel, rev_size, cust_slots),
        in_specs=[vmem] * 3,
        out_specs=[vmem] * 2,
        out_shape=[
            jax.ShapeDtypeStruct((rows, H), bf16),
            jax.ShapeDtypeStruct((prod_rows, H + LANES), bf16),
        ],
    )(sent1, prod_got, prod_got_ids.reshape(1, -1))


def refresh_rows(sums, counts, states, weight):
    normed = (sums / jnp.sqrt(jnp.maximum(counts, 1.0))).astype(bf16)
    update = jax.nn.silu(jnp.dot(normed, weight, preferred_element_type=f32))
    return rms_norm(states.astype(f32) + update).astype(bf16)


def column_of(row_ref):
    return jnp.transpose(jnp.broadcast_to(row_ref[...], (8, row_ref.shape[1])))[:, 0:1]


def gather_kernel(rev_axis, gids_ref, grows_ref, spread_ref, pstate_ref, wpu_ref, pack_ref, pnew_ref):
    rows = pack_ref.shape[0]
    pick = (lax.broadcasted_iota(jnp.int32, (rows, gids_ref.shape[1]), 0) == gids_ref[...]).astype(bf16)
    pack_ref[:, :H] = jnp.dot(pick, grows_ref[...], preferred_element_type=f32)
    cnt = jnp.sum(pick.astype(f32), axis=1, keepdims=True)
    pack_ref[:, H:] = jnp.broadcast_to(cnt, (rows, LANES))
    whole = spread_ref[0].astype(f32)
    for i in range(1, spread_ref.shape[0]):
        whole = whole + spread_ref[i].astype(f32)
    own = pnew_ref.shape[0]
    counts = whole[:, H:H + 1] * 64.0 + whole[:, H + 1:H + 2]
    start = pl.multiple_of(lax.axis_index(rev_axis) * own, own)
    pnew_ref[...] = refresh_rows(whole[:, :H], counts, pstate_ref[pl.ds(start, own), :], wpu_ref[...])


def gather_step(got_ids, got_rows, spread, prod_state, w_prod_up, cust_rows):
    own = prod_state.shape[0] // spread.shape[0]
    vmem = pl.BlockSpec(memory_space=pltpu.VMEM)
    return pl.pallas_call(
        functools.partial(gather_kernel, "rev"),
        in_specs=[vmem] * 5,
        out_specs=[vmem] * 2,
        out_shape=[
            jax.ShapeDtypeStruct((cust_rows, H + LANES), f32),
            jax.ShapeDtypeStruct((own, H), bf16),
        ],
    )(got_ids.reshape(1, -1), got_rows, spread, prod_state, w_prod_up)


def reply_kernel(shape, both_ref, cstate_ref, wcu_ref, gids_ref, newprod_ref, pids_ref, newcust_ref, creply_ref, preply_ref, prod_out_ref):
    tot = both_ref[0] + both_ref[1]
    new_cust = refresh_rows(tot[:, :H], tot[:, H:H + 1], cstate_ref[...], wcu_ref[...])
    newcust_ref[...] = new_cust
    n = gids_ref.shape[1]
    pick_t = (column_of(gids_ref) == lax.broadcasted_iota(jnp.int32, (n, new_cust.shape[0]), 1)).astype(bf16)
    reply = jnp.dot(pick_t, new_cust, preferred_element_type=f32).astype(bf16)
    creply_ref[...] = jnp.dot(order_matrix(n, *shape), reply, preferred_element_type=f32).astype(bf16)
    m = pids_ref.shape[1]
    ppick_t = (column_of(pids_ref) == lax.broadcasted_iota(jnp.int32, (m, newprod_ref.shape[0]), 1)).astype(bf16)
    preply_ref[...] = jnp.dot(ppick_t, newprod_ref[...], preferred_element_type=f32).astype(bf16)
    prod_out_ref[...] = newprod_ref[...]


def reply_step(cust_both, cust_state, w_cust_up, got_ids, shape, new_prod, prod_got_ids):
    vmem = pl.BlockSpec(memory_space=pltpu.VMEM)
    n = got_ids.size
    return pl.pallas_call(
        functools.partial(reply_kernel, shape),
        in_specs=[vmem] * 6,
        out_specs=[vmem] * 4,
        out_shape=[
            jax.ShapeDtypeStruct(cust_state.shape, bf16),
            jax.ShapeDtypeStruct((n, H), bf16),
            jax.ShapeDtypeStruct((prod_got_ids.size, H), bf16),
            jax.ShapeDtypeStruct(new_prod.shape, bf16),
        ],
    )(cust_both, cust_state, w_cust_up, got_ids.reshape(1, -1), new_prod, prod_got_ids.reshape(1, -1))


def refresh(totals, counts, states, weight):
    normed_sum = (totals / jnp.sqrt(jnp.maximum(counts, 1.0))[:, None]).astype(bf16)
    update = jax.nn.silu(jnp.dot(normed_sum, weight, preferred_element_type=f32))
    return rms_norm(states.astype(f32) + update).astype(bf16)


def pick_back(picker, states):
    return lax.dot_general(
        picker, states, (((0,), (0,)), ((), ())), preferred_element_type=f32
    ).astype(bf16)


def one_hot_rows(ids, rows):
    return (ids.reshape(1, -1) == jnp.arange(rows, dtype=jnp.int32)[:, None]).astype(bf16)


def on_device(
    review_cols,
    cust_state,
    prod_state,
    w_qkv,
    w_out,
    w_msg,
    w_cust_up,
    w_prod_up,
    w_back,
    cust_slot,
    prod_slot,
    prod_pos,
    live_count,
):
    review_rows = review_cols.shape[0]
    rev_size = lax.axis_size("rev")
    cust_size = lax.axis_size("cust")
    prod_size = lax.axis_size("prod")
    cust_owners = rev_size * cust_size
    cust_slots = review_rows // cust_owners
    prod_owners = cust_size * prod_size
    prod_slots = review_rows // prod_owners
    cust_rows = cust_state.shape[0]
    prod_rows = prod_state.shape[0]
    own_rows = prod_rows // rev_size

    filled = jnp.arange(cust_slots, dtype=jnp.int32)[None, :] < live_count.reshape(cust_owners, 1)
    live = filled.reshape(review_rows)
    cust_ids = jnp.where(filled, cust_slot.reshape(cust_owners, cust_slots), -1)
    position = prod_pos.reshape(review_rows)
    id_plus = jnp.where(live, prod_slot + 1, 0)
    id_lane = jnp.arange(LANES, dtype=jnp.int32)[None, :]
    id_cols = jnp.where(
        id_lane == 0, (id_plus // 32)[:, None], jnp.where(id_lane == 1, (id_plus % 32)[:, None], 0)
    ).astype(bf16)
    review_h, to_cust, prod_msgs, sorted_ids = encode(review_cols, w_qkv, w_out, w_msg, position, id_cols)
    prod_ids = (sorted_ids[:, 0] * 32.0 + sorted_ids[:, 1]).astype(jnp.int32) - 1

    cust_run = cust_size * cust_slots
    stage_rows = rev_size * cust_slots
    prod_got, prod_got_ids, sent1, ids1 = exchange(
        [
            (("cust", "prod"), [prod_msgs.reshape(prod_owners, prod_slots, H),
                                prod_ids.reshape(prod_owners, 1, prod_slots)]),
            (("rev",), [to_cust.reshape(rev_size, cust_run, H), cust_ids.reshape(rev_size, 1, cust_run)]),
        ],
        0,
    )
    stage2, prod_pack = route_step(
        sent1.reshape(review_rows, H), prod_got.reshape(review_rows, H), prod_got_ids, rev_size, cust_slots, prod_rows
    )
    ids2 = ids1.reshape(rev_size, cust_size, cust_slots).transpose(1, 0, 2)
    got_rows, got_ids, spread = exchange(
        [
            (("cust",), [stage2.reshape(cust_size, stage_rows, H), ids2.reshape(cust_size, 1, stage_rows)]),
            (("rev",), [prod_pack.reshape(rev_size, own_rows, H + LANES)]),
        ],
        1,
    )
    cust_pack, own_new = gather_step(
        got_ids, got_rows.reshape(review_rows, H), spread, prod_state, w_prod_up, cust_rows
    )

    cust_both, new_prod = exchange(
        [
            (("prod",), [cust_pack[None]]),
            (("rev",), [own_new[None]]),
        ],
        2,
    )
    new_prod = new_prod.reshape(prod_rows, H)
    shape = (cust_slots, cust_size, stage_rows, cust_run)
    new_cust, reply, prod_reply, new_prod = reply_step(
        cust_both, cust_state, w_cust_up, got_ids, shape, new_prod, prod_got_ids
    )
    ret_sorted, back1 = exchange(
        [
            (("cust", "prod"), [prod_reply.reshape(prod_owners, prod_slots, H)]),
            (("rev",), [reply.reshape(rev_size, cust_run, H)]),
        ],
        3,
    )
    back2 = back1.reshape(rev_size, cust_size, cust_slots, H).transpose(1, 0, 2, 3)
    (ret_cust,) = exchange([(("cust",), [back2.reshape(cust_size, stage_rows, H)])], 4)
    review_out = tail(
        review_h, ret_cust.reshape(review_rows, H), shape, ret_sorted.reshape(review_rows, H), position, w_back
    )
    return (review_out, new_cust, new_prod)


def solution(mesh):
    in_specs = (
        P(("rev", "cust", "prod"), None),
        P(("rev", "cust"), None),
        P(("cust", "prod"), None),
        P(),
        P(),
        P(),
        P(),
        P(),
        P(),
        P(("rev", "cust", "prod")),
        P(("rev", "cust", "prod")),
        P(("rev", "cust", "prod"), None),
        P(("rev", "cust", "prod"), None),
    )
    out_specs = (
        P(("rev", "cust", "prod"), None),
        P(("rev", "cust"), None),
        P(("cust", "prod"), None),
    )
    return jax.shard_map(
        on_device, mesh=mesh, in_specs=in_specs, out_specs=out_specs, check_vma=False
    )
```
